128 devices in a mesh: wide: 32 (over x_hi, y, z), narrow: 4 (over x_lo, core).
Axes of the slice: x: 4 (x_hi: 2, x_lo: 2; x = x_hi * 2 + x_lo), y: 4, z: 4, core: 2. Of those that a mesh axis runs over, the one named last changes fastest.
Arguments:
- displacement: float32 [3, 16, 2048, 1024], P(None, None, 'wide', 'narrow'), may hold values from -6 to 6
- velocity: float32 [3, 16, 2048, 1024], P(None, None, 'wide', 'narrow'), may hold values from -6 to 6
- region: int32 [16, 2048, 1024], P(None, 'wide', 'narrow'), may hold values from 0 to 3
- flags: int32 [256, 128], P('wide', 'narrow'), may hold values 0 or 1
- shear: float32 [4], replicated, may hold values from 0.5 to 2
- yields: float32 [4], replicated, may hold values from 2 to 16
- history: bfloat16 [32, 2, 3, 1024, 2048], P(None, None, None, ('wide', 'narrow')), may hold values from -6 to 6
- kernel: bfloat16 [33, 3, 1024, 2048], P(None, None, ('wide', 'narrow')), may hold values from -6 to 6
Outputs:
- displacement_out: float32 [3, 16, 2048, 1024], P(None, None, 'wide', 'narrow')
- velocity_out: float32 [3, 16, 2048, 1024], P(None, None, 'wide', 'narrow')
The draws below stay inside these ranges and needn't reach their ends.
Inputs may be any that keep to these rules, and one draw needn't show every extreme that they name: `flags`: 1 marks a block of 8 x 8 cells along strike and dip, through the whole depth, as yielding.
All inputs are finite; a program needn't handle non-finite values.
Results may differ from the reference program's by a relative error of at most 0.0003.
Values sent between devices are 32-bit elements; how exact they have to be, the bound alone decides.
No kernel may reach another device: no remote copies, remote signals or barrier semaphores. Data moves between devices by JAX's collectives and lax.ppermute only.
A program may use at most 256 MiB of HBM per device.

```python
import math
import jax
import jax.numpy as jnp
from jax import lax

NX = 2048
NY = 1024
NZ = 16
HIST = 32
LAGS = 33
STEPS = 2
NREG = 4
BLK = 8


def place_ends(entries, rng, smallest, largest):
    longest = entries.shape.index(max(entries.shape))
    spots = []
    for shift in (0, 1):
        where = [jax.random.randint(jax.random.fold_in(rng, axis), (), 0, length) for axis, length in enumerate(entries.shape)]
        where[longest] = (where[longest] + shift) % entries.shape[longest]
        spots.append(tuple(where))
    return entries.at[spots[0]].set(smallest).at[spots[1]].set(largest)


def block_levels(rng, extent, shards, least, top_value):
    gain = 1.0
    for position, blocks in shards:
        heights = jax.random.uniform(jax.random.fold_in(jax.random.fold_in(rng, 6), position), (blocks,), jnp.float32, least / len(shards), top_value / len(shards))
        gain = gain * jnp.repeat(jnp.exp(heights), extent[position] // blocks).reshape((-1,) + (1,) * (len(extent) - 1 - position))
    return gain


def centred(rng, extent, spread, reach, shards=(), held_as=jnp.bfloat16):
    gain = block_levels(rng, extent, shards, -0.22, 0.18) if shards else 1.0
    drawn = jax.random.normal(rng, extent, jnp.float32) * spread * gain
    return jnp.minimum(jnp.maximum(drawn, -reach), reach).astype(held_as)


def setup_inputs(seed: int = 0) -> dict:
    seeds = jax.random.split(jax.random.key(seed), 9)
    return {
        "displacement": centred(seeds[0], (3, NZ, NX, NY), 1.0, 6.0, ((2, 32), (3, 4)), jnp.float32),
        "velocity": centred(seeds[1], (3, NZ, NX, NY), 1.0, 6.0, ((2, 32), (3, 4)), jnp.float32),
        "region": place_ends(jax.random.randint(seeds[2], (NZ, NX, NY), 0, NREG), jax.random.fold_in(seeds[2], 1), 0, NREG - 1).astype(jnp.int32),
        "flags": place_ends((jax.random.randint(seeds[3], (NX // BLK, NY // BLK), 0, 2) < 1).astype(jnp.int32), jax.random.fold_in(seeds[3], 1), 0, 1),
        "shear": jnp.clip(jnp.exp(jax.random.uniform(seeds[4], (NREG,), jnp.float32, math.log(0.5), math.log(2.0))), 0.5, 2.0),
        "yields": jnp.clip(jnp.exp(jax.random.uniform(seeds[5], (NREG,), jnp.float32, math.log(2.0), math.log(16.0))), 2.0, 16.0),
        "history": centred(seeds[6], (HIST, 2, 3, NY, NX), 1.0, 6.0, ((3, 128),)),
        "kernel": centred(seeds[7], (LAGS, 3, NY, NX), 1.0, 6.0, ((2, 128),)),
    }


TIME_STEP = 0.1
DAMPING = 0.5

def transform(slip):
    spectrum = jnp.fft.fft2(slip, norm='ortho')
    spectrum = jnp.swapaxes(spectrum, 1, 2)
    return jnp.stack([jnp.real(spectrum), jnp.imag(spectrum)])

def untransform(total):
    spectrum = jnp.swapaxes(total[0] + 1j * total[1], 1, 2)
    return jnp.real(jnp.fft.ifft2(spectrum, norm='ortho'))

def yielded_force(displacement, region, flags, shear, yields):
    padded = jnp.pad(displacement, ((0, 0), (1, 1), (1, 1), (1, 1)))
    center = padded[:, 1:-1, 1:-1, 1:-1]
    beside_all = padded[:, 2:, 1:-1, 1:-1] + padded[:, :-2, 1:-1, 1:-1]
    beside_all = beside_all + padded[:, 1:-1, 2:, 1:-1] + padded[:, 1:-1, :-2, 1:-1]
    beside_all = beside_all + padded[:, 1:-1, 1:-1, 2:] + padded[:, 1:-1, 1:-1, :-2]
    modulus = shear[region]
    ceiling = yields[region]
    force = modulus[None] * (beside_all - 6.0 * center)
    squares = lax.optimization_barrier(jnp.sum(force * force, axis=0))
    capped = lax.rsqrt(1.0 + squares / (ceiling * ceiling))
    plastic = jnp.repeat(jnp.repeat(flags, BLK, axis=0), BLK, axis=1)
    scaling = jnp.where(plastic[None] == 1, capped, 1.0)
    return force * scaling[None]

def reference(displacement, velocity, region, flags, shear, yields, history, kernel):
    earlier = []
    for number in range(STEPS):
        spectrum = transform(displacement[:, 0])
        total = kernel[0].astype(jnp.float32)[None] * spectrum
        for offset, former in enumerate(earlier):
            total = total + kernel[offset + 1].astype(jnp.float32)[None] * former
        for offset in range(HIST - len(earlier)):
            weight = kernel[len(earlier) + 1 + offset].astype(jnp.float32)[None]
            total = total + weight * history[offset].astype(jnp.float32)
        earlier = [spectrum] + earlier
        traction = untransform(total) - DAMPING * velocity[:, 0]
        force = yielded_force(displacement, region, flags, shear, yields)
        force = force.at[:, 0].add(traction)
        velocity = velocity + TIME_STEP * force
        displacement = displacement + TIME_STEP * velocity
    return (displacement, velocity)
```

```python
import functools
import math

import jax
import jax.numpy as jnp
import ml_dtypes
import numpy as np
from jax import lax
from jax.experimental import pallas as pl
from jax.experimental.pallas import tpu as pltpu
from jax.sharding import PartitionSpec as P

DT = 0.1
DAMPING = 0.5
ALL = ("wide", "narrow")
F32 = jnp.float32
BF16 = jnp.bfloat16


def split_table(table):
    table = np.asarray(table, np.float64)
    high = table.astype(ml_dtypes.bfloat16)
    low = (table - high.astype(np.float64)).astype(ml_dtypes.bfloat16)
    return np.stack([high, low])


def make_tables():
    factor = 1.0 / math.sqrt(2048 * 1024)
    eye2 = np.eye(2)
    eye4 = np.eye(4)
    eye8 = np.eye(8)
    eye16 = np.eye(16)
    r8 = np.arange(8).reshape(2, 4)
    y1 = np.arange(8).reshape(4, 2)
    theta = 2 * np.pi * r8[:, :, None, None] * y1[None, None] / 8
    radix = np.stack([np.cos(theta), -np.sin(theta)])
    radix = np.einsum("isrnl,xz,fg->isxfrnglz", radix, eye16, eye2).reshape(512, 256)
    unradix = np.stack([np.cos(theta), -np.sin(theta)])
    unradix = np.einsum("isrnl,xz,fg->nglzisxfr", unradix, eye16, eye2).reshape(256, 512)
    y0 = np.arange(128)
    theta = 2 * np.pi * r8[:, :, None] * y0 / 1024
    turn = np.stack([np.cos(theta), -np.sin(theta)])[:, :, None, None]
    dip_turn = np.broadcast_to(turn, (2, 2, 16, 2, 4, 128)).reshape(2, 2, 128, 128) * factor
    alt = (-1.0) ** y0
    place = np.stack([np.arange(64), 63 - np.arange(64)])
    theta = 2 * np.pi * place[:, :, None] * y0 / 128
    cos, sin = np.cos(theta), np.sin(theta)
    dip_out = np.zeros((2, 136, 256))
    dip_out[:, :64] = np.concatenate([cos, sin], -1)
    dip_out[:, 64:128] = np.concatenate([-sin, cos], -1)
    dip_out[0, 128, :128] = alt
    dip_in = np.zeros((2, 128, 2, 2, 128))
    for s in range(2):
        rows = slice(s * 64, s * 64 + 64)
        dip_in[0, rows, s, 0] = cos[s]
        dip_in[0, rows, s, 1] = sin[s]
        dip_in[1, rows, s, 0] = -sin[s]
        dip_in[1, rows, s, 1] = cos[s]
    dip_in = dip_in.reshape(256, 512)
    theta = 2 * np.pi * np.outer(y0, y0) / 128
    cos, sin = np.cos(theta), np.sin(theta)
    strike_in = np.block([[cos, -sin], [sin, cos]])
    strike_out = np.block([[cos, -sin], [sin, cos]])
    a = np.arange(16)
    theta = 2 * np.pi * np.outer(a, y0) / 2048
    turn = np.stack([np.cos(theta), -np.sin(theta)])
    strike_turn = np.broadcast_to(turn[:, :, None], (2, 16, 8, 128)).reshape(2, 128, 128)
    theta = 2 * np.pi * np.outer(a, a) / 16
    cos, sin = np.kron(np.cos(theta), eye8), np.kron(np.sin(theta), eye8)
    strike_mix = np.block([[cos, sin], [-sin, cos]])
    strike_unmix = np.block([[cos, -sin], [sin, cos]]) * factor
    reverse = np.zeros((128, 128))
    reverse[(128 - y0) % 128, y0] = 1.0
    return {
        "radix": split_table(radix),
        "unradix": split_table(unradix),
        "dip_turn": dip_turn.astype(np.float32),
        "undip_turn": (dip_turn / factor * 2.0).astype(np.float32),
        "dip_out": split_table(dip_out),
        "dip_in": split_table(dip_in),
        "strike_in": split_table(strike_in),
        "strike_out": split_table(strike_out),
        "strike_turn": strike_turn.astype(np.float32),
        "strike_mix": split_table(strike_mix),
        "strike_unmix": split_table(strike_unmix),
        "reverse": reverse.astype(ml_dtypes.bfloat16),
    }


TABLES = make_tables()


def halves(x):
    high = x.astype(BF16)
    return high, (x - high.astype(F32)).astype(BF16)


def dot(a, b, contract=(1, 0)):
    return lax.dot_general(
        a, b, (((contract[0],), (contract[1],)), ((), ())), preferred_element_type=F32
    )


def left_dot(table, x, contract=(1, 0)):
    high, low = halves(x)
    return dot(table[0], high, contract) + (
        dot(table[1], high, contract) + dot(table[0], low, contract)
    )


def right_dot(x, table):
    high, low = halves(x)
    return dot(high, table[0]) + (dot(low, table[0]) + dot(high, table[1]))


def lanes(shape):
    return lax.broadcasted_iota(jnp.int32, shape, len(shape) - 1)


def rows_of(shape):
    return lax.broadcasted_iota(jnp.int32, shape, len(shape) - 2)


def neighbour_sum(center, above, below, top, bottom, left, right):
    rows = rows_of(center.shape)
    north = jnp.where(rows == 0, top, pltpu.roll(center, 1, 0))
    south = jnp.where(rows == 63, bottom, pltpu.roll(center, 63, 0))
    c0, c1 = center[:, :128], center[:, 128:]
    lane = lanes(c0.shape)
    w0, w1 = pltpu.roll(c0, 1, 1), pltpu.roll(c1, 1, 1)
    e0, e1 = pltpu.roll(c0, 127, 1), pltpu.roll(c1, 127, 1)
    west = jnp.concatenate([jnp.where(lane == 0, left, w0), jnp.where(lane == 0, w0, w1)], 1)
    east = jnp.concatenate([jnp.where(lane == 127, e1, e0), jnp.where(lane == 127, right, e1)], 1)
    return ((above + below) + (north + south)) + (west + east)


def plane_force(centers, sums, region, plastic, shear_ref, yields_ref):
    modulus = jnp.full(region.shape, shear_ref[0], F32)
    level = jnp.full(region.shape, yields_ref[0], F32)
    for label in range(1, 4):
        modulus = jnp.where(region == label, shear_ref[label], modulus)
        level = jnp.where(region == label, yields_ref[label], level)
    force = [modulus * (total - 6.0 * center) for total, center in zip(sums, centers)]
    squares = force[0] * force[0] + force[1] * force[1] + force[2] * force[2]
    capped = lax.rsqrt(1.0 + squares / (level * level))
    scaling = jnp.where(plastic > 0.5, capped, 1.0)
    return [f * scaling for f in force]


def slot(c, z):
    return c * 16 + z


def halo_columns(left_ref, right_ref, place):
    left = pltpu.roll(left_ref[...], lax.rem(128 - place, 128), 1)
    right = pltpu.roll(right_ref[...], 127 - place, 1)
    return left, right


def put_columns(left_ref, right_ref, center, place):
    c0, c1 = center[:, :128], center[:, 128:]
    lane = lanes(c0.shape)
    left_ref[...] = jnp.where(lane == place, pltpu.roll(c0, place, 1), left_ref[...])
    right_ref[...] = jnp.where(
        lane == place, pltpu.roll(c1, lax.rem(place + 1, 128), 1), right_ref[...]
    )


def edges_kernel(u_ref, flags_ref, first_ref, last_ref, left_ref, right_ref, plastic_ref):
    z = pl.program_id(0)

    @pl.when(z == 0)
    def _():
        left_ref[...] = jnp.zeros_like(left_ref)
        right_ref[...] = jnp.zeros_like(right_ref)
        wide = (rows_of((64, 8)) // 8 == lanes((64, 8))).astype(F32)
        high = (rows_of((32, 256)) == lanes((32, 256)) // 8).astype(F32)
        marks = (flags_ref[...] == 1).astype(F32)
        plastic_ref[...] = dot(dot(wide, marks), high)

    for c in range(3):
        plane = u_ref[c, 0]
        place = slot(c, z)
        first_ref[pl.ds(place, 1), :] = plane[0:1]
        last_ref[pl.ds(place, 1), :] = plane[63:64]
        put_columns(left_ref, right_ref, plane, place)


def slip_kernel(
    shear_ref, yields_ref, u_ref, v_ref, region_ref, plastic_ref,
    top_ref, bottom_ref, left_ref, right_ref, send_ref,
):
    centers, sums = [], []
    for c in range(3):
        center = u_ref[c, 0]
        left, right = halo_columns(left_ref, right_ref, slot(c, 0))
        place = slot(c, 0)
        sums.append(
            neighbour_sum(
                center, u_ref[c, 1], jnp.zeros_like(center),
                top_ref[place : place + 1, :], bottom_ref[place : place + 1, :], left, right,
            )
        )
        centers.append(center)
    force = plane_force(centers, sums, region_ref[0], plastic_ref[...], shear_ref, yields_ref)
    for c in range(3):
        v = v_ref[c, 0]
        v = v + DT * (force[c] - DAMPING * v)
        moved = centers[c] + DT * v
        for f, values in enumerate((centers[c], moved)):
            for n in range(4):
                for half in range(2):
                    start = f * 96 + c * 32 + half * 16
                    send_ref[n, start : start + 16, :] = values[
                        n * 16 : n * 16 + 16, half * 128 : half * 128 + 128
                    ]


def step_one_kernel(
    shear_ref, yields_ref, u_ref, v_ref, region_ref, plastic_ref,
    top_ref, bottom_ref, left_ref, right_ref,
    new_u_ref, new_v_ref, first_ref, last_ref, left_out_ref, right_out_ref,
):
    z = pl.program_id(0)

    @pl.when(z == 0)
    def _():
        left_out_ref[...] = jnp.zeros_like(left_out_ref)
        right_out_ref[...] = jnp.zeros_like(right_out_ref)

    lower = jnp.where(z > 0, 1.0, 0.0).astype(F32)
    upper = jnp.where(z < 15, 1.0, 0.0).astype(F32)
    centers, sums = [], []
    for c in range(3):
        place = slot(c, z)
        center = u_ref[c, z]
        left, right = halo_columns(left_ref, right_ref, place)
        sums.append(
            neighbour_sum(
                center,
                u_ref[c, jnp.minimum(z + 1, 15)] * upper,
                u_ref[c, jnp.maximum(z - 1, 0)] * lower,
                top_ref[pl.ds(place, 1), :], bottom_ref[pl.ds(place, 1), :], left, right,
            )
        )
        centers.append(center)
    force = plane_force(centers, sums, region_ref[0], plastic_ref[...], shear_ref, yields_ref)
    damping = jnp.where(z == 0, DAMPING, 0.0).astype(F32)
    for c in range(3):
        v = v_ref[c, 0]
        v = v + DT * (force[c] - damping * v)
        u = centers[c] + DT * v
        new_v_ref[c, 0] = v
        new_u_ref[c, 0] = u
        place = slot(c, z)
        first_ref[pl.ds(place, 1), :] = u[0:1]
        last_ref[pl.ds(place, 1), :] = u[63:64]
        put_columns(left_out_ref, right_out_ref, u, place)


def step_two_kernel(
    shear_ref, yields_ref, u_ref, v_ref, region_ref, plastic_ref,
    top_ref, bottom_ref, left_ref, right_ref, new_u_ref, new_v_ref,
):
    z = pl.program_id(0) + 2
    upper = jnp.where(z < 15, 1.0, 0.0).astype(F32)
    centers, sums = [], []
    for c in range(3):
        place = slot(c, z)
        center = u_ref[c, z]
        left, right = halo_columns(left_ref, right_ref, place)
        sums.append(
            neighbour_sum(
                center,
                u_ref[c, jnp.minimum(z + 1, 15)] * upper,
                u_ref[c, z - 1],
                top_ref[pl.ds(place, 1), :], bottom_ref[pl.ds(place, 1), :], left, right,
            )
        )
        centers.append(center)
    force = plane_force(centers, sums, region_ref[0], plastic_ref[...], shear_ref, yields_ref)
    for c in range(3):
        v = v_ref[c, 0] + DT * force[c]
        new_v_ref[c, 0] = v
        new_u_ref[c, 0] = centers[c] + DT * v


def traction_plane(recv_ref, f, c):
    parts = []
    for half in range(2):
        start = f * 96 + c * 32 + half * 16
        parts.append(
            jnp.concatenate([recv_ref[n, start : start + 16, :] for n in range(4)], 0)
        )
    return jnp.concatenate(parts, 1)


def traction_edges_kernel(recv_ref, first_ref, last_ref, left_ref, right_ref):
    left_ref[...] = jnp.zeros_like(left_ref)
    right_ref[...] = jnp.zeros_like(right_ref)
    first_ref[...] = jnp.zeros_like(first_ref)
    last_ref[...] = jnp.zeros_like(last_ref)
    for c in range(3):
        plane = traction_plane(recv_ref, 0, c)
        first_ref[c : c + 1, :] = plane[0:1]
        last_ref[c : c + 1, :] = plane[63:64]
        put_columns(left_ref, right_ref, plane, slot(c, 0))


def last_kernel(
    shear_ref, yields_ref, u_ref, v_ref, region_ref, plastic_ref,
    top_ref, bottom_ref, left_ref, right_ref,
    recv_ref, ttop_ref, tbottom_ref, tleft_ref, tright_ref,
    _old_u_ref, _old_v_ref, new_u_ref, new_v_ref,
):
    square = DT * DT
    traction = [traction_plane(recv_ref, 0, c) for c in range(3)]
    surface = [u_ref[c, 0] + square * traction[c] for c in range(3)]
    for z in range(2):
        centers, sums = [], []
        for c in range(3):
            place = slot(c, z)
            left, right = halo_columns(left_ref, right_ref, place)
            top = top_ref[place : place + 1, :]
            bottom = bottom_ref[place : place + 1, :]
            if z == 0:
                tleft, tright = halo_columns(tleft_ref, tright_ref, place)
                left = left + square * tleft
                right = right + square * tright
                top = top + square * ttop_ref[c : c + 1, :]
                bottom = bottom + square * tbottom_ref[c : c + 1, :]
                center = surface[c]
                below = jnp.zeros_like(center)
            else:
                center = u_ref[c, 1]
                below = surface[c]
            sums.append(neighbour_sum(center, u_ref[c, z + 1], below, top, bottom, left, right))
            centers.append(center)
        force = plane_force(
            centers, sums, region_ref[z], plastic_ref[...], shear_ref, yields_ref
        )
        for c in range(3):
            v = v_ref[c, z]
            if z == 0:
                v = v + DT * traction[c]
                v = v + DT * (force[c] + (traction_plane(recv_ref, 1, c) - DAMPING * v))
            else:
                v = v + DT * force[c]
            new_v_ref[c, z] = v
            new_u_ref[c, z] = centers[c] + DT * v


def history_kernel(where_ref, kernel_ref, history_ref, own_ref, main_ref, edge_ref):
    low = where_ref[0] == 1
    width = own_ref.shape[1]

    def step(m, total):
        out = []
        for c in range(3):
            one = kernel_ref[m + 1, c].astype(F32)
            two = kernel_ref[m + 2, c].astype(F32)
            for ri in range(2):
                past = history_ref[m, ri, c].astype(F32)
                p1, p2 = total[c * 2 + ri]
                out.append((p1 + one * past, p2 + two * past))
        return tuple(out)

    zero = jnp.zeros((8, width), F32)
    total = lax.fori_loop(0, 31, step, tuple((zero, zero) for _ in range(6)))
    values = [None] * 18
    for c in range(3):
        one = kernel_ref[32, c].astype(F32)
        for ri in range(2):
            p1, p2 = total[c * 2 + ri]
            values[ri * 3 + c] = p1 + one * history_ref[31, ri, c].astype(F32)
            values[6 + ri * 3 + c] = p2
        values[12 + c] = kernel_ref[0, c].astype(F32)
        values[15 + c] = kernel_ref[1, c].astype(F32)
    for i, value in enumerate(values):
        row = [value[r : r + 1] for r in range(8)]
        for r, (a, b) in enumerate(((0, 4), (1, 3), (2, 2), (3, 1))):
            own_ref[i * 4 + r : i * 4 + r + 1, :] = jnp.where(low, row[a], row[b])
        for r, (a, b) in enumerate(((4, 4), (5, 7), (6, 6), (7, 5))):
            main_ref[i * 4 + r : i * 4 + r + 1, :] = jnp.where(low, row[a], row[b])
        edge_ref[i : i + 1, :] = row[0]


def mirror_kernel(where_ref, reverse_ref, own_ref, main_ref, edge_ref, out_ref, tiles, turned):
    low = where_ref[0] == 1
    special = where_ref[1]
    for i in range(18):
        own = own_ref[i * 4 : i * 4 + 4, :]
        main = main_ref[i * 4 : i * 4 + 4, :]
        edge = edge_ref[i : i + 1, :]
        other = jnp.where(rows_of(main.shape) == 0, edge, main)
        tiles[i * 8 : i * 8 + 4, :] = jnp.where(low, own, main)
        tiles[i * 8 + 4 : i * 8 + 8, :] = jnp.where(low, other, own)
    for block in range(16):
        part = slice(block * 128, block * 128 + 128)
        high, rest = halves(tiles[:, part])
        turned[:, part] = dot(high, reverse_ref[...]) + dot(rest, reverse_ref[...])
    lane = lanes((8, 128))
    row = rows_of((8, 128))
    upper = row >= 4
    chosen = (lax.rem(row, 4) + (1 - special)) == 0

    def swap(x):
        return pltpu.roll(x, 4, 0)

    for block in range(16):
        part = slice(block * 128, block * 128 + 128)
        mirror = slice((15 - block) * 128, (15 - block) * 128 + 128)
        first = ((16 - block) % 16) * 128
        first = slice(first, first + 128)

        def load(i):
            rows = slice(i * 8, i * 8 + 8)
            back = jnp.where(lane == 0, turned[rows, first], turned[rows, mirror])
            return tiles[rows, part], back

        for c in range(3):
            for k in range(2):
                t, b = load(12 + k * 3 + c)
                own = 0.5 * (t + b)
                other = swap(own)
                mean = jnp.where(chosen, 0.5 * (own + other), 0.5 * (t + swap(b)))
                diff = jnp.where(chosen, 0.5 * (own - other), 0.0)
                out_ref[k, c, :, part] = jnp.where(upper, swap(mean), mean)
                out_ref[2 + k, c, :, part] = jnp.where(upper, swap(diff), diff)
            pair = []
            for k in range(2):
                tr, br = load(k * 6 + c)
                ti, bi = load(k * 6 + 3 + c)
                hr, hi = 0.5 * (tr + br), 0.5 * (ti - bi)
                sr, si = swap(hr), swap(hi)
                pair.append(
                    (
                        jnp.where(chosen, hr - si, 0.5 * (tr + swap(br))),
                        jnp.where(chosen, hi + sr, 0.5 * (ti - swap(bi))),
                        hr + si,
                        hi - sr,
                    )
                )
            out_ref[4, c, :, part] = jnp.where(upper, swap(pair[1][0]), pair[0][0])
            out_ref[5, c, :, part] = jnp.where(upper, swap(pair[1][1]), pair[0][1])
            out_ref[6, c, :, part] = pair[0][2]
            out_ref[7, c, :, part] = pair[0][3]


def dip_kernel(radix_ref, turn_ref, out_table_ref, recv_ref, send_ref):
    wide = []
    for c in range(3):
        pieces = []
        for n in range(4):
            for f in range(2):
                start = f * 96 + c * 32
                pieces.append(recv_ref[n, start : start + 32, :])
        wide.append(jnp.concatenate(pieces, 0))
    z = left_dot(radix_ref, jnp.concatenate(wide, 1))
    lane = lanes((1, 128))
    for s in range(2):
        tr, ti = turn_ref[0, s], turn_ref[1, s]
        for c in range(3):
            part = slice(c * 128, c * 128 + 128)
            zr = z[s * 128 : s * 128 + 128, part]
            zi = z[256 + s * 128 : 384 + s * 128, part]
            turned = jnp.concatenate([zr * tr - zi * ti, zr * ti + zi * tr], 1)
            high, low = halves(turned)
            table, rest = out_table_ref[0, s], out_table_ref[1, s]
            res = dot(table, high, (1, 1)) + (dot(rest, high, (1, 1)) + dot(table, low, (1, 1)))
            imag = res[64:128]
            if s == 0:
                extra = jnp.where(lax.rem(lane, 4) == 0, res[128:129], 0.0)
                imag = jnp.where(rows_of(imag.shape) == 0, imag + extra, imag)
            send_ref[pl.ds(s * 384 + c * 2, 64, stride=6), :] = res[0:64]
            send_ref[pl.ds(s * 384 + c * 2 + 1, 64, stride=6), :] = imag


def strike_kernel(
    in_ref, turn_ref, mix_ref, reverse_ref, unmix_ref, out_table_ref,
    coef_ref, recv_ref, send_ref, spec, back, total,
):
    tr, ti = turn_ref[0], turn_ref[1]
    real, imag = [], []
    for c in range(3):
        re = recv_ref[pl.ds(c * 2, 128, stride=6), :].T
        im = recv_ref[pl.ds(c * 2 + 1, 128, stride=6), :].T
        y = right_dot(jnp.concatenate([re, im], 1), in_ref)
        yr, yi = y[:, :128], y[:, 128:]
        real.append(yr * tr - yi * ti)
        imag.append(yr * ti + yi * tr)
    stacked = jnp.concatenate([jnp.concatenate(real, 1), jnp.concatenate(imag, 1)], 0)
    spec[...] = left_dot(mix_ref, stacked)
    for c in range(3):
        part = slice(c * 128, c * 128 + 128)
        high, low = halves(spec[:, part])
        back[:, part] = dot(high, reverse_ref[...]) + dot(low, reverse_ref[...])
    lane = lanes((8, 128))
    upper = rows_of((8, 128)) >= 4

    def swap(x):
        return pltpu.roll(x, 4, 0)

    for c in range(3):
        part = slice(c * 128, c * 128 + 128)
        for block in range(16):
            wave = slice(block * 128, block * 128 + 128)
            a0, a1 = coef_ref[0, c, :, wave], coef_ref[1, c, :, wave]
            m0, m1 = coef_ref[2, c, :, wave], coef_ref[3, c, :, wave]
            for ri in range(2):
                rows = slice(ri * 128 + block * 8, ri * 128 + block * 8 + 8)
                first = ri * 128 + ((16 - block) % 16) * 8
                other = ri * 128 + (15 - block) * 8
                s = spec[rows, part]
                r = jnp.where(
                    lane == 0, back[first : first + 8, part], back[other : other + 8, part]
                )
                if ri == 1:
                    r = -r
                t = a0 * s + m0 * r + coef_ref[4 + ri, c, :, wave]
                q = a0 * r + m0 * s + coef_ref[6 + ri, c, :, wave]
                more = (DT * DT) * (a0 * swap(t) + m0 * swap(q)) + a1 * swap(s) + m1 * swap(r)
                total[rows, part] = t + jnp.where(upper, more, 0.0)
    y = left_dot(unmix_ref, total[...])
    for c in range(3):
        part = slice(c * 128, c * 128 + 128)
        yr, yi = y[:128, part], y[128:, part]
        turned = jnp.concatenate([yr * tr + yi * ti, yi * tr - yr * ti], 1)
        high, low = halves(turned)
        res = dot(out_table_ref[0], high, (1, 1)) + (
            dot(out_table_ref[1], high, (1, 1)) + dot(out_table_ref[0], low, (1, 1))
        )
        send_ref[pl.ds(c * 2, 128, stride=6), :] = res[:128]
        send_ref[pl.ds(c * 2 + 1, 128, stride=6), :] = res[128:]


def undip_kernel(in_ref, turn_ref, unradix_ref, recv_ref, send_ref):
    row = rows_of((128, 128))
    lane = lanes((128, 128))
    alt = jnp.where(lax.rem(lane, 2) == 0, 0.5, -0.5).astype(F32)
    stacks = [[], [], [], []]
    for c in range(3):
        re = recv_ref[pl.ds(c * 2, 128, stride=6), :].T
        im = recv_ref[pl.ds(c * 2 + 1, 128, stride=6), :].T
        h = right_dot(jnp.concatenate([re, im], 1), in_ref)
        for s in range(2):
            hr = h[:, s * 256 : s * 256 + 128]
            hi = h[:, s * 256 + 128 : s * 256 + 256]
            if s == 0:
                fix = alt * im[:, 0:1] - 0.5 * re[:, 0:1]
                hr = hr + jnp.where(lax.rem(row, 4) == 0, fix, 0.0)
            tr, ti = turn_ref[0, s], turn_ref[1, s]
            stacks[s].append(hr * tr + hi * ti)
            stacks[2 + s].append(hi * tr - hr * ti)
    stacked = jnp.concatenate([jnp.concatenate(part, 1) for part in stacks], 0)
    out = left_dot(unradix_ref, stacked)
    for n in range(4):
        for f in range(2):
            for c in range(3):
                start = f * 96 + c * 32
                row0 = (n * 2 + f) * 32
                send_ref[n, start : start + 32, :] = out[row0 : row0 + 32, c * 128 : c * 128 + 128]


def full(shape):
    zeros = (0,) * len(shape)
    return pl.BlockSpec(shape, lambda *_: zeros)


SMEM = pl.BlockSpec(memory_space=pltpu.SMEM)


def shape_of(*shape):
    return jax.ShapeDtypeStruct(shape, F32)


def call(body, out_shape, args, smem=0, scratch=(), flops=0, name=None):
    outs = out_shape if isinstance(out_shape, (tuple, list)) else [out_shape]
    size = sum(math.prod(x.shape) * 4 for x in list(args) + list(outs))
    out_specs = [full(x.shape) for x in outs]
    return pl.pallas_call(
        body,
        grid=(1,),
        in_specs=[SMEM] * smem + [full(x.shape) for x in args[smem:]],
        out_specs=out_specs if isinstance(out_shape, (tuple, list)) else out_specs[0],
        out_shape=out_shape,
        scratch_shapes=scratch,
        cost_estimate=pl.CostEstimate(flops=flops, bytes_accessed=size, transcendentals=0),
        name=name,
    )(*args)


def halo(first, last, left, right):
    up = [(i, i + 1) for i in range(31)]
    down = [(i + 1, i) for i in range(31)]
    top = lax.ppermute(last, "wide", up)
    bottom = lax.ppermute(first, "wide", down)
    up = [(i, i + 1) for i in range(3)]
    down = [(i + 1, i) for i in range(3)]
    from_left = lax.ppermute(right, "narrow", up)
    from_right = lax.ppermute(left, "narrow", down)
    return top, bottom, from_left, from_right


def exchange(x, axis):
    return lax.all_to_all(x, axis, split_axis=0, concat_axis=0, tiled=True)


def all_exchange(x):
    return exchange(x.reshape(128, 1, 768), ALL).reshape(768, 128)


def body(u, v, region, flags, shear, yields, history, kernel):
    device = lax.axis_index(ALL)
    where = jnp.stack([device < 64, device == 0]).astype(jnp.int32)
    edge_shapes = [shape_of(48, 256)] * 2 + [shape_of(64, 128)] * 2
    plane_block = pl.BlockSpec((3, 1, 64, 256), lambda z: (0, z, 0, 0))
    first, last, left, right, plastic = pl.pallas_call(
        edges_kernel,
        grid=(16,),
        in_specs=[plane_block, full((8, 32))],
        out_specs=[full(s.shape) for s in edge_shapes] + [full((64, 256))],
        out_shape=edge_shapes + [shape_of(64, 256)],
        cost_estimate=pl.CostEstimate(flops=0, bytes_accessed=3300000, transcendentals=0),
        name="edges",
    )(u, flags)
    halo_one = halo(first, last, left, right)

    width = 256
    own, main, edge = pl.pallas_call(
        history_kernel,
        grid=(2048 // width,),
        in_specs=[
            SMEM,
            pl.BlockSpec((33, 3, 8, width), lambda i: (0, 0, 0, i)),
            pl.BlockSpec((32, 2, 3, 8, width), lambda i: (0, 0, 0, 0, i)),
        ],
        out_specs=[
            pl.BlockSpec((72, width), lambda i: (0, i)),
            pl.BlockSpec((72, width), lambda i: (0, i)),
            pl.BlockSpec((18, width), lambda i: (0, i)),
        ],
        out_shape=[shape_of(72, 2048), shape_of(72, 2048), shape_of(18, 2048)],
        cost_estimate=pl.CostEstimate(flops=0, bytes_accessed=11000000, transcendentals=0),
        name="history",
    )(where, kernel, history)
    main = lax.ppermute(main, ALL, [(i, 127 - i) for i in range(128)])
    edge = lax.ppermute(edge, ALL, [(64, 0)] + [(i, 128 - i) for i in range(65, 128)])

    near = lambda depth: pl.BlockSpec((3, depth, 64, 256), lambda *_: (0, 0, 0, 0))
    slab = lambda depth: pl.BlockSpec((depth, 64, 256), lambda *_: (0, 0, 0))
    halo_specs = [full((48, 256))] * 2 + [full((64, 128))] * 2
    send = pl.pallas_call(
        slip_kernel,
        grid=(1,),
        in_specs=[SMEM, SMEM, near(2), near(1), slab(1), full((64, 256))] + halo_specs,
        out_specs=full((4, 192, 128)),
        out_shape=shape_of(4, 192, 128),
        cost_estimate=pl.CostEstimate(flops=0, bytes_accessed=1500000, transcendentals=0),
        name="slip",
    )(shear, yields, u, v, region, plastic, *halo_one)
    lines = exchange(send, "narrow")

    t = TABLES
    send = call(
        dip_kernel, shape_of(768, 128), (t["radix"], t["dip_turn"], t["dip_out"], lines), name="dip"
    )
    waves = all_exchange(send)

    new_u, new_v, first, last, left, right = pl.pallas_call(
        step_one_kernel,
        grid=(16,),
        in_specs=[
            SMEM, SMEM, near(16), plane_block,
            pl.BlockSpec((1, 64, 256), lambda z: (z, 0, 0)), full((64, 256)),
        ]
        + halo_specs,
        out_specs=[plane_block] * 2 + [full(s.shape) for s in edge_shapes],
        out_shape=[shape_of(3, 16, 64, 256)] * 2 + edge_shapes,
        cost_estimate=pl.CostEstimate(flops=0, bytes_accessed=14000000, transcendentals=0),
        name="step_one",
    )(shear, yields, u, v, region, plastic, *halo_one)
    halo_two = halo(first, last, left, right)

    coefficients = call(
        mirror_kernel,
        shape_of(8, 3, 8, 2048),
        (where, t["reverse"], own, main, edge),
        smem=1,
        scratch=[pltpu.VMEM((144, 2048), F32)] * 2,
        name="mirror",
    )
    send = call(
        strike_kernel,
        shape_of(768, 128),
        (
            t["strike_in"], t["strike_turn"], t["strike_mix"], t["reverse"],
            t["strike_unmix"], t["strike_out"], coefficients, waves,
        ),
        scratch=[pltpu.VMEM((256, 384), F32)] * 3,
        name="strike",
    )
    columns = all_exchange(send)

    later = lambda z: (0, z + 2, 0, 0)
    out_u, out_v = pl.pallas_call(
        step_two_kernel,
        grid=(14,),
        in_specs=[
            SMEM, SMEM, near(16), pl.BlockSpec((3, 1, 64, 256), later),
            pl.BlockSpec((1, 64, 256), lambda z: (z + 2, 0, 0)), full((64, 256)),
        ]
        + halo_specs,
        out_specs=[pl.BlockSpec((3, 1, 64, 256), later)] * 2,
        out_shape=[shape_of(3, 16, 64, 256)] * 2,
        cost_estimate=pl.CostEstimate(flops=0, bytes_accessed=14000000, transcendentals=0),
        name="step_two",
    )(shear, yields, new_u, new_v, region, plastic, *halo_two)

    send = call(
        undip_kernel,
        shape_of(4, 192, 128),
        (t["dip_in"], t["undip_turn"], t["unradix"], columns),
        name="undip",
    )
    tractions = exchange(send, "narrow")
    edges = call(
        traction_edges_kernel,
        [shape_of(8, 256)] * 2 + [shape_of(64, 128)] * 2,
        (tractions,),
        name="traction_edges",
    )
    halo_three = halo(*edges)
    any_spec = pl.BlockSpec(memory_space=pl.ANY)
    return tuple(
        pl.pallas_call(
            last_kernel,
            grid=(1,),
            in_specs=[SMEM, SMEM, near(4), near(2), slab(2), full((64, 256))]
            + halo_specs
            + [full((4, 192, 128)), full((8, 256)), full((8, 256)), full((64, 128)), full((64, 128))]
            + [any_spec] * 2,
            out_specs=[near(2)] * 2,
            out_shape=[shape_of(3, 16, 64, 256)] * 2,
            input_output_aliases={15: 0, 16: 1},
            cost_estimate=pl.CostEstimate(flops=0, bytes_accessed=4000000, transcendentals=0),
            name="last",
        )(
            shear, yields, new_u, new_v, region, plastic, *halo_two,
            tractions, *halo_three, out_u, out_v,
        )
    )


def solution(mesh):
    tile = P(None, None, "wide", "narrow")
    in_specs = (
        tile,
        tile,
        P(None, "wide", "narrow"),
        P("wide", "narrow"),
        P(),
        P(),
        P(None, None, None, ALL, None),
        P(None, None, ALL, None),
    )
    return jax.shard_map(body, mesh=mesh, in_specs=in_specs, out_specs=(tile, tile), check_vma=False)
```

```python
import functools
import math

import jax
import jax.numpy as jnp
import ml_dtypes
import numpy as np
from jax import lax
from jax.experimental import pallas as pl
from jax.experimental.pallas import tpu as pltpu
from jax.sharding import PartitionSpec as P

DT = 0.1
DAMPING = 0.5
ALL = ("wide", "narrow")
PLANES = 2
F32 = jnp.float32
BF16 = jnp.bfloat16


def split_table(table):
    table = np.asarray(table, np.float64)
    high = table.astype(ml_dtypes.bfloat16)
    low = (table - high.astype(np.float64)).astype(ml_dtypes.bfloat16)
    return np.stack([high, low])


def make_tables():
    factor = 1.0 / math.sqrt(2048 * 1024)
    eye2 = np.eye(2)
    eye4 = np.eye(4)
    eye8 = np.eye(8)
    eye16 = np.eye(16)
    r8 = np.arange(8).reshape(2, 4)
    y1 = np.arange(8).reshape(4, 2)
    theta = 2 * np.pi * r8[:, :, None, None] * y1[None, None] / 8
    radix = np.stack([np.cos(theta), -np.sin(theta)])
    radix = np.einsum("isrnl,xz,fg->isxfrnglz", radix, eye16, eye2).reshape(512, 256)
    unradix = np.stack([np.cos(theta), -np.sin(theta)])
    unradix = np.einsum("isrnl,xz,fg->nglzisxfr", unradix, eye16, eye2).reshape(256, 512)
    y0 = np.arange(128)
    theta = 2 * np.pi * r8[:, :, None] * y0 / 1024
    turn = np.stack([np.cos(theta), -np.sin(theta)])[:, :, None, None]
    dip_turn = np.broadcast_to(turn, (2, 2, 16, 2, 4, 128)).reshape(2, 2, 128, 128) * factor
    alt = (-1.0) ** y0
    place = np.stack([np.arange(64), 63 - np.arange(64)])
    theta = 2 * np.pi * place[:, :, None] * y0 / 128
    cos, sin = np.cos(theta), np.sin(theta)
    dip_out = np.zeros((2, 136, 256))
    dip_out[:, :64] = np.concatenate([cos, sin], -1)
    dip_out[:, 64:128] = np.concatenate([-sin, cos], -1)
    dip_out[0, 128, :128] = alt
    dip_in = np.zeros((2, 128, 2, 2, 128))
    for s in range(2):
        rows = slice(s * 64, s * 64 + 64)
        dip_in[0, rows, s, 0] = cos[s]
        dip_in[0, rows, s, 1] = sin[s]
        dip_in[1, rows, s, 0] = -sin[s]
        dip_in[1, rows, s, 1] = cos[s]
    dip_in = dip_in.reshape(256, 512)
    theta = 2 * np.pi * np.outer(y0, y0) / 128
    cos, sin = np.cos(theta), np.sin(theta)
    strike_in = np.block([[cos, -sin], [sin, cos]])
    strike_out = np.block([[cos, -sin], [sin, cos]])
    a = np.arange(16)
    theta = 2 * np.pi * np.outer(a, y0) / 2048
    turn = np.stack([np.cos(theta), -np.sin(theta)])
    strike_turn = np.broadcast_to(turn[:, :, None], (2, 16, 8, 128)).reshape(2, 128, 128)
    theta = 2 * np.pi * np.outer(a, a) / 16
    cos, sin = np.kron(np.cos(theta), eye8), np.kron(np.sin(theta), eye8)
    strike_mix = np.block([[cos, sin], [-sin, cos]])
    strike_unmix = np.block([[cos, -sin], [sin, cos]]) * factor
    reverse = np.zeros((128, 128))
    reverse[(128 - y0) % 128, y0] = 1.0
    return {
        "radix": split_table(radix),
        "unradix": split_table(unradix),
        "dip_turn": dip_turn.astype(np.float32),
        "undip_turn": (dip_turn / factor * 2.0).astype(np.float32),
        "dip_out": split_table(dip_out),
        "dip_in": split_table(dip_in),
        "strike_in": split_table(strike_in),
        "strike_out": split_table(strike_out),
        "strike_turn": strike_turn.astype(np.float32),
        "strike_mix": split_table(strike_mix),
        "strike_unmix": split_table(strike_unmix),
        "reverse": reverse.astype(ml_dtypes.bfloat16),
    }


TABLES = make_tables()


def halves(x):
    high = x.astype(BF16)
    return high, (x - high.astype(F32)).astype(BF16)


def dot(a, b, contract=(1, 0)):
    return lax.dot_general(
        a, b, (((contract[0],), (contract[1],)), ((), ())), preferred_element_type=F32
    )


def left_dot(table, x, contract=(1, 0)):
    high, low = halves(x)
    return dot(table[0], high, contract) + (
        dot(table[1], high, contract) + dot(table[0], low, contract)
    )


def right_dot(x, table):
    high, low = halves(x)
    return dot(high, table[0]) + (dot(low, table[0]) + dot(high, table[1]))


def lanes(shape):
    return lax.broadcasted_iota(jnp.int32, shape, len(shape) - 1)


def rows_of(shape):
    return lax.broadcasted_iota(jnp.int32, shape, len(shape) - 2)


def neighbour_sum(center, above, below, before, after, left, right):
    rows = rows_of(center.shape)
    north = jnp.where(rows == 0, before, pltpu.roll(center, 1, 0))
    south = jnp.where(rows == 7, after, pltpu.roll(center, 7, 0))
    c0, c1 = center[:, :128], center[:, 128:]
    lane = lanes(c0.shape)
    w0, w1 = pltpu.roll(c0, 1, 1), pltpu.roll(c1, 1, 1)
    e0, e1 = pltpu.roll(c0, 127, 1), pltpu.roll(c1, 127, 1)
    west = jnp.concatenate([jnp.where(lane == 0, left, w0), jnp.where(lane == 0, w0, w1)], 1)
    east = jnp.concatenate([jnp.where(lane == 127, e1, e0), jnp.where(lane == 127, right, e1)], 1)
    total = (north + south) + (west + east)
    for other in (above, below):
        if other is not None:
            total = total + other
    return total


def strip_force(centers, sums, region, plastic, shear_ref, yields_ref):
    one = jnp.ones((8, 128), F32)
    wide = lambda x: jnp.concatenate([x, x], 1)
    modulus = wide(one * shear_ref[0])
    level = one * yields_ref[0]
    level = wide(1.0 / (level * level))
    for label in range(1, 4):
        modulus = jnp.where(region == label, shear_ref[label], modulus)
        other = one * yields_ref[label]
        level = jnp.where(region == label, wide(1.0 / (other * other)), level)
    force = [modulus * (total - 6.0 * center) for total, center in zip(sums, centers)]
    squares = force[0] * force[0] + force[1] * force[1] + force[2] * force[2]
    capped = lax.rsqrt(1.0 + squares * level)
    scaling = jnp.where(plastic > 0.5, capped, 1.0)
    return [f * scaling for f in force]


def strip_of(i):
    return slice(i * 8, i * 8 + 8)


def stencil_strip(i, load, beside, load_above, load_below, halo_refs, z):
    top_ref, bottom_ref, left_ref, right_ref = halo_refs
    centers, sums = [], []
    for c in range(3):
        place = slot(c, z)
        center = load(c, strip_of(i))
        if i == 0:
            before = top_ref[pl.ds(place, 1), :]
        else:
            before = load(c, slice(i * 8 - 1, i * 8))
        if i == 7:
            after = bottom_ref[pl.ds(place, 1), :]
        else:
            after = load(c, slice(i * 8 + 8, i * 8 + 9))
        left = pltpu.roll(left_ref[strip_of(i), :], lax.rem(128 - place, 128), 1)
        right = pltpu.roll(right_ref[strip_of(i), :], 127 - place, 1)
        if beside is not None:
            before, after, left, right = beside(c, i, before, after, left, right)
        above = load_above(c, strip_of(i)) if load_above else None
        below = load_below(c, strip_of(i)) if load_below else None
        sums.append(neighbour_sum(center, above, below, before, after, left, right))
        centers.append(center)
    return centers, sums


def slot(c, z):
    return c * 16 + z


def put_columns(left_ref, right_ref, strip, i, place):
    c0, c1 = strip[:, :128], strip[:, 128:]
    lane = lanes(c0.shape)
    rows = strip_of(i)
    left_ref[rows, :] = jnp.where(lane == place, pltpu.roll(c0, place, 1), left_ref[rows, :])
    right_ref[rows, :] = jnp.where(
        lane == place, pltpu.roll(c1, lax.rem(place + 1, 128), 1), right_ref[rows, :]
    )


def edges_kernel(u_ref, flags_ref, first_ref, last_ref, left_ref, right_ref, plastic_ref):
    step = pl.program_id(0)

    @pl.when(step == 0)
    def _():
        left_ref[...] = jnp.zeros_like(left_ref)
        right_ref[...] = jnp.zeros_like(right_ref)
        wide = (rows_of((64, 8)) // 8 == lanes((64, 8))).astype(F32)
        high = (rows_of((32, 256)) == lanes((32, 256)) // 8).astype(F32)
        marks = (flags_ref[...] == 1).astype(F32)
        plastic_ref[...] = dot(dot(wide, marks), high)

    for k in range(u_ref.shape[1]):
        z = step * u_ref.shape[1] + k
        for c in range(3):
            place = slot(c, z)
            first_ref[pl.ds(place, 1), :] = u_ref[c, k, 0:1, :]
            last_ref[pl.ds(place, 1), :] = u_ref[c, k, 63:64, :]
            for i in range(8):
                put_columns(left_ref, right_ref, u_ref[c, k, strip_of(i), :], i, place)


def slip_kernel(
    shear_ref, yields_ref, u_ref, v_ref, region_ref, plastic_ref,
    top_ref, bottom_ref, left_ref, right_ref, _after_ref, send_ref,
):
    halo_refs = (top_ref, bottom_ref, left_ref, right_ref)
    for i in range(8):
        rows = strip_of(i)
        centers, sums = stencil_strip(
            i,
            lambda c, r: u_ref[c, 0, r, :],
            None,
            lambda c, r: u_ref[c, 1, r, :],
            None,
            halo_refs,
            0,
        )
        force = strip_force(
            centers, sums, region_ref[0, rows, :], plastic_ref[rows, :], shear_ref, yields_ref
        )
        n, part = i // 2, (i % 2) * 8
        for c in range(3):
            v = v_ref[c, 0, rows, :]
            v = v + DT * (force[c] - DAMPING * v)
            moved = centers[c] + DT * v
            for f, values in enumerate((centers[c], moved)):
                for half in range(2):
                    start = f * 96 + c * 32 + half * 16 + part
                    send_ref[n, start : start + 8, :] = values[:, half * 128 : half * 128 + 128]


def step_one_kernel(
    shear_ref, yields_ref, u_ref, v_ref, region_ref, plastic_ref,
    top_ref, bottom_ref, left_ref, right_ref, _after_ref,
    new_u_ref, new_v_ref, first_ref, last_ref, left_out_ref, right_out_ref,
):
    step = pl.program_id(0)

    @pl.when(step == 0)
    def _():
        left_out_ref[...] = jnp.zeros_like(left_out_ref)
        right_out_ref[...] = jnp.zeros_like(right_out_ref)

    halo_refs = (top_ref, bottom_ref, left_ref, right_ref)
    for k in range(PLANES):
        z = step * PLANES + k
        damping = jnp.where(z == 0, DAMPING, 0.0).astype(F32)
        lower = jnp.where(z > 0, 1.0, 0.0).astype(F32)
        upper = jnp.where(z < 15, 1.0, 0.0).astype(F32)
        if k < PLANES - 1:
            load_above = lambda c, r: u_ref[c, z + 1, r, :]
        else:
            load_above = lambda c, r: u_ref[c, jnp.minimum(z + 1, 15), r, :] * upper
        if k > 0:
            load_below = lambda c, r: u_ref[c, z - 1, r, :]
        else:
            load_below = lambda c, r: u_ref[c, jnp.maximum(z - 1, 0), r, :] * lower
        for i in range(8):
            rows = strip_of(i)
            centers, sums = stencil_strip(
                i, lambda c, r: u_ref[c, z, r, :], None, load_above, load_below, halo_refs, z
            )
            force = strip_force(
                centers, sums, region_ref[k, rows, :], plastic_ref[rows, :], shear_ref, yields_ref
            )
            for c in range(3):
                v = v_ref[c, k, rows, :]
                v = v + DT * (force[c] - damping * v)
                u = centers[c] + DT * v
                new_v_ref[c, k, rows, :] = v
                new_u_ref[c, k, rows, :] = u
                place = slot(c, z)
                if i == 0:
                    first_ref[pl.ds(place, 1), :] = u[0:1]
                if i == 7:
                    last_ref[pl.ds(place, 1), :] = u[7:8]
                put_columns(left_out_ref, right_out_ref, u, i, place)


def step_two_kernel(start, *refs):
    (shear_ref, yields_ref, u_ref, v_ref, region_ref, plastic_ref) = refs[:6]
    halo_refs = refs[6:10]
    new_u_ref, new_v_ref = refs[-2:]
    for k in range(PLANES):
        z = pl.program_id(0) * PLANES + (start + k)
        upper = jnp.where(z < 15, 1.0, 0.0).astype(F32)
        if k < PLANES - 1:
            load_above = lambda c, r: u_ref[c, z + 1, r, :]
        else:
            load_above = lambda c, r: u_ref[c, jnp.minimum(z + 1, 15), r, :] * upper
        for i in range(8):
            rows = strip_of(i)
            centers, sums = stencil_strip(
                i,
                lambda c, r: u_ref[c, z, r, :],
                None,
                load_above,
                lambda c, r: u_ref[c, z - 1, r, :],
                halo_refs,
                z,
            )
            force = strip_force(
                centers, sums, region_ref[k, rows, :], plastic_ref[rows, :], shear_ref, yields_ref
            )
            for c in range(3):
                v = v_ref[c, k, rows, :] + DT * force[c]
                new_v_ref[c, k, rows, :] = v
                new_u_ref[c, k, rows, :] = centers[c] + DT * v


def last_kernel(
    shear_ref, yields_ref, u_ref, v_ref, region_ref, plastic_ref,
    top_ref, bottom_ref, left_ref, right_ref,
    recv_ref, _old_u_ref, _old_v_ref, new_u_ref, new_v_ref, surface,
):
    square = DT * DT
    halo_refs = (top_ref, bottom_ref, left_ref, right_ref)

    def traction(f, c, i):
        start = f * 96 + c * 32 + (i % 2) * 8
        return jnp.concatenate(
            [recv_ref[i // 2, start + half * 16 : start + half * 16 + 8, :] for half in range(2)], 1
        )

    def outside(n, c, side):
        row = 208 + c * 2 + side
        return jnp.concatenate(
            [recv_ref[n, row + half * 8 : row + half * 8 + 1, :] for half in range(2)], 1
        )

    def beside(c, i, before, after, left, right):
        if i == 0:
            before = before + square * outside(0, c, 0)
        if i == 7:
            after = after + square * outside(3, c, 1)
        start = 192 + (i % 2) * 8
        columns = recv_ref[i // 2, start : start + 8, :]
        left = left + square * pltpu.roll(columns, (128 - c) % 128, 1)
        right = right + square * pltpu.roll(columns, 127 - (3 + c), 1)
        return before, after, left, right

    for i in range(8):
        for c in range(3):
            surface[c, strip_of(i), :] = u_ref[c, 0, strip_of(i), :] + square * traction(0, c, i)
    for z in range(2):
        for i in range(8):
            rows = strip_of(i)
            above = lambda c, r: u_ref[c, z + 1, r, :]
            if z == 0:
                load, below = lambda c, r: surface[c, r, :], None
            else:
                load, below = lambda c, r: u_ref[c, 1, r, :], lambda c, r: surface[c, r, :]
            centers, sums = stencil_strip(
                i, load, beside if z == 0 else None, above, below, halo_refs, z
            )
            force = strip_force(
                centers, sums, region_ref[z, rows, :], plastic_ref[rows, :], shear_ref, yields_ref
            )
            for c in range(3):
                v = v_ref[c, z, rows, :]
                if z == 0:
                    v = v + DT * traction(0, c, i)
                    v = v + DT * (force[c] + (traction(1, c, i) - DAMPING * v))
                else:
                    v = v + DT * force[c]
                new_v_ref[c, z, rows, :] = v
                new_u_ref[c, z, rows, :] = centers[c] + DT * v


def history_kernel(where_ref, kernel_ref, history_ref, *refs):
    own_ref, main_ref, edge_ref = refs[-3:]
    low = where_ref[0] == 1
    width = own_ref.shape[1]

    def step(m, carry):
        total, ones = carry
        out, twos = [], []
        for c in range(3):
            two = kernel_ref[m + 2, c].astype(F32)
            twos.append(two)
            for ri in range(2):
                past = history_ref[m, ri, c].astype(F32)
                p1, p2 = total[c * 2 + ri]
                out.append((p1 + ones[c] * past, p2 + two * past))
        return tuple(out), tuple(twos)

    zero = jnp.zeros((8, width), F32)
    total, _ = lax.fori_loop(
        0, 31, step,
        (tuple((zero, zero) for _ in range(6)), tuple(kernel_ref[1, c].astype(F32) for c in range(3))),
    )
    values = [None] * 18
    for c in range(3):
        one = kernel_ref[32, c].astype(F32)
        for ri in range(2):
            p1, p2 = total[c * 2 + ri]
            values[ri * 3 + c] = p1 + one * history_ref[31, ri, c].astype(F32)
            values[6 + ri * 3 + c] = p2
        values[12 + c] = kernel_ref[0, c].astype(F32)
        values[15 + c] = kernel_ref[1, c].astype(F32)
    for i, value in enumerate(values):
        row = [value[r : r + 1] for r in range(8)]
        for r, (a, b) in enumerate(((0, 4), (1, 3), (2, 2), (3, 1))):
            own_ref[i * 4 + r : i * 4 + r + 1, :] = jnp.where(low, row[a], row[b])
        for r, (a, b) in enumerate(((4, 4), (5, 7), (6, 6), (7, 5))):
            main_ref[i * 4 + r : i * 4 + r + 1, :] = jnp.where(low, row[a], row[b])
        edge_ref[i : i + 1, :] = row[0]


def mirror_kernel(where_ref, reverse_ref, own_ref, main_ref, edge_ref, out_ref, tiles, turned):
    low = where_ref[0] == 1
    special = where_ref[1]
    for i in range(18):
        own = own_ref[i * 4 : i * 4 + 4, :]
        main = main_ref[i * 4 : i * 4 + 4, :]
        edge = edge_ref[i : i + 1, :]
        other = jnp.where(rows_of(main.shape) == 0, edge, main)
        tiles[i * 8 : i * 8 + 4, :] = jnp.where(low, own, main)
        tiles[i * 8 + 4 : i * 8 + 8, :] = jnp.where(low, other, own)
    for block in range(16):
        part = slice(block * 128, block * 128 + 128)
        high, rest = halves(tiles[:, part])
        turned[:, part] = dot(high, reverse_ref[...]) + dot(rest, reverse_ref[...])
    lane = lanes((8, 128))
    row = rows_of((8, 128))
    upper = row >= 4
    chosen = (lax.rem(row, 4) + (1 - special)) == 0

    def swap(x):
        return pltpu.roll(x, 4, 0)

    for block in range(16):
        part = slice(block * 128, block * 128 + 128)
        mirror = slice((15 - block) * 128, (15 - block) * 128 + 128)
        first = ((16 - block) % 16) * 128
        first = slice(first, first + 128)

        def load(i):
            rows = slice(i * 8, i * 8 + 8)
            back = jnp.where(lane == 0, turned[rows, first], turned[rows, mirror])
            return tiles[rows, part], back

        for c in range(3):
            for k in range(2):
                t, b = load(12 + k * 3 + c)
                own = 0.5 * (t + b)
                other = swap(own)
                mean = jnp.where(chosen, 0.5 * (own + other), 0.5 * (t + swap(b)))
                diff = jnp.where(chosen, 0.5 * (own - other), 0.0)
                out_ref[k, c, :, part] = jnp.where(upper, swap(mean), mean)
                out_ref[2 + k, c, :, part] = jnp.where(upper, swap(diff), diff)
            pair = []
            for k in range(2):
                tr, br = load(k * 6 + c)
                ti, bi = load(k * 6 + 3 + c)
                hr, hi = 0.5 * (tr + br), 0.5 * (ti - bi)
                sr, si = swap(hr), swap(hi)
                pair.append(
                    (
                        jnp.where(chosen, hr - si, 0.5 * (tr + swap(br))),
                        jnp.where(chosen, hi + sr, 0.5 * (ti - swap(bi))),
                        hr + si,
                        hi - sr,
                    )
                )
            out_ref[4, c, :, part] = jnp.where(upper, swap(pair[1][0]), pair[0][0])
            out_ref[5, c, :, part] = jnp.where(upper, swap(pair[1][1]), pair[0][1])
            out_ref[6, c, :, part] = pair[0][2]
            out_ref[7, c, :, part] = pair[0][3]


def dip_kernel(radix_ref, turn_ref, out_table_ref, recv_ref, _after_ref, send_ref):
    wide = []
    for c in range(3):
        pieces = []
        for n in range(4):
            for f in range(2):
                start = f * 96 + c * 32
                pieces.append(recv_ref[n, start : start + 32, :])
        wide.append(jnp.concatenate(pieces, 0))
    z = left_dot(radix_ref, jnp.concatenate(wide, 1))
    lane = lanes((1, 128))
    for s in range(2):
        tr, ti = turn_ref[0, s], turn_ref[1, s]
        for c in range(3):
            part = slice(c * 128, c * 128 + 128)
            zr = z[s * 128 : s * 128 + 128, part]
            zi = z[256 + s * 128 : 384 + s * 128, part]
            turned = jnp.concatenate([zr * tr - zi * ti, zr * ti + zi * tr], 1)
            high, low = halves(turned)
            table, rest = out_table_ref[0, s], out_table_ref[1, s]
            res = dot(table, high, (1, 1)) + (dot(rest, high, (1, 1)) + dot(table, low, (1, 1)))
            imag = res[64:128]
            if s == 0:
                extra = jnp.where(lax.rem(lane, 4) == 0, res[128:129], 0.0)
                imag = jnp.where(rows_of(imag.shape) == 0, imag + extra, imag)
            send_ref[pl.ds(s * 384 + c * 2, 64, stride=6), :] = res[0:64]
            send_ref[pl.ds(s * 384 + c * 2 + 1, 64, stride=6), :] = imag


def strike_kernel(
    in_ref, turn_ref, mix_ref, reverse_ref, unmix_ref, out_table_ref,
    coef_ref, recv_ref, _after_ref, send_ref, spec, back, total,
):
    tr, ti = turn_ref[0], turn_ref[1]
    real, imag = [], []
    for c in range(3):
        re = recv_ref[pl.ds(c * 2, 128, stride=6), :].T
        im = recv_ref[pl.ds(c * 2 + 1, 128, stride=6), :].T
        y = right_dot(jnp.concatenate([re, im], 1), in_ref)
        yr, yi = y[:, :128], y[:, 128:]
        real.append(yr * tr - yi * ti)
        imag.append(yr * ti + yi * tr)
    stacked = jnp.concatenate([jnp.concatenate(real, 1), jnp.concatenate(imag, 1)], 0)
    spec[...] = left_dot(mix_ref, stacked)
    for c in range(3):
        part = slice(c * 128, c * 128 + 128)
        high, low = halves(spec[:, part])
        back[:, part] = dot(high, reverse_ref[...]) + dot(low, reverse_ref[...])
    lane = lanes((8, 128))
    upper = rows_of((8, 128)) >= 4

    def swap(x):
        return pltpu.roll(x, 4, 0)

    for c in range(3):
        part = slice(c * 128, c * 128 + 128)
        for block in range(16):
            wave = slice(block * 128, block * 128 + 128)
            a0, a1 = coef_ref[0, c, :, wave], coef_ref[1, c, :, wave]
            m0, m1 = coef_ref[2, c, :, wave], coef_ref[3, c, :, wave]
            for ri in range(2):
                rows = slice(ri * 128 + block * 8, ri * 128 + block * 8 + 8)
                first = ri * 128 + ((16 - block) % 16) * 8
                other = ri * 128 + (15 - block) * 8
                s = spec[rows, part]
                r = jnp.where(
                    lane == 0, back[first : first + 8, part], back[other : other + 8, part]
                )
                if ri == 1:
                    r = -r
                t = a0 * s + m0 * r + coef_ref[4 + ri, c, :, wave]
                q = a0 * r + m0 * s + coef_ref[6 + ri, c, :, wave]
                more = (DT * DT) * (a0 * swap(t) + m0 * swap(q)) + a1 * swap(s) + m1 * swap(r)
                total[rows, part] = t + jnp.where(upper, more, 0.0)
    y = left_dot(unmix_ref, total[...])
    owner = rows_of((128, 128))
    wide_lane = lanes((128, 128))
    extra = [jnp.zeros((128, 128), F32)] * 2
    for c in range(3):
        part = slice(c * 128, c * 128 + 128)
        yr, yi = y[:128, part], y[128:, part]
        turned = jnp.concatenate([yr * tr + yi * ti, yi * tr - yr * ti], 1)
        high, low = halves(turned)
        res = dot(out_table_ref[0], high, (1, 1)) + (
            dot(out_table_ref[1], high, (1, 1)) + dot(out_table_ref[0], low, (1, 1))
        )
        for ri in range(2):
            lines = res[ri * 128 : ri * 128 + 128]
            send_ref[pl.ds(c * 2 + ri, 128, stride=8), :] = lines
            for side in range(2):
                group = c * 2 + side
                if side == 0:
                    moved = jnp.where(owner == 0, 0.0, pltpu.roll(lines, 1, 0))
                    moved = pltpu.roll(moved, (group * 8 + 8) % 128, 1)
                else:
                    moved = jnp.where(owner == 127, 0.0, pltpu.roll(lines, 127, 0))
                    moved = pltpu.roll(moved, group * 8, 1) if group else moved
                extra[ri] = jnp.where(wide_lane // 8 == group, moved, extra[ri])
    for ri in range(2):
        send_ref[pl.ds(6 + ri, 128, stride=8), :] = extra[ri]


def undip_kernel(in_ref, turn_ref, unradix_ref, recv_ref, _after_ref, send_ref):
    row = rows_of((128, 128))
    lane = lanes((128, 128))
    alt = jnp.where(lax.rem(lane, 2) == 0, 0.5, -0.5).astype(F32)
    stacks = [[], [], [], []]
    for c in range(4):
        re = recv_ref[pl.ds(c * 2, 128, stride=8), :].T
        im = recv_ref[pl.ds(c * 2 + 1, 128, stride=8), :].T
        h = right_dot(jnp.concatenate([re, im], 1), in_ref)
        for s in range(2):
            hr = h[:, s * 256 : s * 256 + 128]
            hi = h[:, s * 256 + 128 : s * 256 + 256]
            if s == 0:
                fix = alt * im[:, 0:1] - 0.5 * re[:, 0:1]
                hr = hr + jnp.where(lax.rem(row, 4) == 0, fix, 0.0)
            tr, ti = turn_ref[0, s], turn_ref[1, s]
            stacks[s].append(hr * tr + hi * ti)
            stacks[2 + s].append(hi * tr - hr * ti)
    stacked = jnp.concatenate([jnp.concatenate(part, 1) for part in stacks], 0)
    out = left_dot(unradix_ref, stacked)
    for n in range(4):
        for f in range(2):
            for c in range(3):
                start = f * 96 + c * 32
                row0 = (n * 2 + f) * 32
                send_ref[n, start : start + 32, :] = out[row0 : row0 + 32, c * 128 : c * 128 + 128]
    small = lanes((16, 128))

    def plane(n, half, c):
        row0 = n * 64 + half * 16
        return out[row0 : row0 + 16, c * 128 : c * 128 + 128]

    for n in range(4):
        columns = jnp.zeros((16, 128), F32)
        for c in range(3):
            if n > 0:
                moved = pltpu.roll(plane(n - 1, 1, c), c + 1, 1)
                columns = jnp.where(small == c, moved, columns)
            if n < 3:
                moved = pltpu.roll(plane(n + 1, 0, c), 3 + c, 1)
                columns = jnp.where(small == 3 + c, moved, columns)
        send_ref[n, 192:208, :] = columns
        for half in range(2):
            send_ref[n, 208 + half * 8 : 216 + half * 8, :] = plane(n, half, 3)[:8]


def full(shape):
    zeros = (0,) * len(shape)
    return pl.BlockSpec(shape, lambda *_: zeros)


SMEM = pl.BlockSpec(memory_space=pltpu.SMEM)


def shape_of(*shape):
    return jax.ShapeDtypeStruct(shape, F32)


def call(body, out_shape, args, smem=0, scratch=(), after=(), name=None):
    outs = out_shape if isinstance(out_shape, (tuple, list)) else [out_shape]
    size = sum(math.prod(x.shape) * 4 for x in list(args) + list(outs))
    out_specs = [full(x.shape) for x in outs]
    return pl.pallas_call(
        body,
        grid=(1,),
        in_specs=[SMEM] * smem
        + [full(x.shape) for x in args[smem:]]
        + [pl.BlockSpec(memory_space=pl.ANY)] * len(after),
        out_specs=out_specs if isinstance(out_shape, (tuple, list)) else out_specs[0],
        out_shape=out_shape,
        scratch_shapes=scratch,
        cost_estimate=pl.CostEstimate(flops=0, bytes_accessed=size, transcendentals=0),
        name=name,
    )(*args, *after)


def halo(first, last, left, right):
    up = [(i, i + 1) for i in range(31)]
    down = [(i + 1, i) for i in range(31)]
    top = lax.ppermute(last, "wide", up)
    bottom = lax.ppermute(first, "wide", down)
    up = [(i, i + 1) for i in range(3)]
    down = [(i + 1, i) for i in range(3)]
    from_left = lax.ppermute(right, "narrow", up)
    from_right = lax.ppermute(left, "narrow", down)
    return top, bottom, from_left, from_right


def exchange(x, axis):
    return lax.all_to_all(x, axis, split_axis=0, concat_axis=0, tiled=True)


def body(u, v, region, flags, shear, yields, history, kernel):
    device = lax.axis_index(ALL)
    where = jnp.stack([device < 64, device == 0]).astype(jnp.int32)
    edge_shapes = [shape_of(48, 256)] * 2 + [shape_of(64, 128)] * 2
    near = lambda depth: pl.BlockSpec((3, depth, 64, 256), lambda *_: (0, 0, 0, 0))
    slab = lambda depth: pl.BlockSpec((depth, 64, 256), lambda *_: (0, 0, 0))
    planes = lambda depth, start=0: pl.BlockSpec(
        (3, depth, 64, 256), lambda z: (0, z + start // depth, 0, 0)
    )
    slabs = lambda depth, start=0: pl.BlockSpec(
        (depth, 64, 256), lambda z: (z + start // depth, 0, 0)
    )
    halo_specs = [full((48, 256))] * 2 + [full((64, 128))] * 2
    any_spec = pl.BlockSpec(memory_space=pl.ANY)
    t = TABLES

    first, last, left, right, plastic = pl.pallas_call(
        edges_kernel,
        grid=(4,),
        in_specs=[planes(4), full((8, 32))],
        out_specs=[full(s.shape) for s in edge_shapes] + [full((64, 256))],
        out_shape=edge_shapes + [shape_of(64, 256)],
        cost_estimate=pl.CostEstimate(flops=0, bytes_accessed=3300000, transcendentals=0),
        name="edges",
    )(u, flags)
    halo_one = halo(first, last, left, right)

    width = 256
    steps = 1024 // width

    def sums(part, after):
        shift = part * steps
        given = [] if part == 0 else list(after)
        return pl.pallas_call(
            history_kernel,
            grid=(steps,),
            in_specs=[
                SMEM,
                pl.BlockSpec((33, 3, 8, width), lambda i: (0, 0, 0, i + shift)),
                pl.BlockSpec((32, 2, 3, 8, width), lambda i: (0, 0, 0, 0, i + shift)),
            ]
            + [any_spec] * len(given),
            out_specs=[
                pl.BlockSpec((72, width), lambda i: (0, i + shift)),
                pl.BlockSpec((72, width), lambda i: (0, i + shift)),
                pl.BlockSpec((18, width), lambda i: (0, i + shift)),
            ],
            out_shape=[shape_of(72, 2048), shape_of(72, 2048), shape_of(18, 2048)],
            input_output_aliases={3: 0, 4: 1, 5: 2} if given else {},
            cost_estimate=pl.CostEstimate(flops=0, bytes_accessed=5500000, transcendentals=0),
            name="history",
        )(where, kernel, history, *given)

    partial = sums(0, None)
    send = pl.pallas_call(
        slip_kernel,
        grid=(1,),
        in_specs=[SMEM, SMEM, near(2), near(1), slab(1), full((64, 256))] + halo_specs + [any_spec],
        out_specs=full((4, 192, 128)),
        out_shape=shape_of(4, 192, 128),
        cost_estimate=pl.CostEstimate(flops=0, bytes_accessed=1500000, transcendentals=0),
        name="slip",
    )(shear, yields, u, v, region, plastic, *halo_one, partial[2])
    lines = exchange(send, "narrow")
    own, main, edge = sums(1, partial)
    main = lax.ppermute(main, ALL, [(i, 127 - i) for i in range(128)])
    edge = lax.ppermute(edge, ALL, [(64, 0)] + [(i, 128 - i) for i in range(65, 128)])

    send = call(
        dip_kernel, shape_of(768, 128), (t["radix"], t["dip_turn"], t["dip_out"], lines),
        after=[own], name="dip",
    )
    waves = exchange(send.reshape(128, 1, 768), ALL).reshape(768, 128)

    new_u, new_v, first, last, left, right = pl.pallas_call(
        step_one_kernel,
        grid=(16 // PLANES,),
        in_specs=[SMEM, SMEM, near(16), planes(PLANES), slabs(PLANES), full((64, 256))]
        + halo_specs
        + [any_spec],
        out_specs=[planes(PLANES)] * 2 + [full(s.shape) for s in edge_shapes],
        out_shape=[shape_of(3, 16, 64, 256)] * 2 + edge_shapes,
        cost_estimate=pl.CostEstimate(flops=0, bytes_accessed=14000000, transcendentals=0),
        name="step_one",
    )(shear, yields, u, v, region, plastic, *halo_one, send)
    halo_two = halo(first, last, left, right)

    coefficients = call(
        mirror_kernel,
        shape_of(8, 3, 8, 2048),
        (where, t["reverse"], own, main, edge),
        smem=1,
        scratch=[pltpu.VMEM((144, 2048), F32)] * 2,
        name="mirror",
    )
    send = call(
        strike_kernel,
        shape_of(1024, 128),
        (
            t["strike_in"], t["strike_turn"], t["strike_mix"], t["reverse"],
            t["strike_unmix"], t["strike_out"], coefficients, waves,
        ),
        scratch=[pltpu.VMEM((256, 384), F32)] * 3,
        after=[new_u],
        name="strike",
    )
    columns = exchange(send.reshape(128, 8, 128), ALL).reshape(1024, 128)

    def later(start, stop, given, after):
        return pl.pallas_call(
            functools.partial(step_two_kernel, start),
            grid=((stop - start) // PLANES,),
            in_specs=[
                SMEM, SMEM, near(16), planes(PLANES, start), slabs(PLANES, start), full((64, 256)),
            ]
            + halo_specs
            + [any_spec] * (len(given) + 1),
            out_specs=[planes(PLANES, start)] * 2,
            out_shape=[shape_of(3, 16, 64, 256)] * 2,
            input_output_aliases={10: 0, 11: 1} if given else {},
            cost_estimate=pl.CostEstimate(
                flops=0, bytes_accessed=(stop - start) * 800000, transcendentals=0
            ),
            name="step_two",
        )(shear, yields, new_u, new_v, region, plastic, *halo_two, *given, after)

    out = later(2, 10, [], send)
    send = call(
        undip_kernel,
        shape_of(4, 224, 128),
        (t["dip_in"], t["undip_turn"], t["unradix"], columns),
        after=[out[0]],
        name="undip",
    )
    tractions = exchange(send, "narrow")
    out = later(10, 16, out, send)
    return tuple(
        pl.pallas_call(
            last_kernel,
            grid=(1,),
            in_specs=[SMEM, SMEM, near(4), near(2), slab(2), full((64, 256))]
            + halo_specs
            + [full((4, 224, 128))]
            + [any_spec] * 2,
            out_specs=[near(2)] * 2,
            out_shape=[shape_of(3, 16, 64, 256)] * 2,
            scratch_shapes=[pltpu.VMEM((3, 64, 256), F32)],
            input_output_aliases={11: 0, 12: 1},
            cost_estimate=pl.CostEstimate(flops=0, bytes_accessed=4000000, transcendentals=0),
            name="last",
        )(shear, yields, new_u, new_v, region, plastic, *halo_two, tractions, *out)
    )


def solution(mesh):
    tile = P(None, None, "wide", "narrow")
    in_specs = (
        tile,
        tile,
        P(None, "wide", "narrow"),
        P("wide", "narrow"),
        P(),
        P(),
        P(None, None, None, ALL, None),
        P(None, None, ALL, None),
    )
    return jax.shard_map(body, mesh=mesh, in_specs=in_specs, out_specs=(tile, tile), check_vma=False)
```

```python
import functools
import math

import jax
import jax.numpy as jnp
import ml_dtypes
import numpy as np
from jax import lax
from jax.experimental import pallas as pl
from jax.experimental.pallas import tpu as pltpu
from jax.sharding import PartitionSpec as P

DT = 0.1
DAMPING = 0.5
ALL = ("wide", "narrow")
PLANES = 2
F32 = jnp.float32
BF16 = jnp.bfloat16


def split_table(table):
    table = np.asarray(table, np.float64)
    high = table.astype(ml_dtypes.bfloat16)
    low = (table - high.astype(np.float64)).astype(ml_dtypes.bfloat16)
    return np.stack([high, low])


def make_tables():
    factor = 1.0 / math.sqrt(2048 * 1024)
    eye2 = np.eye(2)
    eye4 = np.eye(4)
    eye8 = np.eye(8)
    eye16 = np.eye(16)
    r8 = np.arange(8).reshape(2, 4)
    y1 = np.arange(8).reshape(4, 2)
    theta = 2 * np.pi * r8[:, :, None, None] * y1[None, None] / 8
    radix = np.stack([np.cos(theta), -np.sin(theta)])
    radix = np.einsum("isrnl,xz,fg->isxfrnglz", radix, eye16, eye2).reshape(512, 256)
    unradix = np.stack([np.cos(theta), -np.sin(theta)])
    unradix = np.einsum("isrnl,xz,fg->nglzisxfr", unradix, eye16, eye2).reshape(256, 512)
    y0 = np.arange(128)
    theta = 2 * np.pi * r8[:, :, None] * y0 / 1024
    turn = np.stack([np.cos(theta), -np.sin(theta)])[:, :, None, None]
    dip_turn = np.broadcast_to(turn, (2, 2, 16, 2, 4, 128)).reshape(2, 2, 128, 128) * factor
    alt = (-1.0) ** y0
    place = np.stack([np.arange(64), 63 - np.arange(64)])
    theta = 2 * np.pi * place[:, :, None] * y0 / 128
    cos, sin = np.cos(theta), np.sin(theta)
    dip_out = np.zeros((2, 136, 256))
    dip_out[:, :64] = np.concatenate([cos, sin], -1)
    dip_out[:, 64:128] = np.concatenate([-sin, cos], -1)
    dip_out[0, 128, :128] = alt
    dip_in = np.zeros((2, 128, 2, 2, 128))
    for s in range(2):
        rows = slice(s * 64, s * 64 + 64)
        dip_in[0, rows, s, 0] = cos[s]
        dip_in[0, rows, s, 1] = sin[s]
        dip_in[1, rows, s, 0] = -sin[s]
        dip_in[1, rows, s, 1] = cos[s]
    dip_in = dip_in.reshape(256, 512)
    theta = 2 * np.pi * np.outer(y0, y0) / 128
    cos, sin = np.cos(theta), np.sin(theta)
    strike_in = np.block([[cos, -sin], [sin, cos]])
    strike_out = np.block([[cos, -sin], [sin, cos]])
    a = np.arange(16)
    theta = 2 * np.pi * np.outer(a, y0) / 2048
    turn = np.stack([np.cos(theta), -np.sin(theta)])
    strike_turn = np.broadcast_to(turn[:, :, None], (2, 16, 8, 128)).reshape(2, 128, 128)
    theta = 2 * np.pi * np.outer(a, a) / 16
    cos, sin = np.kron(np.cos(theta), eye8), np.kron(np.sin(theta), eye8)
    strike_mix = np.block([[cos, sin], [-sin, cos]])
    strike_unmix = np.block([[cos, -sin], [sin, cos]]) * factor
    reverse = np.zeros((128, 128))
    reverse[(128 - y0) % 128, y0] = 1.0
    return {
        "radix": split_table(radix),
        "unradix": split_table(unradix),
        "dip_turn": dip_turn.astype(np.float32),
        "undip_turn": (dip_turn / factor * 2.0).astype(np.float32),
        "dip_out": split_table(dip_out),
        "dip_in": split_table(dip_in),
        "strike_in": split_table(strike_in),
        "strike_out": split_table(strike_out),
        "strike_turn": strike_turn.astype(np.float32),
        "strike_mix": split_table(strike_mix),
        "strike_unmix": split_table(strike_unmix),
        "reverse": reverse.astype(ml_dtypes.bfloat16),
    }


TABLES = make_tables()


def halves(x):
    high = x.astype(BF16)
    return high, (x - high.astype(F32)).astype(BF16)


def dot(a, b, contract=(1, 0)):
    return lax.dot_general(
        a, b, (((contract[0],), (contract[1],)), ((), ())), preferred_element_type=F32
    )


def left_dot(table, x, contract=(1, 0)):
    high, low = halves(x)
    return dot(table[0], high, contract) + (
        dot(table[1], high, contract) + dot(table[0], low, contract)
    )


def right_dot(x, table):
    high, low = halves(x)
    return dot(high, table[0]) + (dot(low, table[0]) + dot(high, table[1]))


def lanes(shape):
    return lax.broadcasted_iota(jnp.int32, shape, len(shape) - 1)


def rows_of(shape):
    return lax.broadcasted_iota(jnp.int32, shape, len(shape) - 2)


def neighbour_sum(center, above, below, before, after, left, right):
    rows = rows_of(center.shape)
    north = jnp.where(rows == 0, before, pltpu.roll(center, 1, 0))
    south = jnp.where(rows == 7, after, pltpu.roll(center, 7, 0))
    c0, c1 = center[:, :128], center[:, 128:]
    lane = lanes(c0.shape)
    w0, w1 = pltpu.roll(c0, 1, 1), pltpu.roll(c1, 1, 1)
    e0, e1 = pltpu.roll(c0, 127, 1), pltpu.roll(c1, 127, 1)
    west = jnp.concatenate([jnp.where(lane == 0, left, w0), jnp.where(lane == 0, w0, w1)], 1)
    east = jnp.concatenate([jnp.where(lane == 127, e1, e0), jnp.where(lane == 127, right, e1)], 1)
    total = (north + south) + (west + east)
    for other in (above, below):
        if other is not None:
            total = total + other
    return total


def strip_force(centers, sums, region, plastic, shear_ref, yields_ref):
    one = jnp.ones((8, 128), F32)
    wide = lambda x: jnp.concatenate([x, x], 1)
    modulus = wide(one * shear_ref[0])
    level = one * yields_ref[0]
    level = wide(1.0 / (level * level))
    for label in range(1, 4):
        modulus = jnp.where(region == label, shear_ref[label], modulus)
        other = one * yields_ref[label]
        level = jnp.where(region == label, wide(1.0 / (other * other)), level)
    force = [modulus * (total - 6.0 * center) for total, center in zip(sums, centers)]
    squares = force[0] * force[0] + force[1] * force[1] + force[2] * force[2]
    capped = lax.rsqrt(1.0 + squares * level)
    scaling = jnp.where(plastic > 0.5, capped, 1.0)
    return [f * scaling for f in force]


def strip_of(i):
    return slice(i * 8, i * 8 + 8)


def stencil_strip(i, load, beside, load_above, load_below, halo_refs, z):
    top_ref, bottom_ref, left_ref, right_ref = halo_refs
    centers, sums = [], []
    for c in range(3):
        place = slot(c, z)
        center = load(c, strip_of(i))
        if i == 0:
            before = top_ref[pl.ds(place, 1), :]
        else:
            before = load(c, slice(i * 8 - 1, i * 8))
        if i == 7:
            after = bottom_ref[pl.ds(place, 1), :]
        else:
            after = load(c, slice(i * 8 + 8, i * 8 + 9))
        left = pltpu.roll(left_ref[strip_of(i), :], lax.rem(128 - place, 128), 1)
        right = pltpu.roll(right_ref[strip_of(i), :], 127 - place, 1)
        if beside is not None:
            before, after, left, right = beside(c, i, before, after, left, right)
        above = load_above(c, strip_of(i)) if load_above else None
        below = load_below(c, strip_of(i)) if load_below else None
        sums.append(neighbour_sum(center, above, below, before, after, left, right))
        centers.append(center)
    return centers, sums


def slot(c, z):
    return c * 16 + z


def put_columns(left_ref, right_ref, strip, i, place):
    c0, c1 = strip[:, :128], strip[:, 128:]
    lane = lanes(c0.shape)
    rows = strip_of(i)
    left_ref[rows, :] = jnp.where(lane == place, pltpu.roll(c0, place, 1), left_ref[rows, :])
    right_ref[rows, :] = jnp.where(
        lane == place, pltpu.roll(c1, lax.rem(place + 1, 128), 1), right_ref[rows, :]
    )


def edges_kernel(u_ref, flags_ref, first_ref, last_ref, left_ref, right_ref, plastic_ref):
    step = pl.program_id(0)

    @pl.when(step == 0)
    def _():
        left_ref[...] = jnp.zeros_like(left_ref)
        right_ref[...] = jnp.zeros_like(right_ref)
        wide = (rows_of((64, 8)) // 8 == lanes((64, 8))).astype(F32)
        high = (rows_of((32, 256)) == lanes((32, 256)) // 8).astype(F32)
        marks = (flags_ref[...] == 1).astype(F32)
        plastic_ref[...] = dot(dot(wide, marks), high)

    for k in range(u_ref.shape[1]):
        z = step * u_ref.shape[1] + k
        for c in range(3):
            place = slot(c, z)
            first_ref[pl.ds(place, 1), :] = u_ref[c, k, 0:1, :]
            last_ref[pl.ds(place, 1), :] = u_ref[c, k, 63:64, :]
            for i in range(8):
                put_columns(left_ref, right_ref, u_ref[c, k, strip_of(i), :], i, place)


def slip_kernel(
    shear_ref, yields_ref, u_ref, v_ref, region_ref, plastic_ref,
    top_ref, bottom_ref, left_ref, right_ref, _after_ref, send_ref,
):
    halo_refs = (top_ref, bottom_ref, left_ref, right_ref)
    for i in range(8):
        rows = strip_of(i)
        centers, sums = stencil_strip(
            i,
            lambda c, r: u_ref[c, 0, r, :],
            None,
            lambda c, r: u_ref[c, 1, r, :],
            None,
            halo_refs,
            0,
        )
        force = strip_force(
            centers, sums, region_ref[0, rows, :], plastic_ref[rows, :], shear_ref, yields_ref
        )
        n, part = i // 2, (i % 2) * 8
        for c in range(3):
            v = v_ref[c, 0, rows, :]
            v = v + DT * (force[c] - DAMPING * v)
            moved = centers[c] + DT * v
            for f, values in enumerate((centers[c], moved)):
                for half in range(2):
                    start = f * 96 + c * 32 + half * 16 + part
                    send_ref[n, start : start + 8, :] = values[:, half * 128 : half * 128 + 128]


def step_one_kernel(
    shear_ref, yields_ref, u_ref, v_ref, region_ref, plastic_ref,
    top_ref, bottom_ref, left_ref, right_ref, _after_ref,
    new_u_ref, new_v_ref, first_ref, last_ref, left_out_ref, right_out_ref,
):
    step = pl.program_id(0)

    @pl.when(step == 0)
    def _():
        left_out_ref[...] = jnp.zeros_like(left_out_ref)
        right_out_ref[...] = jnp.zeros_like(right_out_ref)

    halo_refs = (top_ref, bottom_ref, left_ref, right_ref)
    for k in range(PLANES):
        z = step * PLANES + k
        damping = jnp.where(z == 0, DAMPING, 0.0).astype(F32)
        lower = jnp.where(z > 0, 1.0, 0.0).astype(F32)
        upper = jnp.where(z < 15, 1.0, 0.0).astype(F32)
        if k < PLANES - 1:
            load_above = lambda c, r: u_ref[c, z + 1, r, :]
        else:
            load_above = lambda c, r: u_ref[c, jnp.minimum(z + 1, 15), r, :] * upper
        if k > 0:
            load_below = lambda c, r: u_ref[c, z - 1, r, :]
        else:
            load_below = lambda c, r: u_ref[c, jnp.maximum(z - 1, 0), r, :] * lower
        for i in range(8):
            rows = strip_of(i)
            centers, sums = stencil_strip(
                i, lambda c, r: u_ref[c, z, r, :], None, load_above, load_below, halo_refs, z
            )
            force = strip_force(
                centers, sums, region_ref[k, rows, :], plastic_ref[rows, :], shear_ref, yields_ref
            )
            for c in range(3):
                v = v_ref[c, k, rows, :]
                v = v + DT * (force[c] - damping * v)
                u = centers[c] + DT * v
                new_v_ref[c, k, rows, :] = v
                new_u_ref[c, k, rows, :] = u
                place = slot(c, z)
                if i == 0:
                    first_ref[pl.ds(place, 1), :] = u[0:1]
                if i == 7:
                    last_ref[pl.ds(place, 1), :] = u[7:8]
                put_columns(left_out_ref, right_out_ref, u, i, place)


def step_two_kernel(start, *refs):
    (shear_ref, yields_ref, u_ref, v_ref, region_ref, plastic_ref) = refs[:6]
    halo_refs = refs[6:10]
    new_u_ref, new_v_ref = refs[-2:]
    for k in range(PLANES):
        z = pl.program_id(0) * PLANES + (start + k)
        upper = jnp.where(z < 15, 1.0, 0.0).astype(F32)
        if k < PLANES - 1:
            load_above = lambda c, r: u_ref[c, z + 1, r, :]
        else:
            load_above = lambda c, r: u_ref[c, jnp.minimum(z + 1, 15), r, :] * upper
        for i in range(8):
            rows = strip_of(i)
            centers, sums = stencil_strip(
                i,
                lambda c, r: u_ref[c, z, r, :],
                None,
                load_above,
                lambda c, r: u_ref[c, z - 1, r, :],
                halo_refs,
                z,
            )
            force = strip_force(
                centers, sums, region_ref[k, rows, :], plastic_ref[rows, :], shear_ref, yields_ref
            )
            for c in range(3):
                v = v_ref[c, k, rows, :] + DT * force[c]
                new_v_ref[c, k, rows, :] = v
                new_u_ref[c, k, rows, :] = centers[c] + DT * v


def last_kernel(
    shear_ref, yields_ref, u_ref, v_ref, region_ref, plastic_ref,
    top_ref, bottom_ref, left_ref, right_ref,
    recv_ref, _old_u_ref, _old_v_ref, new_u_ref, new_v_ref, surface,
):
    square = DT * DT
    halo_refs = (top_ref, bottom_ref, left_ref, right_ref)

    def traction(f, c, i):
        start = f * 96 + c * 32 + (i % 2) * 8
        return jnp.concatenate(
            [recv_ref[i // 2, start + half * 16 : start + half * 16 + 8, :] for half in range(2)], 1
        )

    def outside(n, c, side):
        row = 208 + c * 2 + side
        return jnp.concatenate(
            [recv_ref[n, row + half * 8 : row + half * 8 + 1, :] for half in range(2)], 1
        )

    def beside(c, i, before, after, left, right):
        if i == 0:
            before = before + square * outside(0, c, 0)
        if i == 7:
            after = after + square * outside(3, c, 1)
        start = 192 + (i % 2) * 8
        columns = recv_ref[i // 2, start : start + 8, :]
        left = left + square * pltpu.roll(columns, (128 - c) % 128, 1)
        right = right + square * pltpu.roll(columns, 127 - (3 + c), 1)
        return before, after, left, right

    for i in range(8):
        for c in range(3):
            surface[c, strip_of(i), :] = u_ref[c, 0, strip_of(i), :] + square * traction(0, c, i)
    for z in range(2):
        for i in range(8):
            rows = strip_of(i)
            above = lambda c, r: u_ref[c, z + 1, r, :]
            if z == 0:
                load, below = lambda c, r: surface[c, r, :], None
            else:
                load, below = lambda c, r: u_ref[c, 1, r, :], lambda c, r: surface[c, r, :]
            centers, sums = stencil_strip(
                i, load, beside if z == 0 else None, above, below, halo_refs, z
            )
            force = strip_force(
                centers, sums, region_ref[z, rows, :], plastic_ref[rows, :], shear_ref, yields_ref
            )
            for c in range(3):
                v = v_ref[c, z, rows, :]
                if z == 0:
                    v = v + DT * traction(0, c, i)
                    v = v + DT * (force[c] + (traction(1, c, i) - DAMPING * v))
                else:
                    v = v + DT * force[c]
                new_v_ref[c, z, rows, :] = v
                new_u_ref[c, z, rows, :] = centers[c] + DT * v


def history_kernel(where_ref, kernel_ref, history_ref, *refs):
    own_ref, main_ref, edge_ref = refs[-3:]
    low = where_ref[0] == 1
    width = own_ref.shape[1]

    def step(m, carry):
        total, ones = carry
        out, twos = [], []
        for c in range(3):
            two = kernel_ref[m + 2, c].astype(F32)
            twos.append(two)
            for ri in range(2):
                past = history_ref[m, ri, c].astype(F32)
                p1, p2 = total[c * 2 + ri]
                out.append((p1 + ones[c] * past, p2 + two * past))
        return tuple(out), tuple(twos)

    zero = jnp.zeros((8, width), F32)
    total, _ = lax.fori_loop(
        0, 31, step,
        (tuple((zero, zero) for _ in range(6)), tuple(kernel_ref[1, c].astype(F32) for c in range(3))),
    )
    values = [None] * 18
    for c in range(3):
        one = kernel_ref[32, c].astype(F32)
        for ri in range(2):
            p1, p2 = total[c * 2 + ri]
            values[ri * 3 + c] = p1 + one * history_ref[31, ri, c].astype(F32)
            values[6 + ri * 3 + c] = p2
        values[12 + c] = kernel_ref[0, c].astype(F32)
        values[15 + c] = kernel_ref[1, c].astype(F32)
    for i, value in enumerate(values):
        row = [value[r : r + 1] for r in range(8)]
        for r, (a, b) in enumerate(((0, 4), (1, 3), (2, 2), (3, 1))):
            own_ref[i * 4 + r : i * 4 + r + 1, :] = jnp.where(low, row[a], row[b])
        for r, (a, b) in enumerate(((4, 4), (5, 7), (6, 6), (7, 5))):
            main_ref[i * 4 + r : i * 4 + r + 1, :] = jnp.where(low, row[a], row[b])
        edge_ref[i : i + 1, :] = row[0]


def mirror_kernel(where_ref, reverse_ref, own_ref, main_ref, edge_ref, out_ref, tiles, turned):
    low = where_ref[0] == 1
    special = where_ref[1]
    for i in range(18):
        own = own_ref[i * 4 : i * 4 + 4, :]
        main = main_ref[i * 4 : i * 4 + 4, :]
        edge = edge_ref[i : i + 1, :]
        other = jnp.where(rows_of(main.shape) == 0, edge, main)
        tiles[i * 8 : i * 8 + 4, :] = jnp.where(low, own, main)
        tiles[i * 8 + 4 : i * 8 + 8, :] = jnp.where(low, other, own)
    for block in range(16):
        part = slice(block * 128, block * 128 + 128)
        high, rest = halves(tiles[:, part])
        turned[:, part] = dot(high, reverse_ref[...]) + dot(rest, reverse_ref[...])
    lane = lanes((8, 128))
    row = rows_of((8, 128))
    upper = row >= 4
    chosen = (lax.rem(row, 4) + (1 - special)) == 0

    def swap(x):
        return pltpu.roll(x, 4, 0)

    for block in range(16):
        part = slice(block * 128, block * 128 + 128)
        mirror = slice((15 - block) * 128, (15 - block) * 128 + 128)
        first = ((16 - block) % 16) * 128
        first = slice(first, first + 128)

        def load(i):
            rows = slice(i * 8, i * 8 + 8)
            back = jnp.where(lane == 0, turned[rows, first], turned[rows, mirror])
            return tiles[rows, part], back

        for c in range(3):
            for k in range(2):
                t, b = load(12 + k * 3 + c)
                own = 0.5 * (t + b)
                other = swap(own)
                mean = jnp.where(chosen, 0.5 * (own + other), 0.5 * (t + swap(b)))
                diff = jnp.where(chosen, 0.5 * (own - other), 0.0)
                out_ref[k, c, :, part] = jnp.where(upper, swap(mean), mean)
                out_ref[2 + k, c, :, part] = jnp.where(upper, swap(diff), diff)
            pair = []
            for k in range(2):
                tr, br = load(k * 6 + c)
                ti, bi = load(k * 6 + 3 + c)
                hr, hi = 0.5 * (tr + br), 0.5 * (ti - bi)
                sr, si = swap(hr), swap(hi)
                pair.append(
                    (
                        jnp.where(chosen, hr - si, 0.5 * (tr + swap(br))),
                        jnp.where(chosen, hi + sr, 0.5 * (ti - swap(bi))),
                        hr + si,
                        hi - sr,
                    )
                )
            out_ref[4, c, :, part] = jnp.where(upper, swap(pair[1][0]), pair[0][0])
            out_ref[5, c, :, part] = jnp.where(upper, swap(pair[1][1]), pair[0][1])
            out_ref[6, c, :, part] = pair[0][2]
            out_ref[7, c, :, part] = pair[0][3]


def dip_kernel(radix_ref, turn_ref, out_table_ref, recv_ref, _after_ref, send_ref):
    wide = []
    for c in range(3):
        pieces = []
        for n in range(4):
            for f in range(2):
                start = f * 96 + c * 32
                pieces.append(recv_ref[n, start : start + 32, :])
        wide.append(jnp.concatenate(pieces, 0))
    z = left_dot(radix_ref, jnp.concatenate(wide, 1))
    lane = lanes((1, 128))
    for s in range(2):
        tr, ti = turn_ref[0, s], turn_ref[1, s]
        for c in range(3):
            part = slice(c * 128, c * 128 + 128)
            zr = z[s * 128 : s * 128 + 128, part]
            zi = z[256 + s * 128 : 384 + s * 128, part]
            turned = jnp.concatenate([zr * tr - zi * ti, zr * ti + zi * tr], 1)
            high, low = halves(turned)
            table, rest = out_table_ref[0, s], out_table_ref[1, s]
            res = dot(table, high, (1, 1)) + (dot(rest, high, (1, 1)) + dot(table, low, (1, 1)))
            imag = res[64:128]
            if s == 0:
                extra = jnp.where(lax.rem(lane, 4) == 0, res[128:129], 0.0)
                imag = jnp.where(rows_of(imag.shape) == 0, imag + extra, imag)
            send_ref[pl.ds(s * 384 + c * 2, 64, stride=6), :] = res[0:64]
            send_ref[pl.ds(s * 384 + c * 2 + 1, 64, stride=6), :] = imag


def strike_kernel(
    in_ref, turn_ref, mix_ref, reverse_ref, unmix_ref, out_table_ref,
    coef_ref, recv_ref, _after_ref, send_ref, spec, back, total,
):
    tr, ti = turn_ref[0], turn_ref[1]
    real, imag = [], []
    for c in range(3):
        re = recv_ref[pl.ds(c * 2, 128, stride=6), :].T
        im = recv_ref[pl.ds(c * 2 + 1, 128, stride=6), :].T
        y = right_dot(jnp.concatenate([re, im], 1), in_ref)
        yr, yi = y[:, :128], y[:, 128:]
        real.append(yr * tr - yi * ti)
        imag.append(yr * ti + yi * tr)
    stacked = jnp.concatenate([jnp.concatenate(real, 1), jnp.concatenate(imag, 1)], 0)
    spec[...] = left_dot(mix_ref, stacked)
    for c in range(3):
        part = slice(c * 128, c * 128 + 128)
        high, low = halves(spec[:, part])
        back[:, part] = dot(high, reverse_ref[...]) + dot(low, reverse_ref[...])
    lane = lanes((8, 128))
    upper = rows_of((8, 128)) >= 4

    def swap(x):
        return pltpu.roll(x, 4, 0)

    for c in range(3):
        part = slice(c * 128, c * 128 + 128)
        for block in range(16):
            wave = slice(block * 128, block * 128 + 128)
            a0, a1 = coef_ref[0, c, :, wave], coef_ref[1, c, :, wave]
            m0, m1 = coef_ref[2, c, :, wave], coef_ref[3, c, :, wave]
            for ri in range(2):
                rows = slice(ri * 128 + block * 8, ri * 128 + block * 8 + 8)
                first = ri * 128 + ((16 - block) % 16) * 8
                other = ri * 128 + (15 - block) * 8
                s = spec[rows, part]
                r = jnp.where(
                    lane == 0, back[first : first + 8, part], back[other : other + 8, part]
                )
                if ri == 1:
                    r = -r
                t = a0 * s + m0 * r + coef_ref[4 + ri, c, :, wave]
                q = a0 * r + m0 * s + coef_ref[6 + ri, c, :, wave]
                more = (DT * DT) * (a0 * swap(t) + m0 * swap(q)) + a1 * swap(s) + m1 * swap(r)
                total[rows, part] = t + jnp.where(upper, more, 0.0)
    y = left_dot(unmix_ref, total[...])
    owner = rows_of((128, 128))
    wide_lane = lanes((128, 128))
    extra = [jnp.zeros((128, 128), F32)] * 2
    for c in range(3):
        part = slice(c * 128, c * 128 + 128)
        yr, yi = y[:128, part], y[128:, part]
        turned = jnp.concatenate([yr * tr + yi * ti, yi * tr - yr * ti], 1)
        high, low = halves(turned)
        res = dot(out_table_ref[0], high, (1, 1)) + (
            dot(out_table_ref[1], high, (1, 1)) + dot(out_table_ref[0], low, (1, 1))
        )
        for ri in range(2):
            lines = res[ri * 128 : ri * 128 + 128]
            send_ref[pl.ds(c * 2 + ri, 128, stride=8), :] = lines
            for side in range(2):
                group = c * 2 + side
                if side == 0:
                    moved = jnp.where(owner == 0, 0.0, pltpu.roll(lines, 1, 0))
                    moved = pltpu.roll(moved, (group * 8 + 8) % 128, 1)
                else:
                    moved = jnp.where(owner == 127, 0.0, pltpu.roll(lines, 127, 0))
                    moved = pltpu.roll(moved, group * 8, 1) if group else moved
                extra[ri] = jnp.where(wide_lane // 8 == group, moved, extra[ri])
    for ri in range(2):
        send_ref[pl.ds(6 + ri, 128, stride=8), :] = extra[ri]


def undip_kernel(in_ref, turn_ref, unradix_ref, recv_ref, _after_ref, send_ref):
    row = rows_of((128, 128))
    lane = lanes((128, 128))
    alt = jnp.where(lax.rem(lane, 2) == 0, 0.5, -0.5).astype(F32)
    stacks = [[], [], [], []]
    for c in range(4):
        re = recv_ref[pl.ds(c * 2, 128, stride=8), :].T
        im = recv_ref[pl.ds(c * 2 + 1, 128, stride=8), :].T
        h = right_dot(jnp.concatenate([re, im], 1), in_ref)
        for s in range(2):
            hr = h[:, s * 256 : s * 256 + 128]
            hi = h[:, s * 256 + 128 : s * 256 + 256]
            if s == 0:
                fix = alt * im[:, 0:1] - 0.5 * re[:, 0:1]
                hr = hr + jnp.where(lax.rem(row, 4) == 0, fix, 0.0)
            tr, ti = turn_ref[0, s], turn_ref[1, s]
            stacks[s].append(hr * tr + hi * ti)
            stacks[2 + s].append(hi * tr - hr * ti)
    stacked = jnp.concatenate([jnp.concatenate(part, 1) for part in stacks], 0)
    out = left_dot(unradix_ref, stacked)
    for n in range(4):
        for f in range(2):
            for c in range(3):
                start = f * 96 + c * 32
                row0 = (n * 2 + f) * 32
                send_ref[n, start : start + 32, :] = out[row0 : row0 + 32, c * 128 : c * 128 + 128]
    small = lanes((16, 128))

    def plane(n, half, c):
        row0 = n * 64 + half * 16
        return out[row0 : row0 + 16, c * 128 : c * 128 + 128]

    for n in range(4):
        columns = jnp.zeros((16, 128), F32)
        for c in range(3):
            if n > 0:
                moved = pltpu.roll(plane(n - 1, 1, c), c + 1, 1)
                columns = jnp.where(small == c, moved, columns)
            if n < 3:
                moved = pltpu.roll(plane(n + 1, 0, c), 3 + c, 1)
                columns = jnp.where(small == 3 + c, moved, columns)
        send_ref[n, 192:208, :] = columns
        for half in range(2):
            send_ref[n, 208 + half * 8 : 216 + half * 8, :] = plane(n, half, 3)[:8]


def full(shape):
    del shape
    return pl.BlockSpec(memory_space=pltpu.VMEM)


SMEM = pl.BlockSpec(memory_space=pltpu.SMEM)


def in_hbm(x):
    return pltpu.with_memory_space_constraint(x, pltpu.HBM)


def hbm_shape(*shape):
    return pltpu.HBM(shape, F32)


def shape_of(*shape):
    return jax.ShapeDtypeStruct(shape, F32)


def call(body, out_shape, args, smem=0, scratch=(), after=(), name=None, limit=16 << 20):
    outs = out_shape if isinstance(out_shape, (tuple, list)) else [out_shape]
    size = sum(math.prod(x.shape) * 4 for x in list(args) + list(outs))
    out_specs = [full(x.shape) for x in outs]
    return pl.pallas_call(
        body,
        in_specs=[SMEM] * smem
        + [full(x.shape) for x in args[smem:]]
        + [pl.BlockSpec(memory_space=pl.ANY)] * len(after),
        out_specs=out_specs if isinstance(out_shape, (tuple, list)) else out_specs[0],
        out_shape=out_shape,
        scratch_shapes=scratch,
        cost_estimate=pl.CostEstimate(flops=0, bytes_accessed=size, transcendentals=0),
        compiler_params=pltpu.CompilerParams(vmem_limit_bytes=limit),
        name=name,
    )(*args, *after)


def halo(first, last, left, right):
    up = [(i, i + 1) for i in range(31)]
    down = [(i + 1, i) for i in range(31)]
    top = lax.ppermute(last, "wide", up)
    bottom = lax.ppermute(first, "wide", down)
    up = [(i, i + 1) for i in range(3)]
    down = [(i + 1, i) for i in range(3)]
    from_left = lax.ppermute(right, "narrow", up)
    from_right = lax.ppermute(left, "narrow", down)
    return top, bottom, from_left, from_right


def exchange(x, axis):
    return lax.all_to_all(x, axis, split_axis=0, concat_axis=0, tiled=True)


def body(u, v, region, flags, shear, yields, history, kernel):
    device = lax.axis_index(ALL)
    where = jnp.stack([device < 64, device == 0]).astype(jnp.int32)
    edge_shapes = [shape_of(48, 256)] * 2 + [shape_of(64, 128)] * 2
    near = lambda depth: pl.BlockSpec((3, depth, 64, 256), lambda *_: (0, 0, 0, 0))
    slab = lambda depth: pl.BlockSpec((depth, 64, 256), lambda *_: (0, 0, 0))
    planes = lambda depth, start=0: pl.BlockSpec(
        (3, depth, 64, 256), lambda z: (0, z + start // depth, 0, 0)
    )
    slabs = lambda depth, start=0: pl.BlockSpec(
        (depth, 64, 256), lambda z: (z + start // depth, 0, 0)
    )
    halo_specs = [full((48, 256))] * 2 + [full((64, 128))] * 2
    any_spec = pl.BlockSpec(memory_space=pl.ANY)
    t = TABLES
    u, v, region, history, kernel = (in_hbm(x) for x in (u, v, region, history, kernel))

    first, last, left, right, plastic = pl.pallas_call(
        edges_kernel,
        grid=(4,),
        in_specs=[planes(4), full((8, 32))],
        out_specs=[full(s.shape) for s in edge_shapes] + [full((64, 256))],
        out_shape=edge_shapes + [shape_of(64, 256)],
        cost_estimate=pl.CostEstimate(flops=0, bytes_accessed=3300000, transcendentals=0),
        compiler_params=pltpu.CompilerParams(vmem_limit_bytes=16 << 20),
            name="edges",
    )(u, flags)
    halo_one = halo(first, last, left, right)

    width = 256
    steps = 1024 // width

    def sums(part, after):
        shift = part * steps
        given = [] if part == 0 else list(after)
        return pl.pallas_call(
            history_kernel,
            grid=(steps,),
            in_specs=[
                SMEM,
                pl.BlockSpec((33, 3, 8, width), lambda i: (0, 0, 0, i + shift)),
                pl.BlockSpec((32, 2, 3, 8, width), lambda i: (0, 0, 0, 0, i + shift)),
            ]
            + [any_spec] * len(given),
            out_specs=[
                pl.BlockSpec((72, width), lambda i: (0, i + shift)),
                pl.BlockSpec((72, width), lambda i: (0, i + shift)),
                pl.BlockSpec((18, width), lambda i: (0, i + shift)),
            ],
            out_shape=[hbm_shape(72, 2048), hbm_shape(72, 2048), hbm_shape(18, 2048)],
            input_output_aliases={3: 0, 4: 1, 5: 2} if given else {},
            cost_estimate=pl.CostEstimate(flops=0, bytes_accessed=5500000, transcendentals=0),
            compiler_params=pltpu.CompilerParams(vmem_limit_bytes=16 << 20),
            name="history",
        )(where, kernel, history, *given)

    partial = sums(0, None)
    send = pl.pallas_call(
        slip_kernel,
        grid=(1,),
        in_specs=[SMEM, SMEM, near(2), near(1), slab(1), full((64, 256))] + halo_specs + [any_spec],
        out_specs=full((4, 192, 128)),
        out_shape=shape_of(4, 192, 128),
        cost_estimate=pl.CostEstimate(flops=0, bytes_accessed=1500000, transcendentals=0),
        compiler_params=pltpu.CompilerParams(vmem_limit_bytes=16 << 20),
            name="slip",
    )(shear, yields, u, v, region, plastic, *halo_one, partial[2])
    lines = exchange(send, "narrow")
    own, main, edge = sums(1, partial)
    main = lax.ppermute(main, ALL, [(i, 127 - i) for i in range(128)])
    edge = lax.ppermute(edge, ALL, [(64, 0)] + [(i, 128 - i) for i in range(65, 128)])

    send = call(
        dip_kernel, shape_of(768, 128), (t["radix"], t["dip_turn"], t["dip_out"], lines),
        after=[own], name="dip",
    )
    waves = exchange(send.reshape(128, 1, 768), ALL).reshape(768, 128)

    new_u, new_v, first, last, left, right = pl.pallas_call(
        step_one_kernel,
        grid=(16 // PLANES,),
        in_specs=[SMEM, SMEM, near(16), planes(PLANES), slabs(PLANES), full((64, 256))]
        + halo_specs
        + [any_spec],
        out_specs=[planes(PLANES)] * 2 + [full(s.shape) for s in edge_shapes],
        out_shape=[hbm_shape(3, 16, 64, 256)] * 2 + edge_shapes,
        cost_estimate=pl.CostEstimate(flops=0, bytes_accessed=14000000, transcendentals=0),
        compiler_params=pltpu.CompilerParams(vmem_limit_bytes=24 << 20),
            name="step_one",
    )(shear, yields, u, v, region, plastic, *halo_one, send)
    new_u, new_v = in_hbm(new_u), in_hbm(new_v)
    halo_two = halo(first, last, left, right)

    coefficients = call(
        mirror_kernel,
        shape_of(8, 3, 8, 2048),
        (where, t["reverse"], own, main, edge),
        smem=1,
        scratch=[pltpu.VMEM((144, 2048), F32)] * 2,
        name="mirror",
    )
    send = call(
        strike_kernel,
        shape_of(1024, 128),
        (
            t["strike_in"], t["strike_turn"], t["strike_mix"], t["reverse"],
            t["strike_unmix"], t["strike_out"], coefficients, waves,
        ),
        scratch=[pltpu.VMEM((256, 384), F32)] * 3,
        after=[new_u],
        name="strike",
    )
    columns = exchange(send.reshape(128, 8, 128), ALL).reshape(1024, 128)

    def later(start, stop, given, after):
        return pl.pallas_call(
            functools.partial(step_two_kernel, start),
            grid=((stop - start) // PLANES,),
            in_specs=[
                SMEM, SMEM, near(16), planes(PLANES, start), slabs(PLANES, start), full((64, 256)),
            ]
            + halo_specs
            + [any_spec] * (len(given) + 1),
            out_specs=[planes(PLANES, start)] * 2,
            out_shape=[hbm_shape(3, 16, 64, 256)] * 2,
            input_output_aliases={10: 0, 11: 1} if given else {},
            cost_estimate=pl.CostEstimate(
                flops=0, bytes_accessed=(stop - start) * 800000, transcendentals=0
            ),
            compiler_params=pltpu.CompilerParams(vmem_limit_bytes=24 << 20),
            name="step_two",
        )(shear, yields, new_u, new_v, region, plastic, *halo_two, *given, after)

    out = later(2, 10, [], send)
    send = call(
        undip_kernel,
        shape_of(4, 224, 128),
        (t["dip_in"], t["undip_turn"], t["unradix"], columns),
        after=[out[0]],
        name="undip",
    )
    tractions = exchange(send, "narrow")
    out = later(10, 16, out, send)
    return tuple(
        pl.pallas_call(
            last_kernel,
            grid=(1,),
            in_specs=[SMEM, SMEM, near(4), near(2), slab(2), full((64, 256))]
            + halo_specs
            + [full((4, 224, 128))]
            + [any_spec] * 2,
            out_specs=[near(2)] * 2,
            out_shape=[hbm_shape(3, 16, 64, 256)] * 2,
            scratch_shapes=[pltpu.VMEM((3, 64, 256), F32)],
            input_output_aliases={11: 0, 12: 1},
            cost_estimate=pl.CostEstimate(flops=0, bytes_accessed=4000000, transcendentals=0),
            compiler_params=pltpu.CompilerParams(vmem_limit_bytes=16 << 20),
            name="last",
        )(shear, yields, new_u, new_v, region, plastic, *halo_two, tractions, *out)
    )


def solution(mesh):
    tile = P(None, None, "wide", "narrow")
    in_specs = (
        tile,
        tile,
        P(None, "wide", "narrow"),
        P("wide", "narrow"),
        P(),
        P(),
        P(None, None, None, ALL, None),
        P(None, None, ALL, None),
    )
    return jax.shard_map(body, mesh=mesh, in_specs=in_specs, out_specs=(tile, tile), check_vma=False)
```

```python
import functools
import math

import jax
import jax.numpy as jnp
import ml_dtypes
import numpy as np
from jax import lax
from jax.experimental import pallas as pl
from jax.experimental.pallas import tpu as pltpu
from jax.sharding import PartitionSpec as P

DT = 0.1
DAMPING = 0.5
ALL = ("wide", "narrow")
PLANES = 2
F32 = jnp.float32
BF16 = jnp.bfloat16


def split_table(table):
    table = np.asarray(table, np.float64)
    high = table.astype(ml_dtypes.bfloat16)
    low = (table - high.astype(np.float64)).astype(ml_dtypes.bfloat16)
    return np.stack([high, low])


def make_tables():
    factor = 1.0 / math.sqrt(2048 * 1024)
    eye2 = np.eye(2)
    eye4 = np.eye(4)
    eye8 = np.eye(8)
    eye16 = np.eye(16)
    r8 = np.arange(8).reshape(2, 4)
    y1 = np.arange(8).reshape(4, 2)
    theta = 2 * np.pi * r8[:, :, None, None] * y1[None, None] / 8
    radix = np.stack([np.cos(theta), -np.sin(theta)])
    radix = np.einsum("isrnl,xz,fg->isxfrnglz", radix, eye16, eye2).reshape(512, 256)
    unradix = np.stack([np.cos(theta), -np.sin(theta)])
    unradix = np.einsum("isrnl,xz,fg->nglzisxfr", unradix, eye16, eye2).reshape(256, 512)
    y0 = np.arange(128)
    theta = 2 * np.pi * r8[:, :, None] * y0 / 1024
    turn = np.stack([np.cos(theta), -np.sin(theta)])[:, :, None, None]
    dip_turn = np.broadcast_to(turn, (2, 2, 16, 2, 4, 128)).reshape(2, 2, 128, 128) * factor
    alt = (-1.0) ** y0
    place = np.stack([np.arange(64), 63 - np.arange(64)])
    theta = 2 * np.pi * place[:, :, None] * y0 / 128
    cos, sin = np.cos(theta), np.sin(theta)
    dip_out = np.zeros((2, 136, 256))
    dip_out[:, :64] = np.concatenate([cos, sin], -1)
    dip_out[:, 64:128] = np.concatenate([-sin, cos], -1)
    dip_out[0, 128, :128] = alt
    dip_in = np.zeros((2, 128, 2, 2, 128))
    for s in range(2):
        rows = slice(s * 64, s * 64 + 64)
        dip_in[0, rows, s, 0] = cos[s]
        dip_in[0, rows, s, 1] = sin[s]
        dip_in[1, rows, s, 0] = -sin[s]
        dip_in[1, rows, s, 1] = cos[s]
    dip_in = dip_in.reshape(256, 512)
    theta = 2 * np.pi * np.outer(y0, y0) / 128
    cos, sin = np.cos(theta), np.sin(theta)
    strike_in = np.block([[cos, -sin], [sin, cos]])
    strike_out = np.block([[cos, -sin], [sin, cos]])
    a = np.arange(16)
    theta = 2 * np.pi * np.outer(a, y0) / 2048
    turn = np.stack([np.cos(theta), -np.sin(theta)])
    strike_turn = np.broadcast_to(turn[:, :, None], (2, 16, 8, 128)).reshape(2, 128, 128)
    theta = 2 * np.pi * np.outer(a, a) / 16
    cos, sin = np.kron(np.cos(theta), eye8), np.kron(np.sin(theta), eye8)
    strike_mix = np.block([[cos, sin], [-sin, cos]])
    strike_unmix = np.block([[cos, -sin], [sin, cos]]) * factor
    reverse = np.zeros((128, 128))
    reverse[(128 - y0) % 128, y0] = 1.0
    return {
        "radix": split_table(radix),
        "unradix": split_table(unradix),
        "dip_turn": dip_turn.astype(np.float32),
        "undip_turn": (dip_turn / factor * 2.0).astype(np.float32),
        "dip_out": split_table(dip_out),
        "dip_in": split_table(dip_in),
        "strike_in": split_table(strike_in),
        "strike_out": split_table(strike_out),
        "strike_turn": strike_turn.astype(np.float32),
        "strike_mix": split_table(strike_mix),
        "strike_unmix": split_table(strike_unmix),
        "reverse": reverse.astype(ml_dtypes.bfloat16),
    }


TABLES = make_tables()


def halves(x):
    high = x.astype(BF16)
    return high, (x - high.astype(F32)).astype(BF16)


def dot(a, b, contract=(1, 0)):
    return lax.dot_general(
        a, b, (((contract[0],), (contract[1],)), ((), ())), preferred_element_type=F32
    )


def left_dot(table, x, contract=(1, 0)):
    high, low = halves(x)
    return dot(table[0], high, contract) + (
        dot(table[1], high, contract) + dot(table[0], low, contract)
    )


def right_dot(x, table):
    high, low = halves(x)
    return dot(high, table[0]) + (dot(low, table[0]) + dot(high, table[1]))


def lanes(shape):
    return lax.broadcasted_iota(jnp.int32, shape, len(shape) - 1)


def rows_of(shape):
    return lax.broadcasted_iota(jnp.int32, shape, len(shape) - 2)


def neighbour_sum(center, above, below, before, after, left, right):
    rows = rows_of(center.shape)
    north = jnp.where(rows == 0, before, pltpu.roll(center, 1, 0))
    south = jnp.where(rows == 7, after, pltpu.roll(center, 7, 0))
    c0, c1 = center[:, :128], center[:, 128:]
    lane = lanes(c0.shape)
    w0, w1 = pltpu.roll(c0, 1, 1), pltpu.roll(c1, 1, 1)
    e0, e1 = pltpu.roll(c0, 127, 1), pltpu.roll(c1, 127, 1)
    west = jnp.concatenate([jnp.where(lane == 0, left, w0), jnp.where(lane == 0, w0, w1)], 1)
    east = jnp.concatenate([jnp.where(lane == 127, e1, e0), jnp.where(lane == 127, right, e1)], 1)
    total = (north + south) + (west + east)
    for other in (above, below):
        if other is not None:
            total = total + other
    return total


def label_table(shear_ref, yields_ref):
    one = jnp.ones((8, 128), F32)
    ratios = []
    for label in range(4):
        ratio = (one * shear_ref[label]) / (one * yields_ref[label])
        ratios.append(ratio * ratio)
    return [shear_ref[label] for label in range(4)], ratios


def force_scale(laplace, region, plastic, table):
    shears, ratios = table
    repeats = (region.shape[0] // 8, region.shape[1] // 128)
    modulus = jnp.full(region.shape, shears[0], F32)
    ratio = jnp.tile(ratios[0], repeats)
    for label in range(1, 4):
        modulus = jnp.where(region == label, shears[label], modulus)
        ratio = jnp.where(region == label, jnp.tile(ratios[label], repeats), ratio)
    squares = laplace[0] * laplace[0] + laplace[1] * laplace[1] + laplace[2] * laplace[2]
    capped = lax.rsqrt(1.0 + squares * ratio)
    return modulus * jnp.where(plastic > 0.5, capped, 1.0)


def strip_force(centers, sums, region, plastic, table):
    laplace = [total - 6.0 * center for total, center in zip(sums, centers)]
    scale = force_scale(laplace, region, plastic, table)
    return [scale * part for part in laplace]


def strip_of(i):
    return slice(i * 8, i * 8 + 8)


def stencil_strip(i, load, beside, load_above, load_below, halo_refs, z):
    top_ref, bottom_ref, left_ref, right_ref = halo_refs
    centers, sums = [], []
    for c in range(3):
        place = slot(c, z)
        center = load(c, strip_of(i))
        if i == 0:
            before = top_ref[pl.ds(place, 1), :]
        else:
            before = load(c, slice(i * 8 - 1, i * 8))
        if i == 7:
            after = bottom_ref[pl.ds(place, 1), :]
        else:
            after = load(c, slice(i * 8 + 8, i * 8 + 9))
        left = pltpu.roll(left_ref[strip_of(i), :], lax.rem(128 - place, 128), 1)
        right = pltpu.roll(right_ref[strip_of(i), :], 127 - place, 1)
        if beside is not None:
            before, after, left, right = beside(c, i, before, after, left, right)
        above = load_above(c, strip_of(i)) if load_above else None
        below = load_below(c, strip_of(i)) if load_below else None
        sums.append(neighbour_sum(center, above, below, before, after, left, right))
        centers.append(center)
    return centers, sums


def slot(c, z):
    return c * 16 + z


def edges_kernel(
    u_ref, v_ref, region_ref, flags_ref, first_ref, last_ref, left_ref, right_ref, plastic_ref
):
    step = pl.program_id(0)
    depth = u_ref.shape[1]

    @pl.when(step == 0)
    def _():
        left_ref[...] = jnp.zeros_like(left_ref)
        right_ref[...] = jnp.zeros_like(right_ref)
        wide = (rows_of((64, 8)) // 8 == lanes((64, 8))).astype(F32)
        high = (rows_of((32, 256)) == lanes((32, 256)) // 8).astype(F32)
        marks = (flags_ref[...] == 1).astype(F32)
        plastic = dot(dot(wide, marks), high)
        plastic_ref[...] = plastic
        first_ref[160:168, :] = jnp.broadcast_to(plastic[0:1], (8, 256))
        last_ref[160:168, :] = jnp.broadcast_to(plastic[63:64], (8, 256))
        lane = lanes((64, 128))
        left_ref[1] = jnp.where(lane == 64, pltpu.roll(plastic[:, :128], 64, 1), 0.0)
        right_ref[1] = jnp.where(lane == 64, pltpu.roll(plastic[:, 128:], 65, 1), 0.0)

    for k in range(depth):
        z = step * depth + k
        for c in range(3):
            place = slot(c, z)
            first_ref[pl.ds(place, 1), :] = u_ref[c, k, 0:1, :]
            last_ref[pl.ds(place, 1), :] = u_ref[c, k, 63:64, :]
            first_ref[pl.ds(48 + place, 1), :] = u_ref[c, k, 1:2, :]
            last_ref[pl.ds(48 + place, 1), :] = u_ref[c, k, 62:63, :]
            first_ref[pl.ds(96 + place, 1), :] = v_ref[c, k, 0:1, :]
            last_ref[pl.ds(96 + place, 1), :] = v_ref[c, k, 63:64, :]
        first_ref[pl.ds(144 + z, 1), :] = region_ref[k, 0:1, :].astype(F32)
        last_ref[pl.ds(144 + z, 1), :] = region_ref[k, 63:64, :].astype(F32)
    lane = lanes((8, 128))
    for i in range(8):
        rows = strip_of(i)
        total = [left_ref[0, rows, :], left_ref[1, rows, :], right_ref[0, rows, :], right_ref[1, rows, :]]

        def put(index, tile, source, target):
            moved = pltpu.roll(tile, lax.rem(target + (128 - source), 128), 1)
            total[index] = jnp.where(lane == target, moved, total[index])

        for k in range(depth):
            z = step * depth + k
            for c in range(3):
                place = slot(c, z)
                u0, u1 = u_ref[c, k, rows, 0:128], u_ref[c, k, rows, 128:256]
                put(0, u0, 0, place)
                put(0, u0, 1, place + 48)
                put(2, u1, 127, place)
                put(2, u1, 126, place + 48)
                put(1, v_ref[c, k, rows, 0:128], 0, place)
                put(3, v_ref[c, k, rows, 128:256], 127, place)
            put(1, region_ref[k, rows, 0:128].astype(F32), 0, z + 48)
            put(3, region_ref[k, rows, 128:256].astype(F32), 127, z + 48)
        left_ref[0, rows, :] = total[0]
        left_ref[1, rows, :] = total[1]
        right_ref[0, rows, :] = total[2]
        right_ref[1, rows, :] = total[3]


def beside_kernel(
    where_ref, shear_ref, yields_ref, first_ref, last_ref, left_ref, right_ref,
    top_ref, bottom_ref, west_ref, east_ref, lines_ref,
    new_top_ref, new_bottom_ref, new_west_ref, new_east_ref,
):
    narrow = where_ref[3]
    table = label_table(shear_ref, yields_ref)
    low = jnp.where(narrow > 0, lines_ref[jnp.maximum(narrow - 1, 0), 192:240, :], 0.0)
    high = jnp.where(narrow < 3, lines_ref[jnp.minimum(narrow + 1, 3), 192:240, :], 0.0)

    row = rows_of((16, 256))
    lane = lanes((16, 128))
    sides = (
        (top_ref, first_ref, new_top_ref, 0, where_ref[2] > 0),
        (bottom_ref, last_ref, new_bottom_ref, 1, where_ref[2] < 31),
    )
    for halo_ref, own_ref, out_ref, side, inside in sides:
        laplace = []
        for c in range(3):
            part = slice(c * 16, c * 16 + 16)
            center = halo_ref[part, :]
            total = halo_ref[48 + c * 16 : 64 + c * 16, :] + own_ref[part, :]
            total = total + jnp.where(row == 0, 0.0, pltpu.roll(center, 1, 0))
            total = total + jnp.where(row == 15, 0.0, pltpu.roll(center, 15, 0))
            c0, c1 = center[:, :128], center[:, 128:]
            before = pltpu.roll(low[part], 128 - side, 1) if side else low[part]
            after = pltpu.roll(high[part], 127 - side, 1)
            w0, w1 = pltpu.roll(c0, 1, 1), pltpu.roll(c1, 1, 1)
            e0, e1 = pltpu.roll(c0, 127, 1), pltpu.roll(c1, 127, 1)
            west = [jnp.where(lane == 0, before, w0), jnp.where(lane == 0, w0, w1)]
            east = [jnp.where(lane == 127, e1, e0), jnp.where(lane == 127, after, e1)]
            total = total + jnp.concatenate(west, 1) + jnp.concatenate(east, 1)
            laplace.append(total - 6.0 * center)
        plastic = jnp.broadcast_to(halo_ref[160:161, :], (16, 256))
        scale = force_scale(laplace, halo_ref[144:160, :].astype(jnp.int32), plastic, table)
        damping = jnp.where(row == 0, DAMPING, 0.0)
        for c in range(3):
            part = slice(c * 16, c * 16 + 16)
            v = halo_ref[96 + c * 16 : 112 + c * 16, :]
            v = v + DT * (scale * laplace[c] - damping * v)
            out_ref[part, :] = jnp.where(inside, halo_ref[part, :] + DT * v, 0.0)

    row = rows_of((64, 128))
    lane = lanes((64, 128))
    layer = lax.rem(lane, 16)
    used = lane < 48
    sides = (
        (west_ref, left_ref, new_west_ref, low, narrow > 0),
        (east_ref, right_ref, new_east_ref, high, narrow < 3),
    )
    for halo_ref, own_ref, out_ref, corner, inside in sides:
        tile, other = halo_ref[0], halo_ref[1]
        center = jnp.where(used, tile, 0.0)
        corners = jnp.concatenate([corner, jnp.zeros((80, 128), F32)], 0).T
        total = pltpu.roll(tile, 80, 1) + own_ref[0]
        total = total + jnp.where(row == 0, corners[0:1], pltpu.roll(center, 1, 0))
        total = total + jnp.where(row == 63, corners[1:2], pltpu.roll(center, 63, 0))
        total = total + jnp.where(layer == 0, 0.0, pltpu.roll(center, 1, 1))
        total = total + jnp.where(layer == 15, 0.0, pltpu.roll(center, 127, 1))
        laplace = jnp.where(used, total - 6.0 * center, 0.0)
        squares = laplace * laplace
        squares = (
            (squares + pltpu.roll(squares, 16, 1))
            + (pltpu.roll(squares, 32, 1) + pltpu.roll(squares, 96, 1))
            + pltpu.roll(squares, 112, 1)
        )
        region = jnp.where(
            lane < 16,
            pltpu.roll(other, 80, 1),
            jnp.where(lane < 32, pltpu.roll(other, 96, 1), pltpu.roll(other, 112, 1)),
        ).astype(jnp.int32)
        modulus = jnp.full(region.shape, table[0][0], F32)
        ratio = jnp.tile(table[1][0], (8, 1))
        for label in range(1, 4):
            modulus = jnp.where(region == label, table[0][label], modulus)
            ratio = jnp.where(region == label, jnp.tile(table[1][label], (8, 1)), ratio)
        capped = lax.rsqrt(1.0 + squares * ratio)
        scale = modulus * jnp.where(other[:, 64:65] > 0.5, capped, 1.0)
        v = other + DT * (scale * laplace - jnp.where(layer == 0, DAMPING, 0.0) * other)
        out_ref[...] = jnp.where(used & inside, center + DT * v, 0.0)


def slip_kernel(
    shear_ref, yields_ref, u_ref, v_ref, region_ref, plastic_ref,
    top_ref, bottom_ref, left_ref, right_ref, where_ref, _after_ref, send_ref,
):
    halo_refs = (top_ref, bottom_ref, left_ref.at[0], right_ref.at[0])
    table = label_table(shear_ref, yields_ref)
    lane = lanes((48, 128))
    t0, t1 = top_ref[0:48, 0:128], top_ref[0:48, 128:256]
    b0, b1 = bottom_ref[0:48, 0:128], bottom_ref[0:48, 128:256]
    to_lower = jnp.where(lane == 0, t0, pltpu.roll(b0, 1, 1))
    to_upper = jnp.where(lane == 0, pltpu.roll(t1, 1, 1), pltpu.roll(b1, 2, 1))
    for n in range(4):
        send_ref[n, 192:240, :] = jnp.where(where_ref[3] < n, to_upper, to_lower)
    for i in range(8):
        rows = strip_of(i)
        centers, sums = stencil_strip(
            i,
            lambda c, r: u_ref[c, 0, r, :],
            None,
            lambda c, r: u_ref[c, 1, r, :],
            None,
            halo_refs,
            0,
        )
        force = strip_force(
            centers, sums, region_ref[0, rows, :], plastic_ref[rows, :], table
        )
        n, part = i // 2, (i % 2) * 8
        for c in range(3):
            v = v_ref[c, 0, rows, :]
            v = v + DT * (force[c] - DAMPING * v)
            moved = centers[c] + DT * v
            for f, values in enumerate((centers[c], moved)):
                for half in range(2):
                    start = f * 96 + c * 32 + half * 16 + part
                    send_ref[n, start : start + 8, :] = values[:, half * 128 : half * 128 + 128]


def step_one_kernel(
    shear_ref, yields_ref, u_ref, v_ref, region_ref, plastic_ref,
    top_ref, bottom_ref, left_ref, right_ref, _after_ref,
    new_u_ref, new_v_ref,
):
    step = pl.program_id(0)

    halo_refs = (top_ref, bottom_ref, left_ref.at[0], right_ref.at[0])
    table = label_table(shear_ref, yields_ref)
    for k in range(PLANES):
        z = step * PLANES + k
        damping = jnp.where(z == 0, DAMPING, 0.0).astype(F32)
        lower = jnp.where(z > 0, 1.0, 0.0).astype(F32)
        upper = jnp.where(z < 15, 1.0, 0.0).astype(F32)
        if k < PLANES - 1:
            load_above = lambda c, r: u_ref[c, z + 1, r, :]
        else:
            load_above = lambda c, r: u_ref[c, jnp.minimum(z + 1, 15), r, :] * upper
        if k > 0:
            load_below = lambda c, r: u_ref[c, z - 1, r, :]
        else:
            load_below = lambda c, r: u_ref[c, jnp.maximum(z - 1, 0), r, :] * lower
        for i in range(8):
            rows = strip_of(i)
            centers, sums = stencil_strip(
                i, lambda c, r: u_ref[c, z, r, :], None, load_above, load_below, halo_refs, z
            )
            force = strip_force(
                centers, sums, region_ref[k, rows, :], plastic_ref[rows, :], table
            )
            for c in range(3):
                v = v_ref[c, k, rows, :]
                v = v + DT * (force[c] - damping * v)
                u = centers[c] + DT * v
                new_v_ref[c, k, rows, :] = v
                new_u_ref[c, k, rows, :] = u


def step_two_kernel(start, *refs):
    (shear_ref, yields_ref, u_ref, v_ref, region_ref, plastic_ref) = refs[:6]
    halo_refs = refs[6:10]
    table = label_table(shear_ref, yields_ref)
    new_u_ref, new_v_ref = refs[-2:]
    for k in range(PLANES):
        z = pl.program_id(0) * PLANES + (start + k)
        upper = jnp.where(z < 15, 1.0, 0.0).astype(F32)
        if k < PLANES - 1:
            load_above = lambda c, r: u_ref[c, z + 1, r, :]
        else:
            load_above = lambda c, r: u_ref[c, jnp.minimum(z + 1, 15), r, :] * upper
        for i in range(8):
            rows = strip_of(i)
            centers, sums = stencil_strip(
                i,
                lambda c, r: u_ref[c, z, r, :],
                None,
                load_above,
                lambda c, r: u_ref[c, z - 1, r, :],
                halo_refs,
                z,
            )
            force = strip_force(
                centers, sums, region_ref[k, rows, :], plastic_ref[rows, :], table
            )
            for c in range(3):
                v = v_ref[c, k, rows, :] + DT * force[c]
                new_v_ref[c, k, rows, :] = v
                new_u_ref[c, k, rows, :] = centers[c] + DT * v


def last_kernel(
    shear_ref, yields_ref, u_ref, v_ref, region_ref, plastic_ref,
    top_ref, bottom_ref, left_ref, right_ref,
    recv_ref, _old_u_ref, _old_v_ref, new_u_ref, new_v_ref, surface,
):
    square = DT * DT
    table = label_table(shear_ref, yields_ref)
    halo_refs = (top_ref, bottom_ref, left_ref, right_ref)

    def traction(f, c, i):
        start = f * 96 + c * 32 + (i % 2) * 8
        return jnp.concatenate(
            [recv_ref[i // 2, start + half * 16 : start + half * 16 + 8, :] for half in range(2)], 1
        )

    def outside(n, c, side):
        row = 208 + c * 2 + side
        return jnp.concatenate(
            [recv_ref[n, row + half * 8 : row + half * 8 + 1, :] for half in range(2)], 1
        )

    def beside(c, i, before, after, left, right):
        if i == 0:
            before = before + square * outside(0, c, 0)
        if i == 7:
            after = after + square * outside(3, c, 1)
        start = 192 + (i % 2) * 8
        columns = recv_ref[i // 2, start : start + 8, :]
        left = left + square * pltpu.roll(columns, (128 - c) % 128, 1)
        right = right + square * pltpu.roll(columns, 127 - (3 + c), 1)
        return before, after, left, right

    for i in range(8):
        for c in range(3):
            surface[c, strip_of(i), :] = u_ref[c, 0, strip_of(i), :] + square * traction(0, c, i)
    for z in range(2):
        for i in range(8):
            rows = strip_of(i)
            above = lambda c, r: u_ref[c, z + 1, r, :]
            if z == 0:
                load, below = lambda c, r: surface[c, r, :], None
            else:
                load, below = lambda c, r: u_ref[c, 1, r, :], lambda c, r: surface[c, r, :]
            centers, sums = stencil_strip(
                i, load, beside if z == 0 else None, above, below, halo_refs, z
            )
            force = strip_force(
                centers, sums, region_ref[z, rows, :], plastic_ref[rows, :], table
            )
            for c in range(3):
                v = v_ref[c, z, rows, :]
                if z == 0:
                    v = v + DT * traction(0, c, i)
                    v = v + DT * (force[c] + (traction(1, c, i) - DAMPING * v))
                else:
                    v = v + DT * force[c]
                new_v_ref[c, z, rows, :] = v
                new_u_ref[c, z, rows, :] = centers[c] + DT * v


def history_kernel(where_ref, kernel_ref, history_ref, *refs):
    own_ref, main_ref, edge_ref = refs[-3:]
    low = where_ref[0] == 1
    width = own_ref.shape[1]

    def step(m, carry):
        total, ones = carry
        out, twos = [], []
        for c in range(3):
            two = kernel_ref[m + 2, c].astype(F32)
            twos.append(two)
            for ri in range(2):
                past = history_ref[m, ri, c].astype(F32)
                p1, p2 = total[c * 2 + ri]
                out.append((p1 + ones[c] * past, p2 + two * past))
        return tuple(out), tuple(twos)

    zero = jnp.zeros((8, width), F32)
    total, _ = lax.fori_loop(
        0, 31, step,
        (tuple((zero, zero) for _ in range(6)), tuple(kernel_ref[1, c].astype(F32) for c in range(3))),
    )
    values = [None] * 18
    for c in range(3):
        one = kernel_ref[32, c].astype(F32)
        for ri in range(2):
            p1, p2 = total[c * 2 + ri]
            values[ri * 3 + c] = p1 + one * history_ref[31, ri, c].astype(F32)
            values[6 + ri * 3 + c] = p2
        values[12 + c] = kernel_ref[0, c].astype(F32)
        values[15 + c] = kernel_ref[1, c].astype(F32)
    for i, value in enumerate(values):
        row = [value[r : r + 1] for r in range(8)]
        for r, (a, b) in enumerate(((0, 4), (1, 3), (2, 2), (3, 1))):
            own_ref[i * 4 + r : i * 4 + r + 1, :] = jnp.where(low, row[a], row[b])
        for r, (a, b) in enumerate(((4, 4), (5, 7), (6, 6), (7, 5))):
            main_ref[i * 4 + r : i * 4 + r + 1, :] = jnp.where(low, row[a], row[b])
        edge_ref[i : i + 1, :] = row[0]


def mirror_kernel(where_ref, reverse_ref, own_ref, main_ref, edge_ref, out_ref, tiles, turned):
    low = where_ref[0] == 1
    special = where_ref[1]
    for i in range(18):
        own = own_ref[i * 4 : i * 4 + 4, :]
        main = main_ref[i * 4 : i * 4 + 4, :]
        edge = edge_ref[i : i + 1, :]
        other = jnp.where(rows_of(main.shape) == 0, edge, main)
        tiles[i * 8 : i * 8 + 4, :] = jnp.where(low, own, main)
        tiles[i * 8 + 4 : i * 8 + 8, :] = jnp.where(low, other, own)
    for block in range(16):
        part = slice(block * 128, block * 128 + 128)
        high, rest = halves(tiles[:, part])
        turned[:, part] = dot(high, reverse_ref[...]) + dot(rest, reverse_ref[...])
    lane = lanes((8, 128))
    row = rows_of((8, 128))
    upper = row >= 4
    chosen = (lax.rem(row, 4) + (1 - special)) == 0

    def swap(x):
        return pltpu.roll(x, 4, 0)

    for block in range(16):
        part = slice(block * 128, block * 128 + 128)
        mirror = slice((15 - block) * 128, (15 - block) * 128 + 128)
        first = ((16 - block) % 16) * 128
        first = slice(first, first + 128)

        def load(i):
            rows = slice(i * 8, i * 8 + 8)
            back = jnp.where(lane == 0, turned[rows, first], turned[rows, mirror])
            return tiles[rows, part], back

        for c in range(3):
            for k in range(2):
                t, b = load(12 + k * 3 + c)
                own = 0.5 * (t + b)
                other = swap(own)
                mean = jnp.where(chosen, 0.5 * (own + other), 0.5 * (t + swap(b)))
                diff = jnp.where(chosen, 0.5 * (own - other), 0.0)
                out_ref[k, c, :, part] = jnp.where(upper, swap(mean), mean)
                out_ref[2 + k, c, :, part] = jnp.where(upper, swap(diff), diff)
            pair = []
            for k in range(2):
                tr, br = load(k * 6 + c)
                ti, bi = load(k * 6 + 3 + c)
                hr, hi = 0.5 * (tr + br), 0.5 * (ti - bi)
                sr, si = swap(hr), swap(hi)
                pair.append(
                    (
                        jnp.where(chosen, hr - si, 0.5 * (tr + swap(br))),
                        jnp.where(chosen, hi + sr, 0.5 * (ti - swap(bi))),
                        hr + si,
                        hi - sr,
                    )
                )
            out_ref[4, c, :, part] = jnp.where(upper, swap(pair[1][0]), pair[0][0])
            out_ref[5, c, :, part] = jnp.where(upper, swap(pair[1][1]), pair[0][1])
            out_ref[6, c, :, part] = pair[0][2]
            out_ref[7, c, :, part] = pair[0][3]


def dip_kernel(radix_ref, turn_ref, out_table_ref, recv_ref, _after_ref, send_ref):
    wide = []
    for c in range(3):
        pieces = []
        for n in range(4):
            for f in range(2):
                start = f * 96 + c * 32
                pieces.append(recv_ref[n, start : start + 32, :])
        wide.append(jnp.concatenate(pieces, 0))
    z = left_dot(radix_ref, jnp.concatenate(wide, 1))
    lane = lanes((1, 128))
    for s in range(2):
        tr, ti = turn_ref[0, s], turn_ref[1, s]
        for c in range(3):
            part = slice(c * 128, c * 128 + 128)
            zr = z[s * 128 : s * 128 + 128, part]
            zi = z[256 + s * 128 : 384 + s * 128, part]
            turned = jnp.concatenate([zr * tr - zi * ti, zr * ti + zi * tr], 1)
            high, low = halves(turned)
            table, rest = out_table_ref[0, s], out_table_ref[1, s]
            res = dot(table, high, (1, 1)) + (dot(rest, high, (1, 1)) + dot(table, low, (1, 1)))
            imag = res[64:128]
            if s == 0:
                extra = jnp.where(lax.rem(lane, 4) == 0, res[128:129], 0.0)
                imag = jnp.where(rows_of(imag.shape) == 0, imag + extra, imag)
            send_ref[pl.ds(s * 384 + c * 2, 64, stride=6), :] = res[0:64]
            send_ref[pl.ds(s * 384 + c * 2 + 1, 64, stride=6), :] = imag


def strike_kernel(
    in_ref, turn_ref, mix_ref, reverse_ref, unmix_ref, out_table_ref,
    coef_ref, recv_ref, _after_ref, send_ref, spec, back, total,
):
    tr, ti = turn_ref[0], turn_ref[1]
    real, imag = [], []
    for c in range(3):
        re = recv_ref[pl.ds(c * 2, 128, stride=6), :].T
        im = recv_ref[pl.ds(c * 2 + 1, 128, stride=6), :].T
        y = right_dot(jnp.concatenate([re, im], 1), in_ref)
        yr, yi = y[:, :128], y[:, 128:]
        real.append(yr * tr - yi * ti)
        imag.append(yr * ti + yi * tr)
    stacked = jnp.concatenate([jnp.concatenate(real, 1), jnp.concatenate(imag, 1)], 0)
    spec[...] = left_dot(mix_ref, stacked)
    for c in range(3):
        part = slice(c * 128, c * 128 + 128)
        high, low = halves(spec[:, part])
        back[:, part] = dot(high, reverse_ref[...]) + dot(low, reverse_ref[...])
    lane = lanes((8, 128))
    upper = rows_of((8, 128)) >= 4

    def swap(x):
        return pltpu.roll(x, 4, 0)

    for c in range(3):
        part = slice(c * 128, c * 128 + 128)
        for block in range(16):
            wave = slice(block * 128, block * 128 + 128)
            a0, a1 = coef_ref[0, c, :, wave], coef_ref[1, c, :, wave]
            m0, m1 = coef_ref[2, c, :, wave], coef_ref[3, c, :, wave]
            for ri in range(2):
                rows = slice(ri * 128 + block * 8, ri * 128 + block * 8 + 8)
                first = ri * 128 + ((16 - block) % 16) * 8
                other = ri * 128 + (15 - block) * 8
                s = spec[rows, part]
                r = jnp.where(
                    lane == 0, back[first : first + 8, part], back[other : other + 8, part]
                )
                if ri == 1:
                    r = -r
                t = a0 * s + m0 * r + coef_ref[4 + ri, c, :, wave]
                q = a0 * r + m0 * s + coef_ref[6 + ri, c, :, wave]
                more = (DT * DT) * (a0 * swap(t) + m0 * swap(q)) + a1 * swap(s) + m1 * swap(r)
                total[rows, part] = t + jnp.where(upper, more, 0.0)
    y = left_dot(unmix_ref, total[...])
    owner = rows_of((128, 128))
    wide_lane = lanes((128, 128))
    extra = [jnp.zeros((128, 128), F32)] * 2
    for c in range(3):
        part = slice(c * 128, c * 128 + 128)
        yr, yi = y[:128, part], y[128:, part]
        turned = jnp.concatenate([yr * tr + yi * ti, yi * tr - yr * ti], 1)
        high, low = halves(turned)
        res = dot(out_table_ref[0], high, (1, 1)) + (
            dot(out_table_ref[1], high, (1, 1)) + dot(out_table_ref[0], low, (1, 1))
        )
        for ri in range(2):
            lines = res[ri * 128 : ri * 128 + 128]
            send_ref[pl.ds(c * 2 + ri, 128, stride=8), :] = lines
            for side in range(2):
                group = c * 2 + side
                if side == 0:
                    moved = jnp.where(owner == 0, 0.0, pltpu.roll(lines, 1, 0))
                    moved = pltpu.roll(moved, (group * 8 + 8) % 128, 1)
                else:
                    moved = jnp.where(owner == 127, 0.0, pltpu.roll(lines, 127, 0))
                    moved = pltpu.roll(moved, group * 8, 1) if group else moved
                extra[ri] = jnp.where(wide_lane // 8 == group, moved, extra[ri])
    for ri in range(2):
        send_ref[pl.ds(6 + ri, 128, stride=8), :] = extra[ri]


def undip_kernel(in_ref, turn_ref, unradix_ref, recv_ref, _after_ref, send_ref):
    row = rows_of((128, 128))
    lane = lanes((128, 128))
    alt = jnp.where(lax.rem(lane, 2) == 0, 0.5, -0.5).astype(F32)
    stacks = [[], [], [], []]
    for c in range(4):
        re = recv_ref[pl.ds(c * 2, 128, stride=8), :].T
        im = recv_ref[pl.ds(c * 2 + 1, 128, stride=8), :].T
        h = right_dot(jnp.concatenate([re, im], 1), in_ref)
        for s in range(2):
            hr = h[:, s * 256 : s * 256 + 128]
            hi = h[:, s * 256 + 128 : s * 256 + 256]
            if s == 0:
                fix = alt * im[:, 0:1] - 0.5 * re[:, 0:1]
                hr = hr + jnp.where(lax.rem(row, 4) == 0, fix, 0.0)
            tr, ti = turn_ref[0, s], turn_ref[1, s]
            stacks[s].append(hr * tr + hi * ti)
            stacks[2 + s].append(hi * tr - hr * ti)
    stacked = jnp.concatenate([jnp.concatenate(part, 1) for part in stacks], 0)
    out = left_dot(unradix_ref, stacked)
    for n in range(4):
        for f in range(2):
            for c in range(3):
                start = f * 96 + c * 32
                row0 = (n * 2 + f) * 32
                send_ref[n, start : start + 32, :] = out[row0 : row0 + 32, c * 128 : c * 128 + 128]
    small = lanes((16, 128))

    def plane(n, half, c):
        row0 = n * 64 + half * 16
        return out[row0 : row0 + 16, c * 128 : c * 128 + 128]

    for n in range(4):
        columns = jnp.zeros((16, 128), F32)
        for c in range(3):
            if n > 0:
                moved = pltpu.roll(plane(n - 1, 1, c), c + 1, 1)
                columns = jnp.where(small == c, moved, columns)
            if n < 3:
                moved = pltpu.roll(plane(n + 1, 0, c), 3 + c, 1)
                columns = jnp.where(small == 3 + c, moved, columns)
        send_ref[n, 192:208, :] = columns
        for half in range(2):
            send_ref[n, 208 + half * 8 : 216 + half * 8, :] = plane(n, half, 3)[:8]


def full(shape):
    del shape
    return pl.BlockSpec(memory_space=pltpu.VMEM)


SMEM = pl.BlockSpec(memory_space=pltpu.SMEM)


def in_hbm(x):
    return pltpu.with_memory_space_constraint(x, pltpu.HBM)


def hbm_shape(*shape):
    return pltpu.HBM(shape, F32)


def shape_of(*shape):
    return jax.ShapeDtypeStruct(shape, F32)


def call(body, out_shape, args, smem=0, scratch=(), after=(), name=None, limit=16 << 20):
    outs = out_shape if isinstance(out_shape, (tuple, list)) else [out_shape]
    size = sum(math.prod(x.shape) * 4 for x in list(args) + list(outs))
    out_specs = [full(x.shape) for x in outs]
    return pl.pallas_call(
        body,
        in_specs=[SMEM] * smem
        + [full(x.shape) for x in args[smem:]]
        + [pl.BlockSpec(memory_space=pl.ANY)] * len(after),
        out_specs=out_specs if isinstance(out_shape, (tuple, list)) else out_specs[0],
        out_shape=out_shape,
        scratch_shapes=scratch,
        cost_estimate=pl.CostEstimate(flops=0, bytes_accessed=size, transcendentals=0),
        compiler_params=pltpu.CompilerParams(vmem_limit_bytes=limit),
        name=name,
    )(*args, *(in_hbm(x) for x in after))


def halo(first, last, left, right):
    up = [(i, i + 1) for i in range(31)]
    down = [(i + 1, i) for i in range(31)]
    top = lax.ppermute(last, "wide", up)
    bottom = lax.ppermute(first, "wide", down)
    up = [(i, i + 1) for i in range(3)]
    down = [(i + 1, i) for i in range(3)]
    from_left = lax.ppermute(right, "narrow", up)
    from_right = lax.ppermute(left, "narrow", down)
    return top, bottom, from_left, from_right


def exchange(x, axis):
    return lax.all_to_all(x, axis, split_axis=0, concat_axis=0, tiled=True)


def body(u, v, region, flags, shear, yields, history, kernel):
    device = lax.axis_index(ALL)
    where = jnp.stack(
        [
            (device < 64).astype(jnp.int32),
            (device == 0).astype(jnp.int32),
            lax.axis_index("wide"),
            lax.axis_index("narrow"),
        ]
    )
    edge_shapes = [shape_of(168, 256)] * 2 + [shape_of(2, 64, 128)] * 2
    halo_shapes = [shape_of(48, 256)] * 2 + [shape_of(64, 128)] * 2
    near = lambda depth: pl.BlockSpec((3, depth, 64, 256), lambda *_: (0, 0, 0, 0))
    slab = lambda depth: pl.BlockSpec((depth, 64, 256), lambda *_: (0, 0, 0))
    planes = lambda depth, start=0: pl.BlockSpec(
        (3, depth, 64, 256), lambda z: (0, z + start // depth, 0, 0)
    )
    slabs = lambda depth, start=0: pl.BlockSpec(
        (depth, 64, 256), lambda z: (z + start // depth, 0, 0)
    )
    halo_specs = [full((48, 256))] * 2 + [full((64, 128))] * 2
    any_spec = pl.BlockSpec(memory_space=pl.ANY)
    t = TABLES
    u, v, region, history, kernel = (in_hbm(x) for x in (u, v, region, history, kernel))
    shear, yields, where = in_hbm(shear), in_hbm(yields), in_hbm(where)

    first, last, left, right, plastic = pl.pallas_call(
        edges_kernel,
        grid=(4,),
        in_specs=[planes(4), planes(4), slabs(4), full((8, 32))],
        out_specs=[full(s.shape) for s in edge_shapes] + [full((64, 256))],
        out_shape=edge_shapes + [shape_of(64, 256)],
        cost_estimate=pl.CostEstimate(flops=0, bytes_accessed=8000000, transcendentals=0),
        compiler_params=pltpu.CompilerParams(vmem_limit_bytes=16 << 20),
            name="edges",
    )(u, v, region, flags)
    halo_one = halo(first, last, left, right)
    plastic = in_hbm(plastic)

    width = 256
    steps = 1024 // width

    def sums(part, after):
        shift = part * steps
        given = [] if part == 0 else list(after)
        return pl.pallas_call(
            history_kernel,
            grid=(steps,),
            in_specs=[
                SMEM,
                pl.BlockSpec((33, 3, 8, width), lambda i: (0, 0, 0, i + shift)),
                pl.BlockSpec((32, 2, 3, 8, width), lambda i: (0, 0, 0, 0, i + shift)),
            ]
            + [any_spec] * len(given),
            out_specs=[
                pl.BlockSpec((72, width), lambda i: (0, i + shift)),
                pl.BlockSpec((72, width), lambda i: (0, i + shift)),
                pl.BlockSpec((18, width), lambda i: (0, i + shift)),
            ],
            out_shape=[hbm_shape(72, 2048), hbm_shape(72, 2048), hbm_shape(18, 2048)],
            input_output_aliases={3: 0, 4: 1, 5: 2} if given else {},
            cost_estimate=pl.CostEstimate(flops=0, bytes_accessed=5500000, transcendentals=0),
            compiler_params=pltpu.CompilerParams(vmem_limit_bytes=16 << 20),
            name="history",
        )(where, kernel, history, *(in_hbm(x) for x in given))

    partial = sums(0, None)
    send = pl.pallas_call(
        slip_kernel,
        grid=(1,),
        in_specs=[SMEM, SMEM, near(2), near(1), slab(1), full((64, 256))]
        + halo_specs
        + [SMEM, any_spec],
        out_specs=full((4, 240, 128)),
        out_shape=shape_of(4, 240, 128),
        cost_estimate=pl.CostEstimate(flops=0, bytes_accessed=1500000, transcendentals=0),
        compiler_params=pltpu.CompilerParams(vmem_limit_bytes=16 << 20),
            name="slip",
    )(shear, yields, u, v, region, plastic, *halo_one, where, in_hbm(partial[2]))
    lines = exchange(send, "narrow")
    own, main, edge = sums(1, partial)
    main = lax.ppermute(main, ALL, [(i, 127 - i) for i in range(128)])
    edge = lax.ppermute(edge, ALL, [(64, 0)] + [(i, 128 - i) for i in range(65, 128)])

    send = call(
        dip_kernel, shape_of(768, 128), (t["radix"], t["dip_turn"], t["dip_out"], lines),
        after=[own], name="dip",
    )
    waves = exchange(send.reshape(128, 1, 768), ALL).reshape(768, 128)

    new_u, new_v = pl.pallas_call(
        step_one_kernel,
        grid=(16 // PLANES,),
        in_specs=[SMEM, SMEM, near(16), planes(PLANES), slabs(PLANES), full((64, 256))]
        + halo_specs
        + [any_spec],
        out_specs=[planes(PLANES)] * 2,
        out_shape=[hbm_shape(3, 16, 64, 256)] * 2,
        cost_estimate=pl.CostEstimate(flops=0, bytes_accessed=14000000, transcendentals=0),
        compiler_params=pltpu.CompilerParams(vmem_limit_bytes=24 << 20),
            name="step_one",
    )(shear, yields, u, v, region, plastic, *halo_one, in_hbm(send))
    new_u, new_v = in_hbm(new_u), in_hbm(new_v)
    halo_two = call(
        beside_kernel,
        halo_shapes,
        (where, shear, yields, *(in_hbm(x) for x in (first, last, left, right, *halo_one, lines))),
        smem=3,
        name="beside",
    )

    coefficients = call(
        mirror_kernel,
        shape_of(8, 3, 8, 2048),
        (where, t["reverse"], *(in_hbm(x) for x in (own, main, edge))),
        smem=1,
        scratch=[pltpu.VMEM((144, 2048), F32)] * 2,
        name="mirror",
    )
    send = call(
        strike_kernel,
        shape_of(1024, 128),
        (
            t["strike_in"], t["strike_turn"], t["strike_mix"], t["reverse"],
            t["strike_unmix"], t["strike_out"], coefficients, waves,
        ),
        scratch=[pltpu.VMEM((256, 384), F32)] * 3,
        after=[new_u],
        name="strike",
    )
    columns = exchange(send.reshape(128, 8, 128), ALL).reshape(1024, 128)

    def later(start, stop, given, after):
        return pl.pallas_call(
            functools.partial(step_two_kernel, start),
            grid=((stop - start) // PLANES,),
            in_specs=[
                SMEM, SMEM, near(16), planes(PLANES, start), slabs(PLANES, start), full((64, 256)),
            ]
            + halo_specs
            + [any_spec] * (len(given) + 1),
            out_specs=[planes(PLANES, start)] * 2,
            out_shape=[hbm_shape(3, 16, 64, 256)] * 2,
            input_output_aliases={10: 0, 11: 1} if given else {},
            cost_estimate=pl.CostEstimate(
                flops=0, bytes_accessed=(stop - start) * 800000, transcendentals=0
            ),
            compiler_params=pltpu.CompilerParams(vmem_limit_bytes=24 << 20),
            name="step_two",
        )(shear, yields, new_u, new_v, region, plastic, *halo_two, *given, in_hbm(after))

    out = later(2, 10, [], send)
    send = call(
        undip_kernel,
        shape_of(4, 224, 128),
        (t["dip_in"], t["undip_turn"], t["unradix"], columns),
        after=[out[0]],
        name="undip",
    )
    tractions = exchange(send, "narrow")
    out = later(10, 16, out, send)
    return tuple(
        pl.pallas_call(
            last_kernel,
            grid=(1,),
            in_specs=[SMEM, SMEM, near(4), near(2), slab(2), full((64, 256))]
            + halo_specs
            + [full((4, 224, 128))]
            + [any_spec] * 2,
            out_specs=[near(2)] * 2,
            out_shape=[hbm_shape(3, 16, 64, 256)] * 2,
            scratch_shapes=[pltpu.VMEM((3, 64, 256), F32)],
            input_output_aliases={11: 0, 12: 1},
            cost_estimate=pl.CostEstimate(flops=0, bytes_accessed=4000000, transcendentals=0),
            compiler_params=pltpu.CompilerParams(vmem_limit_bytes=16 << 20),
            name="last",
        )(shear, yields, new_u, new_v, region, plastic, *halo_two, tractions, *out)
    )


def solution(mesh):
    tile = P(None, None, "wide", "narrow")
    in_specs = (
        tile,
        tile,
        P(None, "wide", "narrow"),
        P("wide", "narrow"),
        P(),
        P(),
        P(None, None, None, ALL, None),
        P(None, None, ALL, None),
    )
    return jax.shard_map(body, mesh=mesh, in_specs=in_specs, out_specs=(tile, tile), check_vma=False)
```

```python
import functools
import math

import jax
import jax.numpy as jnp
import ml_dtypes
import numpy as np
from jax import lax
from jax.experimental import pallas as pl
from jax.experimental.pallas import tpu as pltpu
from jax.sharding import PartitionSpec as P

DT = 0.1
DAMPING = 0.5
ALL = ("wide", "narrow")
PLANES = 2
UNROLL = 6
F32 = jnp.float32
BF16 = jnp.bfloat16


def split_table(table):
    table = np.asarray(table, np.float64)
    high = table.astype(ml_dtypes.bfloat16)
    low = (table - high.astype(np.float64)).astype(ml_dtypes.bfloat16)
    return np.stack([high, low])


def make_tables():
    factor = 1.0 / math.sqrt(2048 * 1024)
    eye2 = np.eye(2)
    eye4 = np.eye(4)
    eye8 = np.eye(8)
    eye16 = np.eye(16)
    r8 = np.arange(8).reshape(2, 4)
    y1 = np.arange(8).reshape(4, 2)
    theta = 2 * np.pi * r8[:, :, None, None] * y1[None, None] / 8
    radix = np.stack([np.cos(theta), -np.sin(theta)])
    radix = np.einsum("isrnl,xz,fg->isxfrnglz", radix, eye16, eye2).reshape(512, 256)
    unradix = np.stack([np.cos(theta), -np.sin(theta)])
    unradix = np.einsum("isrnl,xz,fg->nglzisxfr", unradix, eye16, eye2).reshape(256, 512)
    y0 = np.arange(128)
    theta = 2 * np.pi * r8[:, :, None] * y0 / 1024
    turn = np.stack([np.cos(theta), -np.sin(theta)])[:, :, None]
    dip_turn = np.broadcast_to(turn, (2, 2, 2, 4, 128)).reshape(2, 2, 8, 128) * factor
    alt = (-1.0) ** y0
    place = np.stack([np.arange(64), 63 - np.arange(64)])
    theta = 2 * np.pi * place[:, :, None] * y0 / 128
    cos, sin = np.cos(theta), np.sin(theta)
    dip_out = np.zeros((2, 136, 256))
    dip_out[:, :64] = np.concatenate([cos, sin], -1)
    dip_out[:, 64:128] = np.concatenate([-sin, cos], -1)
    dip_out[0, 128, :128] = alt
    dip_in = np.zeros((2, 128, 2, 2, 128))
    for s in range(2):
        rows = slice(s * 64, s * 64 + 64)
        dip_in[0, rows, s, 0] = cos[s]
        dip_in[0, rows, s, 1] = sin[s]
        dip_in[1, rows, s, 0] = -sin[s]
        dip_in[1, rows, s, 1] = cos[s]
    dip_in = dip_in.reshape(256, 512)
    theta = 2 * np.pi * np.outer(y0, y0) / 128
    cos, sin = np.cos(theta), np.sin(theta)
    strike_in = np.block([[cos, -sin], [sin, cos]])
    strike_out = np.block([[cos, -sin], [sin, cos]])
    a = np.arange(16)
    theta = 2 * np.pi * np.outer(a, y0) / 2048
    turn = np.stack([np.cos(theta), -np.sin(theta)])
    strike_turn = np.broadcast_to(turn[:, :, None], (2, 16, 8, 128)).reshape(2, 128, 128)
    theta = 2 * np.pi * np.outer(a, a) / 16
    cos, sin = np.kron(np.cos(theta), eye8), np.kron(np.sin(theta), eye8)
    strike_mix = np.block([[cos, sin], [-sin, cos]])
    reverse = np.zeros((128, 128))
    reverse[(128 - y0) % 128, y0] = 1.0
    return {
        "radix": split_table(radix),
        "unradix": split_table(unradix),
        "dip_turn": dip_turn.astype(np.float32),
        "undip_turn": (dip_turn * 2.0).astype(np.float32),
        "dip_out": split_table(dip_out),
        "dip_in": split_table(dip_in),
        "strike_in": split_table(strike_in),
        "strike_out": split_table(strike_out),
        "strike_turn": strike_turn.astype(np.float32),
        "strike_mix": split_table(strike_mix),
        "reverse": reverse.astype(ml_dtypes.bfloat16),
    }


TABLES = make_tables()


def halves(x):
    high = x.astype(BF16)
    return high, (x - high.astype(F32)).astype(BF16)


def dot(a, b, contract=(1, 0)):
    return lax.dot_general(
        a, b, (((contract[0],), (contract[1],)), ((), ())), preferred_element_type=F32
    )


def left_dot(table, x, contract=(1, 0)):
    high, low = halves(x)
    return dot(table[0], high, contract) + (
        dot(table[1], high, contract) + dot(table[0], low, contract)
    )


def right_dot(x, table):
    high, low = halves(x)
    return dot(high, table[0]) + (dot(low, table[0]) + dot(high, table[1]))


def lanes(shape):
    return lax.broadcasted_iota(jnp.int32, shape, len(shape) - 1)


def rows_of(shape):
    return lax.broadcasted_iota(jnp.int32, shape, len(shape) - 2)


def neighbour_sum(center, above, below, before, after, left, right):
    rows = rows_of(center.shape)
    north = jnp.where(rows == 0, before, pltpu.roll(center, 1, 0))
    south = jnp.where(rows == 7, after, pltpu.roll(center, 7, 0))
    c0, c1 = center[:, :128], center[:, 128:]
    lane = lanes(c0.shape)
    w0, w1 = pltpu.roll(c0, 1, 1), pltpu.roll(c1, 1, 1)
    e0, e1 = pltpu.roll(c0, 127, 1), pltpu.roll(c1, 127, 1)
    west = jnp.concatenate([jnp.where(lane == 0, left, w0), jnp.where(lane == 0, w0, w1)], 1)
    east = jnp.concatenate([jnp.where(lane == 127, e1, e0), jnp.where(lane == 127, right, e1)], 1)
    total = (north + south) + (west + east)
    for other in (above, below):
        if other is not None:
            total = total + other
    return total


def label_table(shear_ref, yields_ref):
    one = jnp.ones((8, 128), F32)
    ratios = []
    for label in range(4):
        ratio = (one * shear_ref[label]) / (one * yields_ref[label])
        ratios.append(ratio * ratio)
    return [shear_ref[label] for label in range(4)], ratios


def force_scale(laplace, region, plastic, table):
    shears, ratios = table
    repeats = (region.shape[0] // 8, region.shape[1] // 128)
    modulus = jnp.full(region.shape, shears[0], F32)
    ratio = jnp.tile(ratios[0], repeats)
    for label in range(1, 4):
        modulus = jnp.where(region == label, shears[label], modulus)
        ratio = jnp.where(region == label, jnp.tile(ratios[label], repeats), ratio)
    squares = laplace[0] * laplace[0] + laplace[1] * laplace[1] + laplace[2] * laplace[2]
    capped = lax.rsqrt(1.0 + squares * ratio)
    return modulus * jnp.where(plastic > 0.5, capped, 1.0)


def strip_force(centers, sums, region, plastic, table):
    laplace = [total - 6.0 * center for total, center in zip(sums, centers)]
    scale = force_scale(laplace, region, plastic, table)
    return [scale * part for part in laplace]


def strip_of(i):
    return slice(i * 8, i * 8 + 8)


def stencil_strip(i, load, beside, load_above, load_below, halo_refs, z):
    top_ref, bottom_ref, left_ref, right_ref = halo_refs
    centers, sums = [], []
    for c in range(3):
        place = slot(c, z)
        center = load(c, strip_of(i))
        if i == 0:
            before = top_ref[pl.ds(place, 1), :]
        else:
            before = load(c, slice(i * 8 - 1, i * 8))
        if i == 7:
            after = bottom_ref[pl.ds(place, 1), :]
        else:
            after = load(c, slice(i * 8 + 8, i * 8 + 9))
        left = pltpu.roll(left_ref[strip_of(i), :], lax.rem(128 - place, 128), 1)
        right = pltpu.roll(right_ref[strip_of(i), :], 127 - place, 1)
        if beside is not None:
            before, after, left, right = beside(c, i, before, after, left, right)
        above = load_above(c, strip_of(i)) if load_above else None
        below = load_below(c, strip_of(i)) if load_below else None
        sums.append(neighbour_sum(center, above, below, before, after, left, right))
        centers.append(center)
    return centers, sums


def slot(c, z):
    return c * 16 + z


def edges_kernel(
    u_ref, v_ref, region_ref, flags_ref, first_ref, last_ref, left_ref, right_ref, plastic_ref
):
    step = pl.program_id(0)
    depth = u_ref.shape[1]

    @pl.when(step == 0)
    def _():
        left_ref[...] = jnp.zeros_like(left_ref)
        right_ref[...] = jnp.zeros_like(right_ref)
        wide = (rows_of((64, 8)) // 8 == lanes((64, 8))).astype(F32)
        high = (rows_of((32, 256)) == lanes((32, 256)) // 8).astype(F32)
        marks = (flags_ref[...] == 1).astype(F32)
        plastic = dot(dot(wide, marks), high)
        plastic_ref[...] = plastic
        first_ref[160:168, :] = jnp.broadcast_to(plastic[0:1], (8, 256))
        last_ref[160:168, :] = jnp.broadcast_to(plastic[63:64], (8, 256))
        lane = lanes((64, 128))
        left_ref[1] = jnp.where(lane == 64, pltpu.roll(plastic[:, :128], 64, 1), 0.0)
        right_ref[1] = jnp.where(lane == 64, pltpu.roll(plastic[:, 128:], 65, 1), 0.0)

    for k in range(depth):
        z = step * depth + k
        for c in range(3):
            place = slot(c, z)
            first_ref[pl.ds(place, 1), :] = u_ref[c, k, 0:1, :]
            last_ref[pl.ds(place, 1), :] = u_ref[c, k, 63:64, :]
            first_ref[pl.ds(48 + place, 1), :] = u_ref[c, k, 1:2, :]
            last_ref[pl.ds(48 + place, 1), :] = u_ref[c, k, 62:63, :]
            first_ref[pl.ds(96 + place, 1), :] = v_ref[c, k, 0:1, :]
            last_ref[pl.ds(96 + place, 1), :] = v_ref[c, k, 63:64, :]
        first_ref[pl.ds(144 + z, 1), :] = region_ref[k, 0:1, :].astype(F32)
        last_ref[pl.ds(144 + z, 1), :] = region_ref[k, 63:64, :].astype(F32)
    lane = lanes((8, 128))
    for i in range(8):
        rows = strip_of(i)
        total = [left_ref[0, rows, :], left_ref[1, rows, :], right_ref[0, rows, :], right_ref[1, rows, :]]

        def put(index, tile, source, target):
            moved = pltpu.roll(tile, lax.rem(target + (128 - source), 128), 1)
            total[index] = jnp.where(lane == target, moved, total[index])

        for k in range(depth):
            z = step * depth + k
            for c in range(3):
                place = slot(c, z)
                u0, u1 = u_ref[c, k, rows, 0:128], u_ref[c, k, rows, 128:256]
                put(0, u0, 0, place)
                put(0, u0, 1, place + 48)
                put(2, u1, 127, place)
                put(2, u1, 126, place + 48)
                put(1, v_ref[c, k, rows, 0:128], 0, place)
                put(3, v_ref[c, k, rows, 128:256], 127, place)
            put(1, region_ref[k, rows, 0:128].astype(F32), 0, z + 48)
            put(3, region_ref[k, rows, 128:256].astype(F32), 127, z + 48)
        left_ref[0, rows, :] = total[0]
        left_ref[1, rows, :] = total[1]
        right_ref[0, rows, :] = total[2]
        right_ref[1, rows, :] = total[3]


def beside_kernel(
    where_ref, shear_ref, yields_ref, first_ref, last_ref, left_ref, right_ref,
    top_ref, bottom_ref, west_ref, east_ref, lines_ref,
    new_top_ref, new_bottom_ref, new_west_ref, new_east_ref,
):
    narrow = where_ref[3]
    table = label_table(shear_ref, yields_ref)
    low = jnp.where(narrow > 0, lines_ref[jnp.maximum(narrow - 1, 0), 192:240, :], 0.0)
    high = jnp.where(narrow < 3, lines_ref[jnp.minimum(narrow + 1, 3), 192:240, :], 0.0)

    row = rows_of((16, 256))
    lane = lanes((16, 128))
    sides = (
        (top_ref, first_ref, new_top_ref, 0, where_ref[2] > 0),
        (bottom_ref, last_ref, new_bottom_ref, 1, where_ref[2] < 31),
    )
    for halo_ref, own_ref, out_ref, side, inside in sides:
        laplace = []
        for c in range(3):
            part = slice(c * 16, c * 16 + 16)
            center = halo_ref[part, :]
            total = halo_ref[48 + c * 16 : 64 + c * 16, :] + own_ref[part, :]
            total = total + jnp.where(row == 0, 0.0, pltpu.roll(center, 1, 0))
            total = total + jnp.where(row == 15, 0.0, pltpu.roll(center, 15, 0))
            c0, c1 = center[:, :128], center[:, 128:]
            before = pltpu.roll(low[part], 128 - side, 1) if side else low[part]
            after = pltpu.roll(high[part], 127 - side, 1)
            w0, w1 = pltpu.roll(c0, 1, 1), pltpu.roll(c1, 1, 1)
            e0, e1 = pltpu.roll(c0, 127, 1), pltpu.roll(c1, 127, 1)
            west = [jnp.where(lane == 0, before, w0), jnp.where(lane == 0, w0, w1)]
            east = [jnp.where(lane == 127, e1, e0), jnp.where(lane == 127, after, e1)]
            total = total + jnp.concatenate(west, 1) + jnp.concatenate(east, 1)
            laplace.append(total - 6.0 * center)
        plastic = jnp.broadcast_to(halo_ref[160:161, :], (16, 256))
        scale = force_scale(laplace, halo_ref[144:160, :].astype(jnp.int32), plastic, table)
        damping = jnp.where(row == 0, DAMPING, 0.0)
        for c in range(3):
            part = slice(c * 16, c * 16 + 16)
            v = halo_ref[96 + c * 16 : 112 + c * 16, :]
            v = v + DT * (scale * laplace[c] - damping * v)
            out_ref[part, :] = jnp.where(inside, halo_ref[part, :] + DT * v, 0.0)

    row = rows_of((64, 128))
    lane = lanes((64, 128))
    layer = lax.rem(lane, 16)
    used = lane < 48
    sides = (
        (west_ref, left_ref, new_west_ref, low, narrow > 0),
        (east_ref, right_ref, new_east_ref, high, narrow < 3),
    )
    for halo_ref, own_ref, out_ref, corner, inside in sides:
        tile, other = halo_ref[0], halo_ref[1]
        center = jnp.where(used, tile, 0.0)
        corners = jnp.concatenate([corner, jnp.zeros((80, 128), F32)], 0).T
        total = pltpu.roll(tile, 80, 1) + own_ref[0]
        total = total + jnp.where(row == 0, corners[0:1], pltpu.roll(center, 1, 0))
        total = total + jnp.where(row == 63, corners[1:2], pltpu.roll(center, 63, 0))
        total = total + jnp.where(layer == 0, 0.0, pltpu.roll(center, 1, 1))
        total = total + jnp.where(layer == 15, 0.0, pltpu.roll(center, 127, 1))
        laplace = jnp.where(used, total - 6.0 * center, 0.0)
        squares = laplace * laplace
        squares = (
            (squares + pltpu.roll(squares, 16, 1))
            + (pltpu.roll(squares, 32, 1) + pltpu.roll(squares, 96, 1))
            + pltpu.roll(squares, 112, 1)
        )
        region = jnp.where(
            lane < 16,
            pltpu.roll(other, 80, 1),
            jnp.where(lane < 32, pltpu.roll(other, 96, 1), pltpu.roll(other, 112, 1)),
        ).astype(jnp.int32)
        modulus = jnp.full(region.shape, table[0][0], F32)
        ratio = jnp.tile(table[1][0], (8, 1))
        for label in range(1, 4):
            modulus = jnp.where(region == label, table[0][label], modulus)
            ratio = jnp.where(region == label, jnp.tile(table[1][label], (8, 1)), ratio)
        capped = lax.rsqrt(1.0 + squares * ratio)
        scale = modulus * jnp.where(other[:, 64:65] > 0.5, capped, 1.0)
        v = other + DT * (scale * laplace - jnp.where(layer == 0, DAMPING, 0.0) * other)
        out_ref[...] = jnp.where(used & inside, center + DT * v, 0.0)


def slip_kernel(
    shear_ref, yields_ref, u_ref, v_ref, region_ref, plastic_ref,
    top_ref, bottom_ref, left_ref, right_ref, where_ref, _after_ref, send_ref,
):
    halo_refs = (top_ref, bottom_ref, left_ref.at[0], right_ref.at[0])
    table = label_table(shear_ref, yields_ref)
    lane = lanes((48, 128))
    t0, t1 = top_ref[0:48, 0:128], top_ref[0:48, 128:256]
    b0, b1 = bottom_ref[0:48, 0:128], bottom_ref[0:48, 128:256]
    to_lower = jnp.where(lane == 0, t0, pltpu.roll(b0, 1, 1))
    to_upper = jnp.where(lane == 0, pltpu.roll(t1, 1, 1), pltpu.roll(b1, 2, 1))
    for n in range(4):
        send_ref[n, 192:240, :] = jnp.where(where_ref[3] < n, to_upper, to_lower)
    for i in range(8):
        rows = strip_of(i)
        centers, sums = stencil_strip(
            i,
            lambda c, r: u_ref[c, 0, r, :],
            None,
            lambda c, r: u_ref[c, 1, r, :],
            None,
            halo_refs,
            0,
        )
        force = strip_force(
            centers, sums, region_ref[0, rows, :], plastic_ref[rows, :], table
        )
        n, part = i // 2, (i % 2) * 8
        for c in range(3):
            v = v_ref[c, 0, rows, :]
            v = v + DT * (force[c] - DAMPING * v)
            moved = centers[c] + DT * v
            for f, values in enumerate((centers[c], moved)):
                for half in range(2):
                    start = f * 96 + c * 32 + half * 16 + part
                    send_ref[n, start : start + 8, :] = values[:, half * 128 : half * 128 + 128]


def step_one_kernel(
    shear_ref, yields_ref, u_ref, v_ref, region_ref, plastic_ref,
    top_ref, bottom_ref, left_ref, right_ref, _after_ref,
    new_u_ref, new_v_ref,
):
    step = pl.program_id(0)

    halo_refs = (top_ref, bottom_ref, left_ref.at[0], right_ref.at[0])
    table = label_table(shear_ref, yields_ref)
    for k in range(PLANES):
        z = step * PLANES + k
        damping = jnp.where(z == 0, DAMPING, 0.0).astype(F32)
        lower = jnp.where(z > 0, 1.0, 0.0).astype(F32)
        upper = jnp.where(z < 15, 1.0, 0.0).astype(F32)
        if k < PLANES - 1:
            load_above = lambda c, r: u_ref[c, z + 1, r, :]
        else:
            load_above = lambda c, r: u_ref[c, jnp.minimum(z + 1, 15), r, :] * upper
        if k > 0:
            load_below = lambda c, r: u_ref[c, z - 1, r, :]
        else:
            load_below = lambda c, r: u_ref[c, jnp.maximum(z - 1, 0), r, :] * lower
        for i in range(8):
            rows = strip_of(i)
            centers, sums = stencil_strip(
                i, lambda c, r: u_ref[c, z, r, :], None, load_above, load_below, halo_refs, z
            )
            force = strip_force(
                centers, sums, region_ref[k, rows, :], plastic_ref[rows, :], table
            )
            for c in range(3):
                v = v_ref[c, k, rows, :]
                v = v + DT * (force[c] - damping * v)
                u = centers[c] + DT * v
                new_v_ref[c, k, rows, :] = v
                new_u_ref[c, k, rows, :] = u


def step_two_kernel(start, *refs):
    (shear_ref, yields_ref, u_ref, v_ref, region_ref, plastic_ref) = refs[:6]
    halo_refs = refs[6:10]
    table = label_table(shear_ref, yields_ref)
    new_u_ref, new_v_ref = refs[-2:]
    for k in range(PLANES):
        z = pl.program_id(0) * PLANES + (start + k)
        upper = jnp.where(z < 15, 1.0, 0.0).astype(F32)
        if k < PLANES - 1:
            load_above = lambda c, r: u_ref[c, z + 1, r, :]
        else:
            load_above = lambda c, r: u_ref[c, jnp.minimum(z + 1, 15), r, :] * upper
        for i in range(8):
            rows = strip_of(i)
            centers, sums = stencil_strip(
                i,
                lambda c, r: u_ref[c, z, r, :],
                None,
                load_above,
                lambda c, r: u_ref[c, z - 1, r, :],
                halo_refs,
                z,
            )
            force = strip_force(
                centers, sums, region_ref[k, rows, :], plastic_ref[rows, :], table
            )
            for c in range(3):
                v = v_ref[c, k, rows, :] + DT * force[c]
                new_v_ref[c, k, rows, :] = v
                new_u_ref[c, k, rows, :] = centers[c] + DT * v


def last_kernel(
    shear_ref, yields_ref, u_ref, v_ref, region_ref, plastic_ref,
    top_ref, bottom_ref, left_ref, right_ref,
    recv_ref, _old_u_ref, _old_v_ref, new_u_ref, new_v_ref, surface,
):
    square = DT * DT
    table = label_table(shear_ref, yields_ref)
    halo_refs = (top_ref, bottom_ref, left_ref, right_ref)

    def traction(f, c, i):
        start = f * 96 + c * 32 + (i % 2) * 8
        return jnp.concatenate(
            [recv_ref[i // 2, start + half * 16 : start + half * 16 + 8, :] for half in range(2)], 1
        )

    def outside(n, c, side):
        row = 208 + c * 2 + side
        return jnp.concatenate(
            [recv_ref[n, row + half * 8 : row + half * 8 + 1, :] for half in range(2)], 1
        )

    def beside(c, i, before, after, left, right):
        if i == 0:
            before = before + square * outside(0, c, 0)
        if i == 7:
            after = after + square * outside(3, c, 1)
        start = 192 + (i % 2) * 8
        columns = recv_ref[i // 2, start : start + 8, :]
        left = left + square * pltpu.roll(columns, (128 - c) % 128, 1)
        right = right + square * pltpu.roll(columns, 127 - (3 + c), 1)
        return before, after, left, right

    for i in range(8):
        for c in range(3):
            surface[c, strip_of(i), :] = u_ref[c, 0, strip_of(i), :] + square * traction(0, c, i)
    for z in range(2):
        for i in range(8):
            rows = strip_of(i)
            above = lambda c, r: u_ref[c, z + 1, r, :]
            if z == 0:
                load, below = lambda c, r: surface[c, r, :], None
            else:
                load, below = lambda c, r: u_ref[c, 1, r, :], lambda c, r: surface[c, r, :]
            centers, sums = stencil_strip(
                i, load, beside if z == 0 else None, above, below, halo_refs, z
            )
            force = strip_force(
                centers, sums, region_ref[z, rows, :], plastic_ref[rows, :], table
            )
            for c in range(3):
                v = v_ref[c, z, rows, :]
                if z == 0:
                    v = v + DT * traction(0, c, i)
                    v = v + DT * (force[c] + (traction(1, c, i) - DAMPING * v))
                else:
                    v = v + DT * force[c]
                new_v_ref[c, z, rows, :] = v
                new_u_ref[c, z, rows, :] = centers[c] + DT * v


def history_kernel(where_ref, kernel_ref, history_ref, *refs):
    own_ref, main_ref, edge_ref = refs[-3:]
    low = where_ref[0] == 1
    width = own_ref.shape[1]

    def step(m, carry):
        total, ones = carry
        out, twos = [], []
        for c in range(3):
            two = kernel_ref[m + 2, c].astype(F32)
            twos.append(two)
            for ri in range(2):
                past = history_ref[m, ri, c].astype(F32)
                p1, p2 = total[c * 2 + ri]
                out.append((p1 + ones[c] * past, p2 + two * past))
        return tuple(out), tuple(twos)

    def block(j, carry):
        for k in range(UNROLL):
            carry = step(j * UNROLL + k, carry)
        return carry

    zero = jnp.zeros((8, width), F32)
    carry = (
        tuple((zero, zero) for _ in range(6)),
        tuple(kernel_ref[1, c].astype(F32) for c in range(3)),
    )
    carry = lax.fori_loop(0, 30 // UNROLL, block, carry)
    total, _ = step(30, carry)
    values = [None] * 18
    for c in range(3):
        one = kernel_ref[32, c].astype(F32)
        for ri in range(2):
            p1, p2 = total[c * 2 + ri]
            values[ri * 3 + c] = p1 + one * history_ref[31, ri, c].astype(F32)
            values[6 + ri * 3 + c] = p2
        values[12 + c] = kernel_ref[0, c].astype(F32)
        values[15 + c] = kernel_ref[1, c].astype(F32)
    for i, value in enumerate(values):
        row = [value[r : r + 1] for r in range(8)]
        for r, (a, b) in enumerate(((0, 4), (1, 3), (2, 2), (3, 1))):
            own_ref[i * 4 + r : i * 4 + r + 1, :] = jnp.where(low, row[a], row[b])
        for r, (a, b) in enumerate(((4, 4), (5, 7), (6, 6), (7, 5))):
            main_ref[i * 4 + r : i * 4 + r + 1, :] = jnp.where(low, row[a], row[b])
        edge_ref[i : i + 1, :] = row[0]


def mirror_kernel(where_ref, reverse_ref, own_ref, main_ref, edge_ref, out_ref, tiles, turned):
    low = where_ref[0] == 1
    special = where_ref[1]
    for i in range(18):
        own = own_ref[i * 4 : i * 4 + 4, :]
        main = main_ref[i * 4 : i * 4 + 4, :]
        edge = edge_ref[i : i + 1, :]
        other = jnp.where(rows_of(main.shape) == 0, edge, main)
        tiles[i * 8 : i * 8 + 4, :] = jnp.where(low, own, main)
        tiles[i * 8 + 4 : i * 8 + 8, :] = jnp.where(low, other, own)
    for block in range(16):
        part = slice(block * 128, block * 128 + 128)
        high, rest = halves(tiles[:, part])
        turned[:, part] = dot(high, reverse_ref[...]) + dot(rest, reverse_ref[...])
    lane = lanes((8, 128))
    row = rows_of((8, 128))
    upper = row >= 4
    chosen = (lax.rem(row, 4) + (1 - special)) == 0

    def swap(x):
        return pltpu.roll(x, 4, 0)

    for block in range(16):
        part = slice(block * 128, block * 128 + 128)
        mirror = slice((15 - block) * 128, (15 - block) * 128 + 128)
        first = ((16 - block) % 16) * 128
        first = slice(first, first + 128)

        def load(i):
            rows = slice(i * 8, i * 8 + 8)
            back = jnp.where(lane == 0, turned[rows, first], turned[rows, mirror])
            return tiles[rows, part], back

        for c in range(3):
            for k in range(2):
                t, b = load(12 + k * 3 + c)
                own = 0.5 * (t + b)
                other = swap(own)
                mean = jnp.where(chosen, 0.5 * (own + other), 0.5 * (t + swap(b)))
                diff = jnp.where(chosen, 0.5 * (own - other), 0.0)
                out_ref[k, c, :, part] = jnp.where(upper, swap(mean), mean)
                out_ref[2 + k, c, :, part] = jnp.where(upper, swap(diff), diff)
            pair = []
            for k in range(2):
                tr, br = load(k * 6 + c)
                ti, bi = load(k * 6 + 3 + c)
                hr, hi = 0.5 * (tr + br), 0.5 * (ti - bi)
                sr, si = swap(hr), swap(hi)
                pair.append(
                    (
                        jnp.where(chosen, hr - si, 0.5 * (tr + swap(br))),
                        jnp.where(chosen, hi + sr, 0.5 * (ti - swap(bi))),
                        hr + si,
                        hi - sr,
                    )
                )
            out_ref[4, c, :, part] = jnp.where(upper, swap(pair[1][0]), pair[0][0])
            out_ref[5, c, :, part] = jnp.where(upper, swap(pair[1][1]), pair[0][1])
            out_ref[6, c, :, part] = pair[0][2]
            out_ref[7, c, :, part] = pair[0][3]


def dip_kernel(radix_ref, turn_ref, out_table_ref, recv_ref, _after_ref, send_ref):
    wide = []
    for c in range(3):
        pieces = []
        for n in range(4):
            for f in range(2):
                start = f * 96 + c * 32
                pieces.append(recv_ref[n, start : start + 32, :])
        wide.append(jnp.concatenate(pieces, 0))
    z = left_dot(radix_ref, jnp.concatenate(wide, 1))
    lane = lanes((1, 128))
    for s in range(2):
        tr, ti = jnp.tile(turn_ref[0, s], (16, 1)), jnp.tile(turn_ref[1, s], (16, 1))
        for c in range(3):
            part = slice(c * 128, c * 128 + 128)
            zr = z[s * 128 : s * 128 + 128, part]
            zi = z[256 + s * 128 : 384 + s * 128, part]
            turned = jnp.concatenate([zr * tr - zi * ti, zr * ti + zi * tr], 1)
            high, low = halves(turned)
            table, rest = out_table_ref[0, s], out_table_ref[1, s]
            res = dot(table, high, (1, 1)) + (dot(rest, high, (1, 1)) + dot(table, low, (1, 1)))
            imag = res[64:128]
            if s == 0:
                extra = jnp.where(lax.rem(lane, 4) == 0, res[128:129], 0.0)
                imag = jnp.where(rows_of(imag.shape) == 0, imag + extra, imag)
            send_ref[pl.ds(s * 384 + c * 2, 64, stride=6), :] = res[0:64]
            send_ref[pl.ds(s * 384 + c * 2 + 1, 64, stride=6), :] = imag


def strike_kernel(
    in_ref, turn_ref, mix_ref, reverse_ref, out_table_ref,
    coef_ref, recv_ref, _after_ref, send_ref, spec, back, total,
):
    tr, ti = turn_ref[0], turn_ref[1]
    real, imag = [], []
    for c in range(3):
        re = recv_ref[pl.ds(c * 2, 128, stride=6), :].T
        im = recv_ref[pl.ds(c * 2 + 1, 128, stride=6), :].T
        y = right_dot(jnp.concatenate([re, im], 1), in_ref)
        yr, yi = y[:, :128], y[:, 128:]
        real.append(yr * tr - yi * ti)
        imag.append(yr * ti + yi * tr)
    stacked = jnp.concatenate([jnp.concatenate(real, 1), jnp.concatenate(imag, 1)], 0)
    spec[...] = left_dot(mix_ref, stacked)
    for c in range(3):
        part = slice(c * 128, c * 128 + 128)
        high, low = halves(spec[:, part])
        back[:, part] = dot(high, reverse_ref[...]) + dot(low, reverse_ref[...])
    lane = lanes((8, 128))
    upper = rows_of((8, 128)) >= 4

    def swap(x):
        return pltpu.roll(x, 4, 0)

    for c in range(3):
        part = slice(c * 128, c * 128 + 128)
        for block in range(16):
            wave = slice(block * 128, block * 128 + 128)
            a0, a1 = coef_ref[0, c, :, wave], coef_ref[1, c, :, wave]
            m0, m1 = coef_ref[2, c, :, wave], coef_ref[3, c, :, wave]
            for ri in range(2):
                rows = slice(ri * 128 + block * 8, ri * 128 + block * 8 + 8)
                first = ri * 128 + ((16 - block) % 16) * 8
                other = ri * 128 + (15 - block) * 8
                s = spec[rows, part]
                r = jnp.where(
                    lane == 0, back[first : first + 8, part], back[other : other + 8, part]
                )
                if ri == 1:
                    r = -r
                t = a0 * s + m0 * r + coef_ref[4 + ri, c, :, wave]
                q = a0 * r + m0 * s + coef_ref[6 + ri, c, :, wave]
                more = (DT * DT) * (a0 * swap(t) + m0 * swap(q)) + a1 * swap(s) + m1 * swap(r)
                g = t + jnp.where(upper, more, 0.0)
                total[rows, part] = g if ri == 0 else -g
    y = left_dot(mix_ref, total[...])
    owner = rows_of((128, 128))
    wide_lane = lanes((128, 128))
    extra = [jnp.zeros((128, 128), F32)] * 2
    for c in range(3):
        part = slice(c * 128, c * 128 + 128)
        yr, yi = y[:128, part], -y[128:, part]
        turned = jnp.concatenate([yr * tr + yi * ti, yi * tr - yr * ti], 1)
        high, low = halves(turned)
        res = dot(out_table_ref[0], high, (1, 1)) + (
            dot(out_table_ref[1], high, (1, 1)) + dot(out_table_ref[0], low, (1, 1))
        )
        for ri in range(2):
            lines = res[ri * 128 : ri * 128 + 128]
            send_ref[pl.ds(c * 2 + ri, 128, stride=8), :] = lines
            for side in range(2):
                group = c * 2 + side
                if side == 0:
                    moved = jnp.where(owner == 0, 0.0, pltpu.roll(lines, 1, 0))
                    moved = pltpu.roll(moved, (group * 8 + 8) % 128, 1)
                else:
                    moved = jnp.where(owner == 127, 0.0, pltpu.roll(lines, 127, 0))
                    moved = pltpu.roll(moved, group * 8, 1) if group else moved
                extra[ri] = jnp.where(wide_lane // 8 == group, moved, extra[ri])
    for ri in range(2):
        send_ref[pl.ds(6 + ri, 128, stride=8), :] = extra[ri]


def undip_kernel(in_ref, turn_ref, unradix_ref, recv_ref, _after_ref, send_ref):
    row = rows_of((128, 128))
    lane = lanes((128, 128))
    alt = jnp.where(lax.rem(lane, 2) == 0, 0.5, -0.5).astype(F32)
    stacks = [[], [], [], []]
    for c in range(4):
        re = recv_ref[pl.ds(c * 2, 128, stride=8), :].T
        im = recv_ref[pl.ds(c * 2 + 1, 128, stride=8), :].T
        h = right_dot(jnp.concatenate([re, im], 1), in_ref)
        for s in range(2):
            hr = h[:, s * 256 : s * 256 + 128]
            hi = h[:, s * 256 + 128 : s * 256 + 256]
            if s == 0:
                fix = alt * im[:, 0:1] - 0.5 * re[:, 0:1]
                hr = hr + jnp.where(lax.rem(row, 4) == 0, fix, 0.0)
            tr, ti = jnp.tile(turn_ref[0, s], (16, 1)), jnp.tile(turn_ref[1, s], (16, 1))
            stacks[s].append(hr * tr + hi * ti)
            stacks[2 + s].append(hi * tr - hr * ti)
    stacked = jnp.concatenate([jnp.concatenate(part, 1) for part in stacks], 0)
    out = left_dot(unradix_ref, stacked)
    for n in range(4):
        for f in range(2):
            for c in range(3):
                start = f * 96 + c * 32
                row0 = (n * 2 + f) * 32
                send_ref[n, start : start + 32, :] = out[row0 : row0 + 32, c * 128 : c * 128 + 128]
    small = lanes((16, 128))

    def plane(n, half, c):
        row0 = n * 64 + half * 16
        return out[row0 : row0 + 16, c * 128 : c * 128 + 128]

    for n in range(4):
        columns = jnp.zeros((16, 128), F32)
        for c in range(3):
            if n > 0:
                moved = pltpu.roll(plane(n - 1, 1, c), c + 1, 1)
                columns = jnp.where(small == c, moved, columns)
            if n < 3:
                moved = pltpu.roll(plane(n + 1, 0, c), 3 + c, 1)
                columns = jnp.where(small == 3 + c, moved, columns)
        send_ref[n, 192:208, :] = columns
        for half in range(2):
            send_ref[n, 208 + half * 8 : 216 + half * 8, :] = plane(n, half, 3)[:8]


def full(shape):
    del shape
    return pl.BlockSpec(memory_space=pltpu.VMEM)


SMEM = pl.BlockSpec(memory_space=pltpu.SMEM)


def in_hbm(x):
    return pltpu.with_memory_space_constraint(x, pltpu.HBM)


def hbm_shape(*shape):
    return pltpu.HBM(shape, F32)


def shape_of(*shape):
    return jax.ShapeDtypeStruct(shape, F32)


def call(body, out_shape, args, smem=0, scratch=(), after=(), name=None, limit=16 << 20):
    outs = out_shape if isinstance(out_shape, (tuple, list)) else [out_shape]
    size = sum(math.prod(x.shape) * 4 for x in list(args) + list(outs))
    out_specs = [full(x.shape) for x in outs]
    return pl.pallas_call(
        body,
        in_specs=[SMEM] * smem
        + [full(x.shape) for x in args[smem:]]
        + [pl.BlockSpec(memory_space=pl.ANY)] * len(after),
        out_specs=out_specs if isinstance(out_shape, (tuple, list)) else out_specs[0],
        out_shape=out_shape,
        scratch_shapes=scratch,
        cost_estimate=pl.CostEstimate(flops=0, bytes_accessed=size, transcendentals=0),
        compiler_params=pltpu.CompilerParams(vmem_limit_bytes=limit),
        name=name,
    )(*args, *(in_hbm(x) for x in after))


def halo(first, last, left, right):
    up = [(i, i + 1) for i in range(31)]
    down = [(i + 1, i) for i in range(31)]
    top = lax.ppermute(last, "wide", up)
    bottom = lax.ppermute(first, "wide", down)
    up = [(i, i + 1) for i in range(3)]
    down = [(i + 1, i) for i in range(3)]
    from_left = lax.ppermute(right, "narrow", up)
    from_right = lax.ppermute(left, "narrow", down)
    return top, bottom, from_left, from_right


def exchange(x, axis):
    return lax.all_to_all(x, axis, split_axis=0, concat_axis=0, tiled=True)


def body(u, v, region, flags, shear, yields, history, kernel):
    device = lax.axis_index(ALL)
    where = jnp.stack(
        [
            (device < 64).astype(jnp.int32),
            (device == 0).astype(jnp.int32),
            lax.axis_index("wide"),
            lax.axis_index("narrow"),
        ]
    )
    edge_shapes = [shape_of(168, 256)] * 2 + [shape_of(2, 64, 128)] * 2
    halo_shapes = [shape_of(48, 256)] * 2 + [shape_of(64, 128)] * 2
    near = lambda depth: pl.BlockSpec((3, depth, 64, 256), lambda *_: (0, 0, 0, 0))
    slab = lambda depth: pl.BlockSpec((depth, 64, 256), lambda *_: (0, 0, 0))
    planes = lambda depth, start=0: pl.BlockSpec(
        (3, depth, 64, 256), lambda z: (0, z + start // depth, 0, 0)
    )
    slabs = lambda depth, start=0: pl.BlockSpec(
        (depth, 64, 256), lambda z: (z + start // depth, 0, 0)
    )
    halo_specs = [full((48, 256))] * 2 + [full((64, 128))] * 2
    any_spec = pl.BlockSpec(memory_space=pl.ANY)
    t = TABLES
    u, v, region, history, kernel = (in_hbm(x) for x in (u, v, region, history, kernel))
    shear, yields, where = in_hbm(shear), in_hbm(yields), in_hbm(where)

    first, last, left, right, plastic = pl.pallas_call(
        edges_kernel,
        grid=(4,),
        in_specs=[planes(4), planes(4), slabs(4), full((8, 32))],
        out_specs=[full(s.shape) for s in edge_shapes] + [full((64, 256))],
        out_shape=edge_shapes + [hbm_shape(64, 256)],
        cost_estimate=pl.CostEstimate(flops=0, bytes_accessed=8000000, transcendentals=0),
        compiler_params=pltpu.CompilerParams(vmem_limit_bytes=16 << 20),
            name="edges",
    )(u, v, region, in_hbm(flags))
    halo_one = halo(first, last, left, right)
    plastic = in_hbm(plastic)

    width = 256
    steps = 1024 // width

    def sums(part, after):
        shift = part * steps
        given = [] if part == 0 else list(after)
        return pl.pallas_call(
            history_kernel,
            grid=(steps,),
            in_specs=[
                SMEM,
                pl.BlockSpec((33, 3, 8, width), lambda i: (0, 0, 0, i + shift)),
                pl.BlockSpec((32, 2, 3, 8, width), lambda i: (0, 0, 0, 0, i + shift)),
            ]
            + [any_spec] * len(given),
            out_specs=[
                pl.BlockSpec((72, width), lambda i: (0, i + shift)),
                pl.BlockSpec((72, width), lambda i: (0, i + shift)),
                pl.BlockSpec((18, width), lambda i: (0, i + shift)),
            ],
            out_shape=[hbm_shape(72, 2048), hbm_shape(72, 2048), hbm_shape(18, 2048)],
            input_output_aliases={3: 0, 4: 1, 5: 2} if given else {},
            cost_estimate=pl.CostEstimate(flops=0, bytes_accessed=5500000, transcendentals=0),
            compiler_params=pltpu.CompilerParams(vmem_limit_bytes=16 << 20),
            name="history",
        )(where, kernel, history, *(in_hbm(x) for x in given))

    partial = sums(0, None)
    send = pl.pallas_call(
        slip_kernel,
        grid=(1,),
        in_specs=[SMEM, SMEM, near(2), near(1), slab(1), full((64, 256))]
        + halo_specs
        + [SMEM, any_spec],
        out_specs=full((4, 240, 128)),
        out_shape=shape_of(4, 240, 128),
        cost_estimate=pl.CostEstimate(flops=0, bytes_accessed=1500000, transcendentals=0),
        compiler_params=pltpu.CompilerParams(vmem_limit_bytes=16 << 20),
            name="slip",
    )(shear, yields, u, v, region, plastic, *halo_one, where, in_hbm(partial[2]))
    lines = exchange(send, "narrow")
    own, main, edge = sums(1, partial)
    main = lax.ppermute(main, ALL, [(i, 127 - i) for i in range(128)])
    edge = lax.ppermute(edge, ALL, [(64, 0)] + [(i, 128 - i) for i in range(65, 128)])

    send = call(
        dip_kernel, shape_of(768, 128), (t["radix"], t["dip_turn"], t["dip_out"], lines),
        after=[own], name="dip",
    )
    waves = exchange(send.reshape(128, 1, 768), ALL).reshape(768, 128)

    new_u, new_v = pl.pallas_call(
        step_one_kernel,
        grid=(16 // PLANES,),
        in_specs=[SMEM, SMEM, near(16), planes(PLANES), slabs(PLANES), full((64, 256))]
        + halo_specs
        + [any_spec],
        out_specs=[planes(PLANES)] * 2,
        out_shape=[hbm_shape(3, 16, 64, 256)] * 2,
        cost_estimate=pl.CostEstimate(flops=0, bytes_accessed=14000000, transcendentals=0),
        compiler_params=pltpu.CompilerParams(vmem_limit_bytes=24 << 20),
            name="step_one",
    )(shear, yields, u, v, region, plastic, *halo_one, in_hbm(send))
    new_u, new_v = in_hbm(new_u), in_hbm(new_v)
    halo_two = call(
        beside_kernel,
        halo_shapes,
        (where, shear, yields, *(in_hbm(x) for x in (first, last, left, right, *halo_one, lines))),
        smem=3,
        name="beside",
    )

    coefficients = call(
        mirror_kernel,
        shape_of(8, 3, 8, 2048),
        (where, t["reverse"], *(in_hbm(x) for x in (own, main, edge))),
        smem=1,
        scratch=[pltpu.VMEM((144, 2048), F32)] * 2,
        name="mirror",
    )
    send = call(
        strike_kernel,
        shape_of(1024, 128),
        (
            t["strike_in"], t["strike_turn"], t["strike_mix"], t["reverse"],
            t["strike_out"], coefficients, waves,
        ),
        scratch=[pltpu.VMEM((256, 384), F32)] * 3,
        after=[new_u],
        name="strike",
    )
    columns = exchange(send.reshape(128, 8, 128), ALL).reshape(1024, 128)

    def later(start, stop, given, after):
        return pl.pallas_call(
            functools.partial(step_two_kernel, start),
            grid=((stop - start) // PLANES,),
            in_specs=[
                SMEM, SMEM, near(16), planes(PLANES, start), slabs(PLANES, start), full((64, 256)),
            ]
            + halo_specs
            + [any_spec] * (len(given) + 1),
            out_specs=[planes(PLANES, start)] * 2,
            out_shape=[hbm_shape(3, 16, 64, 256)] * 2,
            input_output_aliases={10: 0, 11: 1} if given else {},
            cost_estimate=pl.CostEstimate(
                flops=0, bytes_accessed=(stop - start) * 800000, transcendentals=0
            ),
            compiler_params=pltpu.CompilerParams(vmem_limit_bytes=24 << 20),
            name="step_two",
        )(shear, yields, new_u, new_v, region, plastic, *halo_two, *given, in_hbm(after))

    out = later(2, 10, [], send)
    send = call(
        undip_kernel,
        shape_of(4, 224, 128),
        (t["dip_in"], t["undip_turn"], t["unradix"], columns),
        after=[out[0]],
        name="undip",
    )
    tractions = exchange(send, "narrow")
    out = later(10, 16, out, send)
    return tuple(
        pl.pallas_call(
            last_kernel,
            grid=(1,),
            in_specs=[SMEM, SMEM, near(4), near(2), slab(2), full((64, 256))]
            + halo_specs
            + [full((4, 224, 128))]
            + [any_spec] * 2,
            out_specs=[near(2)] * 2,
            out_shape=[hbm_shape(3, 16, 64, 256)] * 2,
            scratch_shapes=[pltpu.VMEM((3, 64, 256), F32)],
            input_output_aliases={11: 0, 12: 1},
            cost_estimate=pl.CostEstimate(flops=0, bytes_accessed=4000000, transcendentals=0),
            compiler_params=pltpu.CompilerParams(vmem_limit_bytes=16 << 20),
            name="last",
        )(shear, yields, new_u, new_v, region, plastic, *halo_two, tractions, *out)
    )


def solution(mesh):
    tile = P(None, None, "wide", "narrow")
    in_specs = (
        tile,
        tile,
        P(None, "wide", "narrow"),
        P("wide", "narrow"),
        P(),
        P(),
        P(None, None, None, ALL, None),
        P(None, None, ALL, None),
    )
    return jax.shard_map(body, mesh=mesh, in_specs=in_specs, out_specs=(tile, tile), check_vma=False)
```

```python
import functools
import math

import jax
import jax.numpy as jnp
import ml_dtypes
import numpy as np
from jax import lax
from jax.experimental import pallas as pl
from jax.experimental.pallas import tpu as pltpu
from jax.sharding import PartitionSpec as P


DT = 0.1
DAMPING = 0.5
ALL = ("wide", "narrow")
UNROLL = 6
CUTS = (4, 11)
F32 = jnp.float32
BF16 = jnp.bfloat16


def split_table(table):
    table = np.asarray(table, np.float64)
    high = table.astype(ml_dtypes.bfloat16)
    low = (table - high.astype(np.float64)).astype(ml_dtypes.bfloat16)
    return np.stack([high, low])


def make_tables():
    factor = 1.0 / math.sqrt(2048 * 1024)
    eye2 = np.eye(2)
    eye8 = np.eye(8)
    eye16 = np.eye(16)
    r8 = np.arange(8).reshape(2, 4)
    y1 = np.arange(8).reshape(4, 2)
    theta = 2 * np.pi * r8[:, :, None, None] * y1[None, None] / 8
    radix = np.stack([np.cos(theta), -np.sin(theta)])
    radix = np.einsum("isrnl,xz,fg->isxfrnglz", radix, eye16, eye2).reshape(512, 256)
    unradix = np.stack([np.cos(theta), -np.sin(theta)])
    unradix = np.einsum("isrnl,xz,fg->nglzisxfr", unradix, eye16, eye2).reshape(256, 512)
    y0 = np.arange(128)
    theta = 2 * np.pi * r8[:, :, None] * y0 / 1024
    turn = np.stack([np.cos(theta), -np.sin(theta)])[:, :, None]
    dip_turn = np.broadcast_to(turn, (2, 2, 2, 4, 128)).reshape(2, 2, 8, 128) * factor
    alt = (-1.0) ** y0
    place = np.stack([np.arange(64), 63 - np.arange(64)])
    theta = 2 * np.pi * place[:, :, None] * y0 / 128
    cos, sin = np.cos(theta), np.sin(theta)
    dip_out = np.zeros((2, 136, 256))
    dip_out[:, :64] = np.concatenate([cos, sin], -1)
    dip_out[:, 64:128] = np.concatenate([-sin, cos], -1)
    dip_out[0, 128, :128] = alt
    dip_in = np.zeros((2, 128, 2, 2, 128))
    for s in range(2):
        rows = slice(s * 64, s * 64 + 64)
        dip_in[0, rows, s, 0] = cos[s]
        dip_in[0, rows, s, 1] = sin[s]
        dip_in[1, rows, s, 0] = -sin[s]
        dip_in[1, rows, s, 1] = cos[s]
    dip_in = dip_in.reshape(256, 512)
    theta = 2 * np.pi * np.outer(y0, y0) / 128
    cos, sin = np.cos(theta), np.sin(theta)
    strike_in = np.block([[cos, -sin], [sin, cos]])
    strike_out = np.block([[cos, -sin], [sin, cos]])
    a = np.arange(16)
    theta = 2 * np.pi * np.outer(a, y0) / 2048
    turn = np.stack([np.cos(theta), -np.sin(theta)])
    strike_turn = np.broadcast_to(turn[:, :, None], (2, 16, 8, 128)).reshape(2, 128, 128)
    theta = 2 * np.pi * np.outer(a, a) / 16
    cos, sin = np.kron(np.cos(theta), eye8), np.kron(np.sin(theta), eye8)
    strike_mix = np.block([[cos, sin], [-sin, cos]])
    reverse = np.zeros((128, 128))
    reverse[(128 - y0) % 128, y0] = 1.0
    return {
        "radix": split_table(radix),
        "unradix": split_table(unradix),
        "dip_turn": dip_turn.astype(np.float32),
        "undip_turn": (dip_turn * 2.0).astype(np.float32),
        "dip_out": split_table(dip_out),
        "dip_in": split_table(dip_in),
        "strike_in": split_table(strike_in),
        "strike_out": split_table(strike_out),
        "strike_turn": strike_turn.astype(np.float32),
        "strike_mix": split_table(strike_mix),
        "reverse": reverse.astype(ml_dtypes.bfloat16),
    }


TABLES = make_tables()


def halves(x):
    high = x.astype(BF16)
    return high, (x - high.astype(F32)).astype(BF16)


def dot(a, b, contract=(1, 0)):
    return lax.dot_general(
        a, b, (((contract[0],), (contract[1],)), ((), ())), preferred_element_type=F32
    )


def left_dot(table, x, contract=(1, 0)):
    high, low = halves(x)
    return dot(table[0], high, contract) + (
        dot(table[1], high, contract) + dot(table[0], low, contract)
    )


def right_dot(x, table):
    high, low = halves(x)
    return dot(high, table[0]) + (dot(low, table[0]) + dot(high, table[1]))


def lanes(shape):
    return lax.broadcasted_iota(jnp.int32, shape, len(shape) - 1)


def rows_of(shape):
    return lax.broadcasted_iota(jnp.int32, shape, len(shape) - 2)


def neighbour_sum(center, above, below, before, after, left, right):
    rows = rows_of(center.shape)
    north = jnp.where(rows == 0, before, pltpu.roll(center, 1, 0))
    south = jnp.where(rows == 7, after, pltpu.roll(center, 7, 0))
    c0, c1 = center[:, :128], center[:, 128:]
    lane = lanes(c0.shape)
    w0, w1 = pltpu.roll(c0, 1, 1), pltpu.roll(c1, 1, 1)
    e0, e1 = pltpu.roll(c0, 127, 1), pltpu.roll(c1, 127, 1)
    west = jnp.concatenate([jnp.where(lane == 0, left, w0), jnp.where(lane == 0, w0, w1)], 1)
    east = jnp.concatenate([jnp.where(lane == 127, e1, e0), jnp.where(lane == 127, right, e1)], 1)
    total = (north + south) + (west + east)
    for other in (above, below):
        if other is not None:
            total = total + other
    return total


def label_table(shear_ref, yields_ref):
    one = jnp.ones((8, 128), F32)
    ratios = []
    for label in range(4):
        ratio = (one * shear_ref[label]) / (one * yields_ref[label])
        ratios.append(ratio * ratio)
    return [shear_ref[label] for label in range(4)], ratios


def force_scale(laplace, region, plastic, table):
    shears, ratios = table
    repeats = (region.shape[0] // 8, region.shape[1] // 128)
    modulus = jnp.full(region.shape, shears[0], F32)
    ratio = jnp.tile(ratios[0], repeats)
    for label in range(1, 4):
        modulus = jnp.where(region == label, shears[label], modulus)
        ratio = jnp.where(region == label, jnp.tile(ratios[label], repeats), ratio)
    squares = laplace[0] * laplace[0] + laplace[1] * laplace[1] + laplace[2] * laplace[2]
    capped = lax.rsqrt(1.0 + squares * ratio)
    return modulus * jnp.where(plastic > 0.5, capped, 1.0)


def strip_force(centers, sums, region, plastic, table):
    laplace = [total - 6.0 * center for total, center in zip(sums, centers)]
    scale = force_scale(laplace, region, plastic, table)
    return [scale * part for part in laplace]


def strip_of(i):
    return slice(i * 8, i * 8 + 8)


def stencil_strip(i, load, beside, load_above, load_below, halo_refs, z):
    top_ref, bottom_ref, left_ref, right_ref = halo_refs
    centers, sums = [], []
    for c in range(3):
        place = slot(c, z)
        center = load(c, strip_of(i))
        if i == 0:
            before = top_ref[pl.ds(place, 1), :]
        else:
            before = load(c, slice(i * 8 - 1, i * 8))
        if i == 7:
            after = bottom_ref[pl.ds(place, 1), :]
        else:
            after = load(c, slice(i * 8 + 8, i * 8 + 9))
        left = pltpu.roll(left_ref[strip_of(i), :], lax.rem(128 - place, 128), 1)
        right = pltpu.roll(right_ref[strip_of(i), :], 127 - place, 1)
        if beside is not None:
            before, after, left, right = beside(c, i, before, after, left, right)
        above = load_above(c, strip_of(i)) if load_above else None
        below = load_below(c, strip_of(i)) if load_below else None
        sums.append(neighbour_sum(center, above, below, before, after, left, right))
        centers.append(center)
    return centers, sums


def slot(c, z):
    return c * 16 + z


def edges_kernel(
    u_ref, v_ref, region_ref, flags_ref, first_ref, last_ref, left_ref, right_ref, plastic_ref
):
    step = pl.program_id(0)
    depth = u_ref.shape[1]

    @pl.when(step == 0)
    def _():
        left_ref[...] = jnp.zeros_like(left_ref)
        right_ref[...] = jnp.zeros_like(right_ref)
        wide = (rows_of((64, 8)) // 8 == lanes((64, 8))).astype(F32)
        high = (rows_of((32, 256)) == lanes((32, 256)) // 8).astype(F32)
        marks = (flags_ref[...] == 1).astype(F32)
        plastic = dot(dot(wide, marks), high)
        plastic_ref[...] = plastic
        first_ref[160:168, :] = jnp.broadcast_to(plastic[0:1], (8, 256))
        last_ref[160:168, :] = jnp.broadcast_to(plastic[63:64], (8, 256))
        lane = lanes((64, 128))
        left_ref[1] = jnp.where(lane == 64, pltpu.roll(plastic[:, :128], 64, 1), 0.0)
        right_ref[1] = jnp.where(lane == 64, pltpu.roll(plastic[:, 128:], 65, 1), 0.0)

    for k in range(depth):
        z = step * depth + k
        for c in range(3):
            place = slot(c, z)
            first_ref[pl.ds(place, 1), :] = u_ref[c, k, 0:1, :]
            last_ref[pl.ds(place, 1), :] = u_ref[c, k, 63:64, :]
            first_ref[pl.ds(48 + place, 1), :] = u_ref[c, k, 1:2, :]
            last_ref[pl.ds(48 + place, 1), :] = u_ref[c, k, 62:63, :]
            first_ref[pl.ds(96 + place, 1), :] = v_ref[c, k, 0:1, :]
            last_ref[pl.ds(96 + place, 1), :] = v_ref[c, k, 63:64, :]
        first_ref[pl.ds(144 + z, 1), :] = region_ref[k, 0:1, :].astype(F32)
        last_ref[pl.ds(144 + z, 1), :] = region_ref[k, 63:64, :].astype(F32)
    lane = lanes((8, 128))
    for i in range(8):
        rows = strip_of(i)
        total = [left_ref[0, rows, :], left_ref[1, rows, :], right_ref[0, rows, :], right_ref[1, rows, :]]

        def put(index, tile, source, target):
            moved = pltpu.roll(tile, lax.rem(target + (128 - source), 128), 1)
            total[index] = jnp.where(lane == target, moved, total[index])

        for k in range(depth):
            z = step * depth + k
            for c in range(3):
                place = slot(c, z)
                u0, u1 = u_ref[c, k, rows, 0:128], u_ref[c, k, rows, 128:256]
                put(0, u0, 0, place)
                put(0, u0, 1, place + 48)
                put(2, u1, 127, place)
                put(2, u1, 126, place + 48)
                put(1, v_ref[c, k, rows, 0:128], 0, place)
                put(3, v_ref[c, k, rows, 128:256], 127, place)
            put(1, region_ref[k, rows, 0:128].astype(F32), 0, z + 48)
            put(3, region_ref[k, rows, 128:256].astype(F32), 127, z + 48)
        left_ref[0, rows, :] = total[0]
        left_ref[1, rows, :] = total[1]
        right_ref[0, rows, :] = total[2]
        right_ref[1, rows, :] = total[3]


def beside_kernel(
    where_ref, shear_ref, yields_ref, first_ref, last_ref, left_ref, right_ref,
    top_ref, bottom_ref, west_ref, east_ref, lines_ref,
    new_top_ref, new_bottom_ref, new_west_ref, new_east_ref,
):
    narrow = where_ref[3]
    table = label_table(shear_ref, yields_ref)
    low = jnp.where(narrow > 0, lines_ref[jnp.maximum(narrow - 1, 0), 192:240, :], 0.0)
    high = jnp.where(narrow < 3, lines_ref[jnp.minimum(narrow + 1, 3), 192:240, :], 0.0)

    row = rows_of((16, 256))
    lane = lanes((16, 128))
    sides = (
        (top_ref, first_ref, new_top_ref, 0, where_ref[2] > 0),
        (bottom_ref, last_ref, new_bottom_ref, 1, where_ref[2] < 31),
    )
    for halo_ref, own_ref, out_ref, side, inside in sides:
        laplace = []
        for c in range(3):
            part = slice(c * 16, c * 16 + 16)
            center = halo_ref[part, :]
            total = halo_ref[48 + c * 16 : 64 + c * 16, :] + own_ref[part, :]
            total = total + jnp.where(row == 0, 0.0, pltpu.roll(center, 1, 0))
            total = total + jnp.where(row == 15, 0.0, pltpu.roll(center, 15, 0))
            c0, c1 = center[:, :128], center[:, 128:]
            before = pltpu.roll(low[part], 128 - side, 1) if side else low[part]
            after = pltpu.roll(high[part], 127 - side, 1)
            w0, w1 = pltpu.roll(c0, 1, 1), pltpu.roll(c1, 1, 1)
            e0, e1 = pltpu.roll(c0, 127, 1), pltpu.roll(c1, 127, 1)
            west = [jnp.where(lane == 0, before, w0), jnp.where(lane == 0, w0, w1)]
            east = [jnp.where(lane == 127, e1, e0), jnp.where(lane == 127, after, e1)]
            total = total + jnp.concatenate(west, 1) + jnp.concatenate(east, 1)
            laplace.append(total - 6.0 * center)
        plastic = jnp.broadcast_to(halo_ref[160:161, :], (16, 256))
        scale = force_scale(laplace, halo_ref[144:160, :].astype(jnp.int32), plastic, table)
        damping = jnp.where(row == 0, DAMPING, 0.0)
        for c in range(3):
            part = slice(c * 16, c * 16 + 16)
            v = halo_ref[96 + c * 16 : 112 + c * 16, :]
            v = v + DT * (scale * laplace[c] - damping * v)
            out_ref[part, :] = jnp.where(inside, halo_ref[part, :] + DT * v, 0.0)

    row = rows_of((64, 128))
    lane = lanes((64, 128))
    layer = lax.rem(lane, 16)
    used = lane < 48
    sides = (
        (west_ref, left_ref, new_west_ref, low, narrow > 0),
        (east_ref, right_ref, new_east_ref, high, narrow < 3),
    )
    for halo_ref, own_ref, out_ref, corner, inside in sides:
        tile, other = halo_ref[0], halo_ref[1]
        center = jnp.where(used, tile, 0.0)
        corners = jnp.concatenate([corner, jnp.zeros((80, 128), F32)], 0).T
        total = pltpu.roll(tile, 80, 1) + own_ref[0]
        total = total + jnp.where(row == 0, corners[0:1], pltpu.roll(center, 1, 0))
        total = total + jnp.where(row == 63, corners[1:2], pltpu.roll(center, 63, 0))
        total = total + jnp.where(layer == 0, 0.0, pltpu.roll(center, 1, 1))
        total = total + jnp.where(layer == 15, 0.0, pltpu.roll(center, 127, 1))
        laplace = jnp.where(used, total - 6.0 * center, 0.0)
        squares = laplace * laplace
        squares = (
            (squares + pltpu.roll(squares, 16, 1))
            + (pltpu.roll(squares, 32, 1) + pltpu.roll(squares, 96, 1))
            + pltpu.roll(squares, 112, 1)
        )
        region = jnp.where(
            lane < 16,
            pltpu.roll(other, 80, 1),
            jnp.where(lane < 32, pltpu.roll(other, 96, 1), pltpu.roll(other, 112, 1)),
        ).astype(jnp.int32)
        modulus = jnp.full(region.shape, table[0][0], F32)
        ratio = jnp.tile(table[1][0], (8, 1))
        for label in range(1, 4):
            modulus = jnp.where(region == label, table[0][label], modulus)
            ratio = jnp.where(region == label, jnp.tile(table[1][label], (8, 1)), ratio)
        capped = lax.rsqrt(1.0 + squares * ratio)
        scale = modulus * jnp.where(other[:, 64:65] > 0.5, capped, 1.0)
        v = other + DT * (scale * laplace - jnp.where(layer == 0, DAMPING, 0.0) * other)
        out_ref[...] = jnp.where(used & inside, center + DT * v, 0.0)


def slip_kernel(
    shear_ref, yields_ref, u_ref, v_ref, region_ref, plastic_ref,
    top_ref, bottom_ref, left_ref, right_ref, where_ref, _after_ref, send_ref,
):
    halo_refs = (top_ref, bottom_ref, left_ref.at[0], right_ref.at[0])
    table = label_table(shear_ref, yields_ref)
    lane = lanes((48, 128))
    t0, t1 = top_ref[0:48, 0:128], top_ref[0:48, 128:256]
    b0, b1 = bottom_ref[0:48, 0:128], bottom_ref[0:48, 128:256]
    to_lower = jnp.where(lane == 0, t0, pltpu.roll(b0, 1, 1))
    to_upper = jnp.where(lane == 0, pltpu.roll(t1, 1, 1), pltpu.roll(b1, 2, 1))
    for n in range(4):
        send_ref[n, 192:240, :] = jnp.where(where_ref[3] < n, to_upper, to_lower)
    for i in range(8):
        rows = strip_of(i)
        centers, sums = stencil_strip(
            i,
            lambda c, r: u_ref[c, 0, r, :],
            None,
            lambda c, r: u_ref[c, 1, r, :],
            None,
            halo_refs,
            0,
        )
        force = strip_force(
            centers, sums, region_ref[0, rows, :], plastic_ref[rows, :], table
        )
        n, part = i // 2, (i % 2) * 8
        for c in range(3):
            v = v_ref[c, 0, rows, :]
            v = v + DT * (force[c] - DAMPING * v)
            moved = centers[c] + DT * v
            for f, values in enumerate((centers[c], moved)):
                for half in range(2):
                    start = f * 96 + c * 32 + half * 16 + part
                    send_ref[n, start : start + 8, :] = values[:, half * 128 : half * 128 + 128]


def both_steps_kernel(low, high, *refs):
    (shear_ref, yields_ref, u_hbm, v_hbm, region_hbm, plastic_ref) = refs[:6]
    halo_one = (refs[6], refs[7], refs[8].at[0], refs[9].at[0])
    halo_two = refs[10:14]
    head = low == 2
    count = 4 if head else 2
    outs, scratch = refs[-10 - count : -10], refs[-10:]
    us, vs, rs, new_us, new_vs, out_us, out_vs, in_sems, out_sems, head_sems = scratch
    table = label_table(shear_ref, yields_ref)
    start = 0 if head else low - 1
    stop = min(high, 15)
    begin, end = max(start - 1, 0), min(stop + 1, 15)

    def bring(z):
        return (
            pltpu.make_async_copy(u_hbm.at[:, z], us.at[:, z - begin], in_sems.at[z - begin, 0]),
            pltpu.make_async_copy(v_hbm.at[:, z], vs.at[:, z - begin], in_sems.at[z - begin, 1]),
            pltpu.make_async_copy(region_hbm.at[z], rs.at[z - begin], in_sems.at[z - begin, 2]),
        )

    def put(z):
        return (
            pltpu.make_async_copy(out_us.at[:, z - low], outs[0].at[:, z], out_sems.at[z - low, 0]),
            pltpu.make_async_copy(out_vs.at[:, z - low], outs[1].at[:, z], out_sems.at[z - low, 1]),
        )

    for z in range(begin, end + 1):
        for copy in bring(z):
            copy.start()

    def ready(z):
        for copy in bring(z):
            copy.wait()

    for z in range(begin, start + 1):
        ready(z)

    @pl.loop(start, stop + 1)
    def _(z):
        @pl.when(z < end)
        def _():
            ready(z + 1)

        damping = jnp.where(z == 0, DAMPING, 0.0).astype(F32)
        lower = jnp.where(z > 0, 1.0, 0.0).astype(F32)
        upper = jnp.where(z < 15, 1.0, 0.0).astype(F32)
        here = z - begin
        for i in range(8):
            rows = strip_of(i)
            centers, sums = stencil_strip(
                i,
                lambda c, r: us[c, here, r, :],
                None,
                lambda c, r: us[c, jnp.minimum(here + 1, end - begin), r, :] * upper,
                lambda c, r: us[c, jnp.maximum(here - 1, 0), r, :] * lower,
                halo_one,
                z,
            )
            force = strip_force(centers, sums, rs[here, rows, :], plastic_ref[rows, :], table)
            for c in range(3):
                v = vs[c, here, rows, :]
                v = v + DT * (force[c] - damping * v)
                new_vs[c, z - start, rows, :] = v
                new_us[c, z - start, rows, :] = centers[c] + DT * v

    heads = []
    if head:
        heads = [
            pltpu.make_async_copy(new_us.at[:, 0:4], outs[2], head_sems.at[0]),
            pltpu.make_async_copy(new_vs.at[:, 0:2], outs[3], head_sems.at[1]),
        ]
        for copy in heads:
            copy.start()

    @pl.loop(low, high)
    def _(z):
        upper = jnp.where(z < 15, 1.0, 0.0).astype(F32)
        here = z - start
        for i in range(8):
            rows = strip_of(i)
            centers, sums = stencil_strip(
                i,
                lambda c, r: new_us[c, here, r, :],
                None,
                lambda c, r: new_us[c, jnp.minimum(here + 1, stop - start), r, :] * upper,
                lambda c, r: new_us[c, here - 1, r, :],
                halo_two,
                z,
            )
            force = strip_force(centers, sums, rs[z - begin, rows, :], plastic_ref[rows, :], table)
            for c in range(3):
                v = new_vs[c, here, rows, :] + DT * force[c]
                out_vs[c, z - low, rows, :] = v
                out_us[c, z - low, rows, :] = centers[c] + DT * v
        for copy in put(z):
            copy.start()

    @pl.loop(low, high)
    def _(z):
        for copy in put(z):
            copy.wait()

    for copy in heads:
        copy.wait()


def last_kernel(
    shear_ref, yields_ref, u_ref, v_ref, region_ref, plastic_ref,
    top_ref, bottom_ref, left_ref, right_ref,
    recv_ref, _old_u_ref, _old_v_ref, new_u_ref, new_v_ref, surface,
):
    square = DT * DT
    table = label_table(shear_ref, yields_ref)
    halo_refs = (top_ref, bottom_ref, left_ref, right_ref)

    def traction(f, c, i):
        start = f * 96 + c * 32 + (i % 2) * 8
        return jnp.concatenate(
            [recv_ref[i // 2, start + half * 16 : start + half * 16 + 8, :] for half in range(2)], 1
        )

    def outside(n, c, side):
        row = 208 + c * 2 + side
        return jnp.concatenate(
            [recv_ref[n, row + half * 8 : row + half * 8 + 1, :] for half in range(2)], 1
        )

    def beside(c, i, before, after, left, right):
        if i == 0:
            before = before + square * outside(0, c, 0)
        if i == 7:
            after = after + square * outside(3, c, 1)
        start = 192 + (i % 2) * 8
        columns = recv_ref[i // 2, start : start + 8, :]
        left = left + square * pltpu.roll(columns, (128 - c) % 128, 1)
        right = right + square * pltpu.roll(columns, 127 - (3 + c), 1)
        return before, after, left, right

    for i in range(8):
        for c in range(3):
            surface[c, strip_of(i), :] = u_ref[c, 0, strip_of(i), :] + square * traction(0, c, i)
    for z in range(2):
        for i in range(8):
            rows = strip_of(i)
            above = lambda c, r: u_ref[c, z + 1, r, :]
            if z == 0:
                load, below = lambda c, r: surface[c, r, :], None
            else:
                load, below = lambda c, r: u_ref[c, 1, r, :], lambda c, r: surface[c, r, :]
            centers, sums = stencil_strip(
                i, load, beside if z == 0 else None, above, below, halo_refs, z
            )
            force = strip_force(
                centers, sums, region_ref[z, rows, :], plastic_ref[rows, :], table
            )
            for c in range(3):
                v = v_ref[c, z, rows, :]
                if z == 0:
                    v = v + DT * traction(0, c, i)
                    v = v + DT * (force[c] + (traction(1, c, i) - DAMPING * v))
                else:
                    v = v + DT * force[c]
                new_v_ref[c, z, rows, :] = v
                new_u_ref[c, z, rows, :] = centers[c] + DT * v


def history_kernel(where_ref, kernel_ref, history_ref, *refs):
    own_ref, main_ref, edge_ref = refs[-3:]
    low = where_ref[0] == 1
    width = own_ref.shape[1]

    def step(m, carry):
        total, ones = carry
        out, twos = [], []
        for c in range(3):
            two = kernel_ref[m + 2, c].astype(F32)
            twos.append(two)
            for ri in range(2):
                past = history_ref[m, ri, c].astype(F32)
                p1, p2 = total[c * 2 + ri]
                out.append((p1 + ones[c] * past, p2 + two * past))
        return tuple(out), tuple(twos)

    def block(j, carry):
        for k in range(UNROLL):
            carry = step(j * UNROLL + k, carry)
        return carry

    zero = jnp.zeros((8, width), F32)
    carry = (
        tuple((zero, zero) for _ in range(6)),
        tuple(kernel_ref[1, c].astype(F32) for c in range(3)),
    )
    carry = lax.fori_loop(0, 30 // UNROLL, block, carry)
    total, _ = step(30, carry)
    values = [None] * 18
    for c in range(3):
        one = kernel_ref[32, c].astype(F32)
        for ri in range(2):
            p1, p2 = total[c * 2 + ri]
            values[ri * 3 + c] = p1 + one * history_ref[31, ri, c].astype(F32)
            values[6 + ri * 3 + c] = p2
        values[12 + c] = kernel_ref[0, c].astype(F32)
        values[15 + c] = kernel_ref[1, c].astype(F32)
    for i, value in enumerate(values):
        row = [value[r : r + 1] for r in range(8)]
        for r, (a, b) in enumerate(((0, 4), (1, 3), (2, 2), (3, 1))):
            own_ref[i * 4 + r : i * 4 + r + 1, :] = jnp.where(low, row[a], row[b])
        for r, (a, b) in enumerate(((4, 4), (5, 7), (6, 6), (7, 5))):
            main_ref[i * 4 + r : i * 4 + r + 1, :] = jnp.where(low, row[a], row[b])
        edge_ref[i : i + 1, :] = row[0]


def mirror_kernel(where_ref, reverse_ref, own_ref, main_ref, edge_ref, out_ref, tiles, turned):
    low = where_ref[0] == 1
    special = where_ref[1]
    for i in range(18):
        own = own_ref[i * 4 : i * 4 + 4, :]
        main = main_ref[i * 4 : i * 4 + 4, :]
        edge = edge_ref[i : i + 1, :]
        other = jnp.where(rows_of(main.shape) == 0, edge, main)
        tiles[i * 8 : i * 8 + 4, :] = jnp.where(low, own, main)
        tiles[i * 8 + 4 : i * 8 + 8, :] = jnp.where(low, other, own)
    for block in range(16):
        part = slice(block * 128, block * 128 + 128)
        high, rest = halves(tiles[:, part])
        turned[:, part] = dot(high, reverse_ref[...]) + dot(rest, reverse_ref[...])
    lane = lanes((8, 128))
    row = rows_of((8, 128))
    upper = row >= 4
    chosen = (lax.rem(row, 4) + (1 - special)) == 0

    def swap(x):
        return pltpu.roll(x, 4, 0)

    for block in range(16):
        part = slice(block * 128, block * 128 + 128)
        mirror = slice((15 - block) * 128, (15 - block) * 128 + 128)
        first = ((16 - block) % 16) * 128
        first = slice(first, first + 128)

        def load(i):
            rows = slice(i * 8, i * 8 + 8)
            back = jnp.where(lane == 0, turned[rows, first], turned[rows, mirror])
            return tiles[rows, part], back

        for c in range(3):
            for k in range(2):
                t, b = load(12 + k * 3 + c)
                own = 0.5 * (t + b)
                other = swap(own)
                mean = jnp.where(chosen, 0.5 * (own + other), 0.5 * (t + swap(b)))
                diff = jnp.where(chosen, 0.5 * (own - other), 0.0)
                out_ref[k, c, :, part] = jnp.where(upper, swap(mean), mean)
                out_ref[2 + k, c, :, part] = jnp.where(upper, swap(diff), diff)
            pair = []
            for k in range(2):
                tr, br = load(k * 6 + c)
                ti, bi = load(k * 6 + 3 + c)
                hr, hi = 0.5 * (tr + br), 0.5 * (ti - bi)
                sr, si = swap(hr), swap(hi)
                pair.append(
                    (
                        jnp.where(chosen, hr - si, 0.5 * (tr + swap(br))),
                        jnp.where(chosen, hi + sr, 0.5 * (ti - swap(bi))),
                        hr + si,
                        hi - sr,
                    )
                )
            out_ref[4, c, :, part] = jnp.where(upper, swap(pair[1][0]), pair[0][0])
            out_ref[5, c, :, part] = jnp.where(upper, swap(pair[1][1]), pair[0][1])
            out_ref[6, c, :, part] = pair[0][2]
            out_ref[7, c, :, part] = pair[0][3]


def dip_kernel(radix_ref, turn_ref, out_table_ref, recv_ref, _after_ref, send_ref):
    wide = []
    for c in range(3):
        pieces = []
        for n in range(4):
            for f in range(2):
                start = f * 96 + c * 32
                pieces.append(recv_ref[n, start : start + 32, :])
        wide.append(jnp.concatenate(pieces, 0))
    z = left_dot(radix_ref, jnp.concatenate(wide, 1))
    lane = lanes((1, 128))
    for s in range(2):
        tr, ti = jnp.tile(turn_ref[0, s], (16, 1)), jnp.tile(turn_ref[1, s], (16, 1))
        for c in range(3):
            part = slice(c * 128, c * 128 + 128)
            zr = z[s * 128 : s * 128 + 128, part]
            zi = z[256 + s * 128 : 384 + s * 128, part]
            turned = jnp.concatenate([zr * tr - zi * ti, zr * ti + zi * tr], 1)
            high, low = halves(turned)
            table, rest = out_table_ref[0, s], out_table_ref[1, s]
            res = dot(table, high, (1, 1)) + (dot(rest, high, (1, 1)) + dot(table, low, (1, 1)))
            imag = res[64:128]
            if s == 0:
                extra = jnp.where(lax.rem(lane, 4) == 0, res[128:129], 0.0)
                imag = jnp.where(rows_of(imag.shape) == 0, imag + extra, imag)
            send_ref[pl.ds(s * 384 + c * 2, 64, stride=6), :] = res[0:64]
            send_ref[pl.ds(s * 384 + c * 2 + 1, 64, stride=6), :] = imag


def strike_kernel(
    in_ref, turn_ref, mix_ref, reverse_ref, out_table_ref,
    coef_ref, recv_ref, _after_ref, send_ref, spec, back, total,
):
    tr, ti = turn_ref[0], turn_ref[1]
    real, imag = [], []
    for c in range(3):
        re = recv_ref[pl.ds(c * 2, 128, stride=6), :].T
        im = recv_ref[pl.ds(c * 2 + 1, 128, stride=6), :].T
        y = right_dot(jnp.concatenate([re, im], 1), in_ref)
        yr, yi = y[:, :128], y[:, 128:]
        real.append(yr * tr - yi * ti)
        imag.append(yr * ti + yi * tr)
    stacked = jnp.concatenate([jnp.concatenate(real, 1), jnp.concatenate(imag, 1)], 0)
    spec[...] = left_dot(mix_ref, stacked)
    for c in range(3):
        part = slice(c * 128, c * 128 + 128)
        high, low = halves(spec[:, part])
        back[:, part] = dot(high, reverse_ref[...]) + dot(low, reverse_ref[...])
    lane = lanes((8, 128))
    upper = rows_of((8, 128)) >= 4

    def swap(x):
        return pltpu.roll(x, 4, 0)

    for c in range(3):
        part = slice(c * 128, c * 128 + 128)
        for block in range(16):
            wave = slice(block * 128, block * 128 + 128)
            a0, a1 = coef_ref[0, c, :, wave], coef_ref[1, c, :, wave]
            m0, m1 = coef_ref[2, c, :, wave], coef_ref[3, c, :, wave]
            for ri in range(2):
                rows = slice(ri * 128 + block * 8, ri * 128 + block * 8 + 8)
                first = ri * 128 + ((16 - block) % 16) * 8
                other = ri * 128 + (15 - block) * 8
                s = spec[rows, part]
                r = jnp.where(
                    lane == 0, back[first : first + 8, part], back[other : other + 8, part]
                )
                if ri == 1:
                    r = -r
                t = a0 * s + m0 * r + coef_ref[4 + ri, c, :, wave]
                q = a0 * r + m0 * s + coef_ref[6 + ri, c, :, wave]
                more = (DT * DT) * (a0 * swap(t) + m0 * swap(q)) + a1 * swap(s) + m1 * swap(r)
                g = t + jnp.where(upper, more, 0.0)
                total[rows, part] = g if ri == 0 else -g
    y = left_dot(mix_ref, total[...])
    owner = rows_of((128, 128))
    wide_lane = lanes((128, 128))
    extra = [jnp.zeros((128, 128), F32)] * 2
    for c in range(3):
        part = slice(c * 128, c * 128 + 128)
        yr, yi = y[:128, part], -y[128:, part]
        turned = jnp.concatenate([yr * tr + yi * ti, yi * tr - yr * ti], 1)
        high, low = halves(turned)
        res = dot(out_table_ref[0], high, (1, 1)) + (
            dot(out_table_ref[1], high, (1, 1)) + dot(out_table_ref[0], low, (1, 1))
        )
        for ri in range(2):
            lines = res[ri * 128 : ri * 128 + 128]
            send_ref[pl.ds(c * 2 + ri, 128, stride=8), :] = lines
            for side in range(2):
                group = c * 2 + side
                if side == 0:
                    moved = jnp.where(owner == 0, 0.0, pltpu.roll(lines, 1, 0))
                    moved = pltpu.roll(moved, (group * 8 + 8) % 128, 1)
                else:
                    moved = jnp.where(owner == 127, 0.0, pltpu.roll(lines, 127, 0))
                    moved = pltpu.roll(moved, group * 8, 1) if group else moved
                extra[ri] = jnp.where(wide_lane // 8 == group, moved, extra[ri])
    for ri in range(2):
        send_ref[pl.ds(6 + ri, 128, stride=8), :] = extra[ri]


def undip_kernel(in_ref, turn_ref, unradix_ref, recv_ref, _after_ref, send_ref):
    row = rows_of((128, 128))
    lane = lanes((128, 128))
    alt = jnp.where(lax.rem(lane, 2) == 0, 0.5, -0.5).astype(F32)
    stacks = [[], [], [], []]
    for c in range(4):
        re = recv_ref[pl.ds(c * 2, 128, stride=8), :].T
        im = recv_ref[pl.ds(c * 2 + 1, 128, stride=8), :].T
        h = right_dot(jnp.concatenate([re, im], 1), in_ref)
        for s in range(2):
            hr = h[:, s * 256 : s * 256 + 128]
            hi = h[:, s * 256 + 128 : s * 256 + 256]
            if s == 0:
                fix = alt * im[:, 0:1] - 0.5 * re[:, 0:1]
                hr = hr + jnp.where(lax.rem(row, 4) == 0, fix, 0.0)
            tr, ti = jnp.tile(turn_ref[0, s], (16, 1)), jnp.tile(turn_ref[1, s], (16, 1))
            stacks[s].append(hr * tr + hi * ti)
            stacks[2 + s].append(hi * tr - hr * ti)
    stacked = jnp.concatenate([jnp.concatenate(part, 1) for part in stacks], 0)
    out = left_dot(unradix_ref, stacked)
    for n in range(4):
        for f in range(2):
            for c in range(3):
                start = f * 96 + c * 32
                row0 = (n * 2 + f) * 32
                send_ref[n, start : start + 32, :] = out[row0 : row0 + 32, c * 128 : c * 128 + 128]
    small = lanes((16, 128))

    def plane(n, half, c):
        row0 = n * 64 + half * 16
        return out[row0 : row0 + 16, c * 128 : c * 128 + 128]

    for n in range(4):
        columns = jnp.zeros((16, 128), F32)
        for c in range(3):
            if n > 0:
                moved = pltpu.roll(plane(n - 1, 1, c), c + 1, 1)
                columns = jnp.where(small == c, moved, columns)
            if n < 3:
                moved = pltpu.roll(plane(n + 1, 0, c), 3 + c, 1)
                columns = jnp.where(small == 3 + c, moved, columns)
        send_ref[n, 192:208, :] = columns
        for half in range(2):
            send_ref[n, 208 + half * 8 : 216 + half * 8, :] = plane(n, half, 3)[:8]


def full(shape):
    del shape
    return pl.BlockSpec(memory_space=pltpu.VMEM)


SMEM = pl.BlockSpec(memory_space=pltpu.SMEM)


def in_hbm(x):
    return pltpu.with_memory_space_constraint(x, pltpu.HBM)


def hbm_shape(*shape):
    return pltpu.HBM(shape, F32)


def shape_of(*shape):
    return jax.ShapeDtypeStruct(shape, F32)


def call(body, out_shape, args, smem=0, scratch=(), after=(), limit=16 << 20):
    outs = out_shape if isinstance(out_shape, (tuple, list)) else [out_shape]
    size = sum(math.prod(x.shape) * 4 for x in list(args) + list(outs))
    out_specs = [full(x.shape) for x in outs]
    return pl.pallas_call(
        body,
        in_specs=[SMEM] * smem
        + [full(x.shape) for x in args[smem:]]
        + [pl.BlockSpec(memory_space=pl.ANY)] * len(after),
        out_specs=out_specs if isinstance(out_shape, (tuple, list)) else out_specs[0],
        out_shape=out_shape,
        scratch_shapes=scratch,
        cost_estimate=pl.CostEstimate(flops=0, bytes_accessed=size, transcendentals=0),
        compiler_params=pltpu.CompilerParams(vmem_limit_bytes=limit),
    )(*args, *(in_hbm(x) for x in after))


def halo(first, last, left, right):
    up = [(i, i + 1) for i in range(31)]
    down = [(i + 1, i) for i in range(31)]
    top = lax.ppermute(last, "wide", up)
    bottom = lax.ppermute(first, "wide", down)
    up = [(i, i + 1) for i in range(3)]
    down = [(i + 1, i) for i in range(3)]
    from_left = lax.ppermute(right, "narrow", up)
    from_right = lax.ppermute(left, "narrow", down)
    return top, bottom, from_left, from_right


def exchange(x, axis):
    return lax.all_to_all(x, axis, split_axis=0, concat_axis=0, tiled=True)


def program(u, v, region, flags, shear, yields, history, kernel):
    device = lax.axis_index(ALL)
    where = jnp.stack(
        [
            (device < 64).astype(jnp.int32),
            (device == 0).astype(jnp.int32),
            lax.axis_index("wide"),
            lax.axis_index("narrow"),
        ]
    )
    edge_shapes = [shape_of(168, 256)] * 2 + [shape_of(2, 64, 128)] * 2
    halo_shapes = [hbm_shape(48, 256)] * 2 + [hbm_shape(64, 128)] * 2
    near = lambda depth: pl.BlockSpec((3, depth, 64, 256), lambda *_: (0, 0, 0, 0))
    slab = lambda depth: pl.BlockSpec((depth, 64, 256), lambda *_: (0, 0, 0))
    planes = lambda depth, start=0: pl.BlockSpec(
        (3, depth, 64, 256), lambda z: (0, z + start // depth, 0, 0)
    )
    slabs = lambda depth, start=0: pl.BlockSpec(
        (depth, 64, 256), lambda z: (z + start // depth, 0, 0)
    )
    halo_specs = [full((48, 256))] * 2 + [full((64, 128))] * 2
    any_spec = pl.BlockSpec(memory_space=pl.ANY)
    t = TABLES
    u, v, region, history, kernel = (in_hbm(x) for x in (u, v, region, history, kernel))
    shear, yields, where = in_hbm(shear), in_hbm(yields), in_hbm(where)

    first, last, left, right, plastic = pl.pallas_call(
        edges_kernel,
        grid=(4,),
        in_specs=[planes(4), planes(4), slabs(4), full((8, 32))],
        out_specs=[full(s.shape) for s in edge_shapes] + [full((64, 256))],
        out_shape=edge_shapes + [hbm_shape(64, 256)],
        cost_estimate=pl.CostEstimate(flops=0, bytes_accessed=8000000, transcendentals=0),
        compiler_params=pltpu.CompilerParams(vmem_limit_bytes=16 << 20),
            name="edges",
    )(u, v, region, in_hbm(flags))
    halo_one = halo(first, last, left, right)
    plastic = in_hbm(plastic)

    width = 256
    steps = 1024 // width

    def sums(part, after):
        shift = part * steps
        given = [] if part == 0 else list(after)
        return pl.pallas_call(
            history_kernel,
            grid=(steps,),
            in_specs=[
                SMEM,
                pl.BlockSpec((33, 3, 8, width), lambda i: (0, 0, 0, i + shift)),
                pl.BlockSpec((32, 2, 3, 8, width), lambda i: (0, 0, 0, 0, i + shift)),
            ]
            + [any_spec] * len(given),
            out_specs=[
                pl.BlockSpec((72, width), lambda i: (0, i + shift)),
                pl.BlockSpec((72, width), lambda i: (0, i + shift)),
                pl.BlockSpec((18, width), lambda i: (0, i + shift)),
            ],
            out_shape=[hbm_shape(72, 2048), hbm_shape(72, 2048), hbm_shape(18, 2048)],
            input_output_aliases={3: 0, 4: 1, 5: 2} if given else {},
            cost_estimate=pl.CostEstimate(flops=0, bytes_accessed=5500000, transcendentals=0),
            compiler_params=pltpu.CompilerParams(vmem_limit_bytes=16 << 20),
            name="history",
        )(where, kernel, history, *(in_hbm(x) for x in given))

    partial = sums(0, None)
    send = pl.pallas_call(
        slip_kernel,
        grid=(1,),
        in_specs=[SMEM, SMEM, near(2), near(1), slab(1), full((64, 256))]
        + halo_specs
        + [SMEM, any_spec],
        out_specs=full((4, 240, 128)),
        out_shape=shape_of(4, 240, 128),
        cost_estimate=pl.CostEstimate(flops=0, bytes_accessed=1500000, transcendentals=0),
        compiler_params=pltpu.CompilerParams(vmem_limit_bytes=16 << 20),
            name="slip",
    )(shear, yields, u, v, region, plastic, *halo_one, where, in_hbm(partial[2]))
    lines = exchange(send, "narrow")
    own, main, edge = sums(1, partial)
    main = lax.ppermute(main, ALL, [(i, 127 - i) for i in range(128)])
    edge = lax.ppermute(edge, ALL, [(64, 0)] + [(i, 128 - i) for i in range(65, 128)])

    send = call(
        dip_kernel, shape_of(768, 128), (t["radix"], t["dip_turn"], t["dip_out"], lines),
        after=[own],
    )
    waves = exchange(send.reshape(128, 1, 768), ALL).reshape(768, 128)

    halo_two = call(
        beside_kernel,
        halo_shapes,
        (where, shear, yields, *(in_hbm(x) for x in (first, last, left, right, *halo_one, lines))),
        smem=3,
    )

    def both_steps(low, high, given, after):
        head = low == 2
        start = 0 if head else low - 1
        stop = min(high, 15)
        held = min(stop + 1, 15) - max(start - 1, 0) + 1
        made = stop - start + 1
        tile = lambda n: pltpu.VMEM((3, n, 64, 256), F32)
        extra = [hbm_shape(3, 4, 64, 256), hbm_shape(3, 2, 64, 256)] if head else []
        return pl.pallas_call(
            functools.partial(both_steps_kernel, low, high),
            in_specs=[SMEM, SMEM] + [any_spec] * 3 + [full(None)] * 9
            + [any_spec] * (len(given) + 1),
            out_specs=[any_spec] * (2 + len(extra)),
            out_shape=[hbm_shape(3, 16, 64, 256)] * 2 + extra,
            input_output_aliases={14: 0, 15: 1} if given else {},
            scratch_shapes=[
                tile(held), tile(held), pltpu.VMEM((held, 64, 256), jnp.int32),
                tile(made), tile(made), tile(high - low), tile(high - low),
                pltpu.SemaphoreType.DMA((held, 3)),
                pltpu.SemaphoreType.DMA((high - low, 2)),
                pltpu.SemaphoreType.DMA((2,)),
            ],
            cost_estimate=pl.CostEstimate(
                flops=0, bytes_accessed=(high - low) * 1000000, transcendentals=0
            ),
            compiler_params=pltpu.CompilerParams(vmem_limit_bytes=24 << 20),
            name="both_steps",
        )(
            shear, yields, u, v, region, plastic,
            *(in_hbm(x) for x in halo_one), *(in_hbm(x) for x in halo_two),
            *(in_hbm(x) for x in given), in_hbm(after),
        )

    out_u, out_v, new_u, new_v = both_steps(2, CUTS[0], [], send)
    coefficients = call(
        mirror_kernel,
        shape_of(8, 3, 8, 2048),
        (where, t["reverse"], *(in_hbm(x) for x in (own, main, edge))),
        smem=1,
        scratch=[pltpu.VMEM((144, 2048), F32)] * 2,
    )
    send = call(
        strike_kernel,
        shape_of(1024, 128),
        (
            t["strike_in"], t["strike_turn"], t["strike_mix"], t["reverse"],
            t["strike_out"], coefficients, waves,
        ),
        scratch=[pltpu.VMEM((256, 384), F32)] * 3,
        after=[out_u],
    )
    columns = exchange(send.reshape(128, 8, 128), ALL).reshape(1024, 128)

    out = both_steps(CUTS[0], CUTS[1], [out_u, out_v], send)
    send = call(
        undip_kernel,
        shape_of(4, 224, 128),
        (t["dip_in"], t["undip_turn"], t["unradix"], columns),
        after=[out[0]],
    )
    tractions = exchange(send, "narrow")
    out = both_steps(CUTS[1], 16, out, send)
    return tuple(
        pl.pallas_call(
            last_kernel,
            grid=(1,),
            in_specs=[SMEM, SMEM, near(4), near(2), slab(2), full((64, 256))]
            + halo_specs
            + [full((4, 224, 128))]
            + [any_spec] * 2,
            out_specs=[near(2)] * 2,
            out_shape=[hbm_shape(3, 16, 64, 256)] * 2,
            scratch_shapes=[pltpu.VMEM((3, 64, 256), F32)],
            input_output_aliases={11: 0, 12: 1},
            cost_estimate=pl.CostEstimate(flops=0, bytes_accessed=4000000, transcendentals=0),
            compiler_params=pltpu.CompilerParams(vmem_limit_bytes=16 << 20),
            name="last",
        )(shear, yields, new_u, new_v, region, plastic, *halo_two, tractions, *out)
    )


def solution(mesh):
    tile = P(None, None, "wide", "narrow")
    in_specs = (
        tile,
        tile,
        P(None, "wide", "narrow"),
        P("wide", "narrow"),
        P(),
        P(),
        P(None, None, None, ALL, None),
        P(None, None, ALL, None),
    )
    return jax.shard_map(program, mesh=mesh, in_specs=in_specs, out_specs=(tile, tile), check_vma=False)
```
